32 devices in a mesh: gx: 16 (over z, y, core), gy: 2 (over x).
Axes of the slice: x: 2, y: 2, z: 4, core: 2. Of those that a mesh axis runs over, the one named last changes fastest.
Arguments:
- velocity: float32 [3, 256, 32, 128], P(None, 'gx', 'gy'), may hold values from -6 to 6
- pressure: float32 [256, 32, 128], P('gx', 'gy'), may hold values from -6 to 6
- land_type: int32 [256, 32], P('gx', 'gy'), may hold values from 0 to 15
- turbine_cells: int32 [256, 32, 128], P('gx', 'gy'), may hold values 0 or 1
- surface_drag: float32 [16], replicated, may hold values from 0.2 to 2
Outputs:
- velocity_new: float32 [3, 256, 32, 128], P(None, 'gx', 'gy')
- pressure_new: float32 [256, 32, 128], P('gx', 'gy')
The draws below stay inside these ranges and needn't reach their ends.
All inputs are finite; a program needn't handle non-finite values. No bound on the sum of `turbine_cells` on one device may be relied on, other than what follows from the above.
Results may differ from the reference program's by a relative error of at most 0.00002.
Values sent between devices are 32-bit elements; how exact they have to be, the bound alone decides.
A program may use at most 64 MiB of HBM per device.

```python
import math
import jax
import jax.numpy as jnp
from jax import lax

NZ = 128
TYPES = 16
SWEEPS = 2
COARSE_SWEEPS = 4
NX = 256
NY = 32


def set_ends(result, rng, low, top_value):
    spot = [jax.random.randint(jax.random.fold_in(rng, axis), (), 0, length) for axis, length in enumerate(result.shape)]
    main_axis = result.shape.index(max(result.shape))
    neighbour = spot[:main_axis] + [(spot[main_axis] + 1) % result.shape[main_axis]] + spot[main_axis + 1:]
    return result.at[tuple(spot)].set(low).at[tuple(neighbour)].set(top_value)


def shard_levels(own_key, shape, shards, low, high):
    def one(position, blocks):
        heights = jax.random.uniform(jax.random.fold_in(jax.random.fold_in(own_key, 6), position), (blocks,), jnp.float32, low / len(shards), high / len(shards))
        return jnp.repeat(jnp.exp(heights), shape[position] // blocks).reshape((-1,) + (1,) * (len(shape) - position - 1))

    factor_of = one(*shards[0])
    for cut in shards[1:]:
        factor_of = factor_of * one(*cut)
    return factor_of


def centred(stream_key, extent, width, reach, split=(), held_as=jnp.bfloat16):
    result = width * jax.random.normal(stream_key, extent, jnp.float32)
    if split:
        result = result * shard_levels(stream_key, extent, split, -0.22, 0.18)
    return jnp.clip(result, -reach, reach).astype(held_as)


def setup_inputs(seed: int = 0) -> dict:
    arg_keys = jax.random.split(jax.random.key(seed), 6)
    return {
        "velocity": centred(arg_keys[0], (3, NX, NY, NZ), 1.0, 6.0, ((1, 16), (2, 2)), jnp.float32),
        "pressure": centred(arg_keys[1], (NX, NY, NZ), 1.0, 6.0, ((0, 16), (1, 2)), jnp.float32),
        "land_type": set_ends(jax.random.randint(arg_keys[2], (NX, NY), 0, TYPES), jax.random.fold_in(arg_keys[2], 1), 0, TYPES - 1).astype(jnp.int32),
        "turbine_cells": set_ends((jax.random.randint(arg_keys[3], (NX, NY, NZ), 0, 8) < 1).astype(jnp.int32), jax.random.fold_in(arg_keys[3], 1), 0, 1),
        "surface_drag": jnp.clip(jnp.exp(jax.random.uniform(arg_keys[4], (TYPES,), jnp.float32, math.log(0.2), math.log(2.0))), 0.2, 2.0),
    }


time_step = 0.1
vertical_step = 0.5
eddy_coeff = 0.03
thrust_factor = 2.0
relax_weight = 0.8
driving_force = 1.0

def shifted(values, axis_pos, offset):
    starts = [1, 1, 1]
    starts[axis_pos] = 1 + offset
    length = [values.shape[-3] - 2, values.shape[-2] - 2, values.shape[-1] - 2]
    return values[..., starts[0]:starts[0] + length[0], starts[1]:starts[1] + length[1], starts[2]:starts[2] + length[2]]

def central(values, axis_pos):
    spacing = vertical_step if axis_pos == 2 else 1.0
    return (shifted(values, axis_pos, 1) - shifted(values, axis_pos, -1)) * (0.5 / spacing)

def surface_field(land_type, turbine_cells, surface_drag):
    kind_ids = jnp.arange(surface_drag.shape[0], dtype=jnp.int32)
    ground = lax.optimization_barrier(jnp.sum(jnp.where(land_type[:, :, None] == kind_ids, surface_drag, 0.0), axis=-1))
    ground_layer = jnp.arange(turbine_cells.shape[2], dtype=jnp.int32) == 0
    return thrust_factor * turbine_cells.astype(jnp.float32) + jnp.where(ground_layer, ground[:, :, None], 0.0)

def advance(padded, drag_field):
    gradient = [central(padded, axis_pos) for axis_pos in range(3)]
    strain = [[0.5 * (gradient[col_idx][row_idx] + gradient[row_idx][col_idx]) for col_idx in range(3)] for row_idx in range(3)]
    square_sum = strain[0][0] * strain[0][0]
    for row_idx in range(3):
        for col_idx in range(3):
            if row_idx + col_idx > 0:
                square_sum = square_sum + strain[row_idx][col_idx] * strain[row_idx][col_idx]
    viscosity = eddy_coeff * jnp.sqrt(2.0 * square_sum)
    centre = padded[:, 2:-2, 2:-2, 2:-2]
    wind_speed = jnp.sqrt(centre[0] * centre[0] + centre[1] * centre[1])
    updated = []
    for row_idx in range(3):
        change = jnp.zeros_like(centre[0])
        for col_idx in range(3):
            stress = 2.0 * viscosity * strain[row_idx][col_idx]
            change = change + central(stress, col_idx) - centre[col_idx] * gradient[col_idx][row_idx][1:-1, 1:-1, 1:-1]
        if row_idx < 2:
            change = change - drag_field * wind_speed * centre[row_idx]
        if row_idx == 0:
            change = change + driving_force
        updated.append(centre[row_idx] + time_step * change)
    return jnp.stack(updated)

def divergence(padded):
    return central(padded[0], 0) + central(padded[1], 1) + central(padded[2], 2)

def laplace(padded, spacing):
    centre = padded[1:-1, 1:-1, 1:-1]
    upright = vertical_step * spacing
    horizontal = (shifted(padded, 0, 1) + shifted(padded, 0, -1) + shifted(padded, 1, 1) + shifted(padded, 1, -1) - 4.0 * centre) / (spacing * spacing)
    vertical = (shifted(padded, 2, 1) + shifted(padded, 2, -1) - 2.0 * centre) / (upright * upright)
    return horizontal + vertical

def diagonal_of(spacing):
    upright = vertical_step * spacing
    return -(4.0 / (spacing * spacing) + 2.0 / (upright * upright))

def relax(pressure, padded, source, spacing):
    return pressure + relax_weight * (source - laplace(padded, spacing)) / diagonal_of(spacing)

def line_correct(pressure, residual, spacing):
    return pressure + relax_weight * lax.optimization_barrier(jnp.mean(residual, axis=1, keepdims=True)) / diagonal_of(spacing)

def periodic(values, pad_width, vertical_mode):
    leading = [(0, 0)] * (values.ndim - 3)
    values = jnp.pad(values, leading + [(pad_width, pad_width), (pad_width, pad_width), (0, 0)], mode='wrap')
    return jnp.pad(values, leading + [(0, 0), (0, 0), (pad_width, pad_width)], mode=vertical_mode)

def coarsen(values):
    return values.reshape(values.shape[0] // 2, 2, values.shape[1] // 2, 2, values.shape[2] // 2, 2).mean(axis=(1, 3, 5))

def refine(values):
    return jnp.repeat(jnp.repeat(jnp.repeat(values, 2, axis=0), 2, axis=1), 2, axis=2)

def cycle(pressure, source, depth_level):
    spacing = 2.0 ** depth_level
    if depth_level == 3:
        for sweep_idx in range(COARSE_SWEEPS):
            pressure = relax(pressure, periodic(pressure, 1, 'edge'), source, spacing)
        residual = source - laplace(periodic(pressure, 1, 'edge'), spacing)
        return line_correct(pressure, residual, spacing)
    for sweep_idx in range(SWEEPS):
        pressure = relax(pressure, periodic(pressure, 1, 'edge'), source, spacing)
    residual = source - laplace(periodic(pressure, 1, 'edge'), spacing)
    coarse_source = coarsen(residual)
    correction = cycle(jnp.zeros_like(coarse_source), coarse_source, depth_level + 1)
    pressure = pressure + refine(correction)
    for sweep_idx in range(SWEEPS):
        pressure = relax(pressure, periodic(pressure, 1, 'edge'), source, spacing)
    return pressure

def reference(velocity, pressure, land_type, turbine_cells, surface_drag):
    drag_field = surface_field(land_type, turbine_cells, surface_drag)
    star_velocity = advance(periodic(velocity, 2, 'constant'), drag_field)
    source = divergence(periodic(star_velocity, 1, 'constant')) / time_step
    pressure_new = cycle(pressure, source, 0)
    padded = periodic(pressure_new, 1, 'edge')
    gradient = jnp.stack([central(padded, 0), central(padded, 1), central(padded, 2)])
    return (star_velocity - time_step * gradient, pressure_new)
```

```python
import functools

import jax
import jax.numpy as jnp
from jax import lax
from jax.experimental import pallas as pl
from jax.experimental.pallas import tpu as pltpu
from jax.sharding import PartitionSpec as P

MESH = pl.DeviceIdType.MESH
F32 = jnp.float32
STEP = 0.1
WEIGHT = 0.8 / 12.0
KEEP = 0.2
OFF = 3
G_STRESS = 4
G_FINE = 8
VMEM_LIMIT = 24000 * 1024
REACH = 4


def loop(low, high, body, group):
    def run(indices):
        found = [store for index in indices for store in body(index)]
        for ref, at, value in found:
            ref[at] = value

    whole = (high - low) // group
    if whole == 1:
        run(range(low, low + group))
    elif whole > 1:

        def step(index, carry):
            run([low + index * group + k for k in range(group)])
            return carry

        lax.fori_loop(0, whole, step, 0)
    if low + whole * group < high:
        run(range(low + whole * group, high))


def kernel(
    nx, ny, vel_in, pre_in, turb_in, land_in, coeff_in, vel_out, pre_out,
    W, WLO, WHI, WSL, WSH, D, DLO, DHI, DSL, DSH, PA, PLO, PHI, PSL, PSH,
    PB, PC, CLO, CHI, CSL, CSH, F, FLO, FHI, FSL, FSH, T, S, tmp, tmp2, turb, land, coeff,
    G1, F1, P1A, P1B, G2, F2, P2A, P2B, F3, P3A, P3B, E1, E0,
    load_sem, send_sem, recv_sem,
):
    me_x, me_y = lax.axis_index("gx"), lax.axis_index("gy")
    own_x, own_y, nz = pre_out.shape
    side = (own_y // 8 + 1) * 8
    rows = own_x + 2 * OFF

    loads = [
        pltpu.make_async_copy(vel_in, W.at[:, OFF : OFF + own_x, 0:own_y], load_sem.at[0]),
        pltpu.make_async_copy(pre_in, PA.at[OFF : OFF + own_x, 0:own_y], load_sem.at[1]),
        pltpu.make_async_copy(turb_in, turb, load_sem.at[2]),
        pltpu.make_async_copy(land_in, land, load_sem.at[3]),
        pltpu.make_async_copy(coeff_in, coeff, load_sem.at[4]),
    ]
    for load in loads:
        load.start()

    def device(dx, dy):
        return (lax.rem(me_x + dx + nx, nx), lax.rem(me_y + dy + ny, ny))

    friends = [(dx, 0) for dx in range(-REACH, REACH + 1) if dx != 0]
    friends += [(dx, dy) for dx in (-1, 0, 1) for dy in range(1, ny)]
    close = [(dx, dy) for dx, dy in friends if abs(dx) < 2]
    barrier = pltpu.get_barrier_semaphore()
    for dx, dy in close:
        pl.semaphore_signal(barrier, inc=1, device_id=device(dx, dy), device_id_type=MESH)

    used = [0]

    def remote(src, dst, where):
        slot = used[0]
        used[0] += 1
        copy = pltpu.make_async_remote_copy(
            src_ref=src, dst_ref=dst, send_sem=send_sem.at[slot], recv_sem=recv_sem.at[slot],
            device_id=where, device_id_type=MESH,
        )
        copy.start()
        return copy

    def spans(dx, width, base):
        if dx == 0:
            return pl.ds(base, own_x), pl.ds(base, own_x)
        if dx == 1:
            return pl.ds(base + own_x - width, width), pl.ds(base - width, width)
        return pl.ds(base, width), pl.ds(base + own_x, width)

    def pick(ref, span, lead):
        return ref.at[:, span] if lead else ref.at[span]

    def send_x(M, width, lead=False):
        copies = []
        for dx in (1, -1):
            src, dst = spans(dx, width, OFF)
            a = M.at[:, src, 0:own_y] if lead else M.at[src, 0:own_y]
            b = M.at[:, dst, 0:own_y] if lead else M.at[dst, 0:own_y]
            copies.append(remote(a, b, device(dx, 0)))
        return copies

    def send_y(M, LO, HI, SL, SH, width, lead=False):
        if lead:
            SL[...] = M[:, OFF : OFF + own_x, own_y - width : own_y, :]
            SH[...] = M[:, OFF : OFF + own_x, 0:width, :]
        else:
            SL[...] = M[OFF : OFF + own_x, own_y - width : own_y, :]
            SH[...] = M[OFF : OFF + own_x, 0:width, :]
        copies = []
        for dx in (0, 1, -1):
            src, dst = spans(dx, width, width)
            if dx == 0:
                src = pl.ds(0, own_x)
            elif dx == 1:
                src = pl.ds(own_x - width, width)
            else:
                src = pl.ds(0, width)
            copies.append(remote(pick(SL, src, lead), pick(LO, dst, lead), device(dx, 1)))
            copies.append(remote(pick(SH, src, lead), pick(HI, dst, lead), device(dx, -1)))
        return copies

    def finish(copies):
        for copy in copies:
            copy.wait()

    def place(M, LO, HI, width, lead=False):
        lo, hi = OFF - width, OFF + own_x + width
        if lead:
            M[:, lo:hi, own_y : own_y + width, :] = HI[...]
            M[:, lo:hi, side - width : side, :] = LO[...]
        else:
            M[lo:hi, own_y : own_y + width, :] = HI[...]
            M[lo:hi, side - width : side, :] = LO[...]

    def lane_of(count):
        return lax.broadcasted_iota(jnp.int32, (count, nz), 1)

    def roll(v, shift, axis):
        return pltpu.roll(v, shift % v.shape[axis], axis)

    shape = (own_y, own_y)
    diagonal = lax.broadcasted_iota(jnp.int32, shape, 0) == lax.broadcasted_iota(jnp.int32, shape, 1)
    lane16 = lane_of(own_y)
    loads[3].wait()
    loads[4].wait()
    kinds = land[...]
    ground = jnp.zeros(kinds.shape, F32)
    for kind in range(coeff.shape[0]):
        ground = jnp.where(kinds == kind, coeff[kind], ground)
    loads[2].wait()
    for x in range(own_x):
        column = jnp.sum(jnp.where(diagonal, ground[x : x + 1, :], 0.0), axis=1, keepdims=True)
        low = jnp.where(lane16 == 0, column, 0.0)
        D[OFF + x, 0:own_y, :] = 2.0 * turb[x].astype(F32) + low
    loads[0].wait()
    loads[1].wait()
    pl.semaphore_wait(barrier, len(close))
    w_copies = send_y(W, WLO, WHI, WSL, WSH, 3, True) + send_x(W, 3, True)
    d_copies = send_y(D, DLO, DHI, DSL, DSH, 1) + send_x(D, 1)
    p_copies = send_y(PA, PLO, PHI, PSL, PSH, 3) + send_x(PA, 3)
    finish(w_copies)
    place(W, WLO, WHI, 3, True)
    finish(d_copies)
    place(D, DLO, DHI, 1)

    lane = lane_of(side)
    first, last = lane == 0, lane == nz - 1

    def up0(v):
        return jnp.where(last, 0.0, roll(v, -1, 1))

    def down0(v):
        return jnp.where(first, 0.0, roll(v, 1, 1))

    def stress_row(r):
        v = [W[a, r] for a in range(3)]
        gx = [0.5 * (W[a, r + 1] - W[a, r - 1]) for a in range(3)]
        gy = [0.5 * (roll(v[a], -1, 0) - roll(v[a], 1, 0)) for a in range(3)]
        gz = [up0(v[a]) - down0(v[a]) for a in range(3)]
        e01, e02, e12 = gx[1] + gy[0], gx[2] + gz[0], gy[2] + gz[1]
        q = 2.0 * (gx[0] * gx[0] + gy[1] * gy[1] + gz[2] * gz[2]) + e01 * e01 + e02 * e02 + e12 * e12
        visc = 0.03 * jnp.sqrt(q)
        twice = visc + visc
        t00, t11, t22 = twice * gx[0], twice * gy[1], twice * gz[2]
        t01, t02, t12 = visc * e01, visc * e02, visc * e12
        flat = v[0] * v[0] + v[1] * v[1]
        ghost = 0.03 * jnp.sqrt(2.0 * v[2] * v[2] + flat)
        ghosts = [ghost * v[0], ghost * v[1], (ghost + ghost) * v[2]]
        out = [(T, (0, r), t00), (T, (1, r), t01), (T, (2, r), t02)]
        drag = D[r] * jnp.sqrt(flat)
        for a, (ty, tz) in enumerate(((t01, t02), (t11, t12), (t12, t22))):
            change = 0.5 * (roll(ty, -1, 0) - roll(ty, 1, 0))
            change += jnp.where(last, -ghosts[a], roll(tz, -1, 1)) - jnp.where(first, ghosts[a], roll(tz, 1, 1))
            change -= v[0] * gx[a] + v[1] * gy[a] + v[2] * gz[a]
            if a < 2:
                change -= drag * v[a]
            if a == 0:
                change += 1.0
            out.append((S, (a, r), v[a] + STEP * change))
        return out

    loop(1, rows - 1, stress_row, G_STRESS)

    def star_row(r):
        return [
            (S, (a, r), S[a, r] + (0.5 * STEP) * (T[a, r + 1] - T[a, r - 1])) for a in range(3)
        ]

    loop(2, rows - 2, star_row, G_FINE)

    def source_row(r):
        s1, s2 = S[1, r], S[2, r]
        flat = 0.5 * (S[0, r + 1] - S[0, r - 1] + roll(s1, -1, 0) - roll(s1, 1, 0))
        return [(F, r, (flat + up0(s2) - down0(s2)) / STEP)]

    loop(OFF, OFF + own_x, source_row, G_FINE)
    f_copies = send_y(F, FLO, FHI, FSL, FSH, 2) + send_x(F, 2)
    finish(p_copies)
    place(PA, PLO, PHI, 3)
    finish(f_copies)
    place(F, FLO, FHI, 2)

    def stencil(src, r, sy, sz):
        p = src[r]
        lanes = lane_of(p.shape[0])
        z = jnp.where(lanes >= nz - sz, p, roll(p, -sz, 1)) + jnp.where(lanes < sz, p, roll(p, sz, 1))
        s = src[r + 1] + src[r - 1] + roll(p, -sy, 0) + roll(p, sy, 0)
        return p, s + 4.0 * z

    def sweep(src, dst, f, low, high, sy, sz, group=64):
        def body(r):
            p, around = stencil(src, r, sy, sz)
            return [(dst, r, KEEP * p + WEIGHT * (around - f[r]))]

        loop(low, high, body, min(group, high - low))

    def residual(src, f, r, sy, sz):
        p, around = stencil(src, r, sy, sz)
        return f[r] - (around - 12.0 * p)

    def pair(v, stride, axis):
        at = lax.broadcasted_iota(jnp.int32, v.shape, axis)
        even = (at // stride) % 2 == 0
        return v + jnp.where(even, roll(v, -stride, axis), roll(v, stride, axis))

    def spread(v, stride, bit):
        at = (lane_of(v.shape[0]) // stride) % 2
        return jnp.where(at == bit, v, roll(v, stride if bit == 0 else -stride, 1))

    sweep(PA, PB, F, 1, rows - 1, 1, 1, G_FINE)
    sweep(PB, PA, F, 2, rows - 2, 1, 1, G_FINE)
    PC[OFF : OFF + own_x, 0:own_y, :] = PA[OFF : OFF + own_x, 0:own_y, :]

    half = own_x // 2
    y1 = own_y // 2

    def fine_residual(i):
        r = OFF + 2 * i
        v = residual(PA, F, r, 1, 1) + residual(PA, F, r + 1, 1, 1)
        return [(tmp, i, pair(v[0:own_y], 1, 1))]

    loop(0, half, fine_residual, 2)
    packed = half // 2
    lane8 = lane_of(y1)
    for i in range(packed):
        parts = []
        for x in (2 * i, 2 * i + 1):
            parts.append(0.5 * (tmp[x, pl.ds(0, y1, 2), :] + tmp[x, pl.ds(1, y1, 2), :]))
        G1[0, 3 + i] = jnp.where(lane8 % 2 == 0, parts[0], parts[1])
    g_copies = []
    for dx in (1, -1, 0):
        for dy in range(ny):
            if dx == 0 and dy == 0:
                continue
            if dx == 0:
                src, dst = pl.ds(3, packed), pl.ds(3, packed)
            elif dx == 1:
                src, dst = pl.ds(packed, 3), pl.ds(0, 3)
            else:
                src, dst = pl.ds(3, 3), pl.ds(3 + packed, 3)
            g_copies.append(remote(G1.at[0, src], G1.at[(ny - dy) % ny, dst], device(dx, dy)))
    c_copies = send_y(PC, CLO, CHI, CSL, CSH, 3) + send_x(PC, 3)
    finish(g_copies)
    rows1 = 2 * (packed + 6)
    for k in range(ny):
        for j in range(packed + 6):
            v = G1[k, j]
            for bit in (0, 1):
                f = spread(v, 1, bit)
                F1[2 * j + bit, k * y1 : (k + 1) * y1, :] = f
                P1A[2 * j + bit, k * y1 : (k + 1) * y1, :] = -WEIGHT * f
    sweep(P1A, P1B, F1, 1, rows1 - 1, 1, 2)
    quarter = half // 2
    y2 = ny * y1 // 2
    lane2 = lane_of(y2)
    gathered = None
    for i in range(quarter):
        r = 6 + 2 * i
        tmp2[i] = pair(residual(P1B, F1, r, 1, 2) + residual(P1B, F1, r + 1, 1, 2), 2, 1)
        v = 0.5 * (tmp2[i, pl.ds(0, y2, 2), :] + tmp2[i, pl.ds(1, y2, 2), :])
        gathered = v if gathered is None else jnp.where(lane2 % 4 == i, v, gathered)
    G2[REACH] = gathered
    finish([remote(G2.at[REACH], G2.at[REACH - dx], device(dx, 0)) for dx, dy in friends if dy == 0])
    for s in range(2 * REACH + 1):
        v = G2[s]
        for b0 in (0, 1):
            u = spread(v, 1, b0)
            for b1 in (0, 1):
                f = spread(u, 2, b1)
                F2[4 * s + 2 * b1 + b0] = f
                P2A[4 * s + 2 * b1 + b0] = -WEIGHT * f
    rows2 = 4 * (2 * REACH + 1)
    sweep(P2A, P2B, F2, 1, rows2 - 1, 1, 4)

    def coarse_source(i):
        v = residual(P2B, F2, 2 * i, 1, 4) + residual(P2B, F2, 2 * i + 1, 1, 4)
        f = 0.5 * pair(pair(v, 4, 1), 1, 0)
        return [(F3, i, f), (P3A, i, -WEIGHT * f)]

    loop(1, rows2 // 2 - 1, coarse_source, rows2 // 2 - 2)
    sweep(P3A, P3B, F3, 2, 16, 2, 8)
    sweep(P3B, P3A, F3, 3, 15, 2, 8)
    sweep(P3A, P3B, F3, 4, 14, 2, 8)

    def line_row(r):
        mean = jnp.mean(residual(P3B, F3, r, 2, 8), axis=0, keepdims=True)
        v = P3B[r] - WEIGHT * mean
        return [(P2B, x, P2B[x] + v) for x in (2 * r, 2 * r + 1)]

    loop(6, 12, line_row, 6)
    sweep(P2B, P2A, F2, 13, 23, 1, 4)

    def second_row(m):
        p, around = stencil(P2A, m, 1, 4)
        v = KEEP * p + WEIGHT * (around - F2[m])
        E1[m - 14, pl.ds(0, y2, 2), :] = v
        E1[m - 14, pl.ds(1, y2, 2), :] = v
        e = E1[m - 14]
        r = 2 * (m - 13)
        P1B[r] = P1B[r] + e
        P1B[r + 1] = P1B[r + 1] + e

    for m in range(14, 22):
        second_row(m)
    sweep(P1B, P1A, F1, 3, 17, 1, 2)
    sweep(P1A, P1B, F1, 4, 16, 1, 2)
    finish(c_copies)
    place(PC, CLO, CHI, 3)
    full1 = ny * y1
    for m in range(4, 16):
        e = m - 4
        for shift in (0, 1):
            E0[e, pl.ds(shift, y1, 2), :] = P1B[m, 0:y1, :]
            E0[e, pl.ds(own_y + shift, 2, 2), :] = P1B[m, y1 : y1 + 2, :]
            E0[e, pl.ds(own_y + 4 + shift, 2, 2), :] = P1B[m, full1 - 2 : full1, :]
        for r in (2 * m - 9, 2 * m - 8):
            if 0 <= r < rows:
                PC[r] = PC[r] + E0[e]
    sweep(PC, PA, F, 1, rows - 1, 1, 1, G_FINE)
    sweep(PA, PB, F, 2, rows - 2, 1, 1, G_FINE)

    def out_row(x):
        r = OFF + x
        p = PB[r]
        out = [(pre_out, x, p[0:own_y])]
        gx = (0.5 * STEP) * (PB[r + 1] - PB[r - 1])
        gy = (0.5 * STEP) * (roll(p, -1, 0) - roll(p, 1, 0))
        gz = STEP * (jnp.where(last, p, roll(p, -1, 1)) - jnp.where(first, p, roll(p, 1, 1)))
        for a, g in enumerate((gx, gy, gz)):
            out.append((vel_out, (a, x), (S[a, r] - g)[0:own_y]))
        return out

    loop(0, own_x, out_row, 2)


def per_device(nx, ny, velocity, pressure, land_type, turbine_cells, surface_drag):
    _, own_x, own_y, nz = velocity.shape
    side = (own_y // 8 + 1) * 8
    rows = own_x + 2 * OFF
    window = pltpu.VMEM((rows, side, nz), F32)

    def rims(width, *lead):
        rim = pltpu.VMEM((*lead, own_x + 2 * width, width, nz), F32)
        stage = pltpu.VMEM((*lead, own_x, width, nz), F32)
        return [rim, rim, stage, stage]

    three = pltpu.VMEM((3, rows, side, nz), F32)
    half, quarter = own_x // 2, own_x // 4
    y1 = own_y // 2
    full1, full2 = ny * y1, ny * y1 // 2
    packed = half // 2
    level1 = pltpu.VMEM((2 * (packed + 6), full1, nz), F32)
    rows2 = quarter * (2 * REACH + 1)
    level2 = pltpu.VMEM((rows2, full2, nz), F32)
    level3 = pltpu.VMEM((rows2 // 2, full2, nz), F32)
    count = 5 * 8 + 3 * ny - 1 + 2 * REACH
    scratch = [three] + rims(3, 3) + [window] + rims(1) + [window] + rims(3)
    scratch += [window, window] + rims(3) + [window] + rims(2) + [three, three]
    scratch += [
        pltpu.VMEM((half, own_y, nz), F32),
        pltpu.VMEM((quarter, full1, nz), F32),
        pltpu.VMEM((own_x, own_y, nz), jnp.int32),
        pltpu.VMEM(land_type.shape, jnp.int32),
        pltpu.SMEM(surface_drag.shape, F32),
        pltpu.VMEM((ny, packed + 6, y1, nz), F32),
        level1, level1, level1,
        pltpu.VMEM((2 * REACH + 1, full2, nz), F32),
        level2, level2, level2, level3, level3, level3,
        pltpu.VMEM((8, full1, nz), F32),
        pltpu.VMEM((12, side, nz), F32),
        pltpu.SemaphoreType.DMA((5,)),
        pltpu.SemaphoreType.DMA((count,)),
        pltpu.SemaphoreType.DMA((count,)),
    ]
    inside = pl.BlockSpec(memory_space=pltpu.VMEM)
    velocity, pressure, land_type, turbine_cells, surface_drag = [pltpu.with_memory_space_constraint(a, pltpu.HBM) for a in (velocity, pressure, land_type, turbine_cells, surface_drag)]
    moved = tuple(
        pl.pallas_call(
            functools.partial(kernel, nx, ny),
            out_shape=(
                jax.ShapeDtypeStruct(velocity.shape, F32),
                jax.ShapeDtypeStruct(pressure.shape, F32),
            ),
            in_specs=[pl.BlockSpec(memory_space=pltpu.HBM)] * 5,
            out_specs=(inside, inside),
            scratch_shapes=scratch,
            compiler_params=pltpu.CompilerParams(
                collective_id=0, has_side_effects=True, vmem_limit_bytes=VMEM_LIMIT
            ),
        )(velocity, pressure, turbine_cells, land_type, surface_drag)
    )
    parts = 2
    vel_block = pl.BlockSpec((3, own_x // parts, own_y, nz), lambda i: (0, i, 0, 0))
    pre_block = pl.BlockSpec((own_x // parts, own_y, nz), lambda i: (i, 0, 0))
    return pl.pallas_call(
        hand_over,
        grid=(parts,),
        out_shape=(
            jax.ShapeDtypeStruct(velocity.shape, F32),
            jax.ShapeDtypeStruct(pressure.shape, F32),
        ),
        in_specs=[vel_block, pre_block],
        out_specs=(vel_block, pre_block), compiler_params=pltpu.CompilerParams(vmem_limit_bytes=VMEM_LIMIT),
    )(*moved)


def hand_over(vel_in, pre_in, vel_out, pre_out):
    vel_out[...] = vel_in[...]
    pre_out[...] = pre_in[...]


def solution(mesh):
    in_specs = (
        P(None, "gx", "gy", None),
        P("gx", "gy", None),
        P("gx", "gy"),
        P("gx", "gy", None),
        P(),
    )
    out_specs = (P(None, "gx", "gy", None), P("gx", "gy", None))
    body = functools.partial(per_device, mesh.shape["gx"], mesh.shape["gy"])
    return jax.shard_map(
        body, mesh=mesh, in_specs=in_specs, out_specs=out_specs, check_vma=False
    )
```

```python
import functools

import jax
import jax.numpy as jnp
from jax import lax
from jax.experimental import pallas as pl
from jax.experimental.pallas import tpu as pltpu
from jax.sharding import PartitionSpec as P

MESH = pl.DeviceIdType.MESH
F32 = jnp.float32
STEP = 0.1
WEIGHT = 0.8 / 12.0
KEEP = 0.2
OFF = 3
RIM = 4
G_STRESS = 4
G_FINE = 8
VMEM_LIMIT = 24000 * 1024
REACH = 4


def loop(low, high, body, group):
    def run(indices):
        found = [store for index in indices for store in body(index)]
        for ref, at, value in found:
            ref[at] = value

    whole = (high - low) // group
    if whole == 1:
        run(range(low, low + group))
    elif whole > 1:

        def step(index, carry):
            run([low + index * group + k for k in range(group)])
            return carry

        lax.fori_loop(0, whole, step, 0)
    if low + whole * group < high:
        run(range(low + whole * group, high))


def lane_of(count, nz):
    return lax.broadcasted_iota(jnp.int32, (count, nz), 1)


def row_of(count, nz):
    return lax.broadcasted_iota(jnp.int32, (count, nz), 0)


def roll(v, shift, axis):
    return pltpu.roll(v, shift % v.shape[axis], axis)


def kernel(
    nx, ny, vel_in, pre_in, turb_in, land_in, coeff_in, S, PN,
    W, D, PA, F, T, R0, Z, ZA, ZB, X1, X2, A, Y1, tmp, tmp1, turb, land, coeff,
    H1, H1A, H1B, G1, F1, P1A, P1B, G2, F2, P2A, P2B, F3, P3A, P3B, E1, E0,
    load_sem, send_sem, recv_sem, token,
):
    me_x, me_y = lax.axis_index("gx"), lax.axis_index("gy")
    _, own_x, own_y, nz = vel_in.shape
    side = W.shape[2]
    rows = own_x + 2 * OFF
    half, quarter = own_x // 2, own_x // 4
    y1, y2 = own_y // 2, own_y // 4

    loads = [
        pltpu.make_async_copy(turb_in, turb, load_sem.at[0]),
        pltpu.make_async_copy(land_in, land, load_sem.at[1]),
        pltpu.make_async_copy(coeff_in, coeff, load_sem.at[2]),
        pltpu.make_async_copy(vel_in, W.at[:, OFF : OFF + own_x, 0:own_y], load_sem.at[3]),
        pltpu.make_async_copy(pre_in, PA.at[OFF : OFF + own_x, 0:own_y], load_sem.at[4]),
    ]

    def device(dx, dy):
        return (lax.rem(me_x + dx + nx, nx), lax.rem(me_y + dy + ny, ny))

    far = [(dx, dy) for dx in range(-REACH, REACH + 1) for dy in range(ny) if dx or dy]
    close = [(dx, dy) for dx, dy in far if abs(dx) < 2]
    barrier = pltpu.get_barrier_semaphore()
    for dx, dy in close:
        pl.semaphore_signal(barrier, inc=1, device_id=device(dx, dy), device_id_type=MESH)
    for load in loads:
        load.start()

    used = [0]

    def remote(src, dst, dx, dy):
        slot = used[0]
        used[0] += 1
        copy = pltpu.make_async_remote_copy(
            src_ref=src, dst_ref=dst, send_sem=send_sem.at[slot], recv_sem=recv_sem.at[slot],
            device_id=device(dx, dy), device_id_type=MESH,
        )
        copy.start()
        return copy

    def x_spans(dx, width, src_base, dst_base):
        if dx == 0:
            return slice(src_base, src_base + own_x), slice(dst_base, dst_base + own_x)
        if dx == 1:
            high = src_base + own_x
            return slice(high - width, high), slice(dst_base - width, dst_base)
        return slice(src_base, src_base + width), slice(dst_base + own_x, dst_base + own_x + width)

    def y_spans(dy, width):
        if dy == 0:
            return slice(0, own_y), slice(0, own_y)
        if dy == 1:
            return slice(own_y - width, own_y), slice(side - width, side)
        return slice(0, width), slice(own_y, own_y + width)

    def send(src, dst, src_base, dst_base, width, dx, dy, lead=False):
        sx, tx = x_spans(dx, width, src_base, dst_base)
        sy, ty = y_spans(dy, width)
        if lead:
            return remote(src.at[:, sx, sy], dst.at[:, tx, ty], dx, dy)
        return remote(src.at[sx, sy], dst.at[tx, ty], dx, dy)

    corners = [(dx, dy) for dx in (1, -1) for dy in (1, -1)]
    faces = [(0, 1), (0, -1), (1, 0), (-1, 0)]

    def finish(copies):
        for copy in copies:
            copy.wait()

    def tell(turn):
        for side_of, dx in enumerate((1, -1)):
            pl.semaphore_signal(
                token.at[turn, side_of], inc=1, device_id=device(dx, 0), device_id_type=MESH
            )

    def hear(turn):
        for side_of in range(2):
            pl.semaphore_wait(token.at[turn, side_of], 1)

    pl.semaphore_wait(barrier, len(close))
    w_copies = [send(vel_in, W, 0, OFF, 2, dx, dy, True) for dx, dy in corners]
    w_copies += [send(vel_in, W, 0, OFF, 3, dx, dy, True) for dx, dy in faces]
    p_copies = [send(pre_in, PA, 0, OFF, 1, dx, dy) for dx, dy in faces]
    shape = (own_y, own_y)
    diagonal = lax.broadcasted_iota(jnp.int32, shape, 0) == lax.broadcasted_iota(jnp.int32, shape, 1)
    lane16 = lane_of(own_y, nz)
    loads[1].wait()
    loads[2].wait()
    kinds = land[...]
    ground = jnp.zeros(kinds.shape, F32)
    for kind in range(coeff.shape[0]):
        ground = jnp.where(kinds == kind, coeff[kind], ground)
    loads[0].wait()
    for x in range(own_x):
        column = jnp.sum(jnp.where(diagonal, ground[x : x + 1, :], 0.0), axis=1, keepdims=True)
        low = jnp.where(lane16 == 0, column, 0.0)
        D[OFF + x, 0:own_y, :] = 2.0 * turb[x].astype(F32) + low
    d_copies = [send(D, D, OFF, OFF, 1, dx, dy) for dx, dy in faces]
    blank = jnp.zeros((side, nz), F32)
    for r in (1, 2, rows - 3, rows - 2):
        Z[r] = blank
    for r in (0, 1, rows - 2, rows - 1):
        ZA[r] = blank
    blank1 = jnp.zeros((2 * y1, nz), F32)
    for r in (1, 2, half + 5, half + 6):
        H1[r] = blank1
    for r in (0, 1, half + 6, half + 7):
        H1A[r] = blank1
    for r in (0, half + 7):
        H1B[r] = blank1
    loads[3].wait()
    loads[4].wait()
    finish(w_copies)
    tell(0)
    lane = lane_of(side, nz)
    first, last = lane == 0, lane == nz - 1

    def up0(v):
        return jnp.where(last, 0.0, roll(v, -1, 1))

    def down0(v):
        return jnp.where(first, 0.0, roll(v, 1, 1))

    def stress_row(r):
        v = [W[a, r] for a in range(3)]
        gx = [0.5 * (W[a, r + 1] - W[a, r - 1]) for a in range(3)]
        gy = [0.5 * (roll(v[a], -1, 0) - roll(v[a], 1, 0)) for a in range(3)]
        gz = [up0(v[a]) - down0(v[a]) for a in range(3)]
        e01, e02, e12 = gx[1] + gy[0], gx[2] + gz[0], gy[2] + gz[1]
        q = 2.0 * (gx[0] * gx[0] + gy[1] * gy[1] + gz[2] * gz[2]) + e01 * e01 + e02 * e02 + e12 * e12
        visc = 0.03 * jnp.sqrt(q)
        twice = visc + visc
        t00, t11, t22 = twice * gx[0], twice * gy[1], twice * gz[2]
        t01, t02, t12 = visc * e01, visc * e02, visc * e12
        flat = v[0] * v[0] + v[1] * v[1]
        ghost = 0.03 * jnp.sqrt(2.0 * v[2] * v[2] + flat)
        ghosts = [ghost * v[0], ghost * v[1], (ghost + ghost) * v[2]]
        out = [(T, (0, r), t00), (T, (1, r), t01), (T, (2, r), t02)]
        drag = D[r] * jnp.sqrt(flat)
        for a, (ty, tz) in enumerate(((t01, t02), (t11, t12), (t12, t22))):
            change = 0.5 * (roll(ty, -1, 0) - roll(ty, 1, 0))
            change += jnp.where(last, -ghosts[a], roll(tz, -1, 1)) - jnp.where(first, ghosts[a], roll(tz, 1, 1))
            change -= v[0] * gx[a] + v[1] * gy[a] + v[2] * gz[a]
            if a < 2:
                change -= drag * v[a]
            if a == 0:
                change += 1.0
            out.append((S, (a, r), v[a] + STEP * change))
        return out

    finish(d_copies)
    loop(1, rows - 1, stress_row, G_STRESS)
    hear(0)
    tell(1)

    def star_row(r):
        return [
            (S, (a, r), S[a, r] + (0.5 * STEP) * (T[a, r + 1] - T[a, r - 1])) for a in range(3)
        ]

    loop(2, rows - 2, star_row, G_FINE)
    finish(p_copies)

    def stencil(src, r, sy, sz):
        p = src[r]
        lanes = lane_of(p.shape[0], nz)
        z = jnp.where(lanes >= nz - sz, p, roll(p, -sz, 1)) + jnp.where(lanes < sz, p, roll(p, sz, 1))
        s = src[r + 1] + src[r - 1] + roll(p, -sy, 0) + roll(p, sy, 0)
        return p, s + 4.0 * z

    def smooth(src, r, sy, sz):
        p, around = stencil(src, r, sy, sz)
        return KEEP * p + WEIGHT * around

    def smooth_all(src, dst, low, high, sy, sz, group=64):
        loop(low, high, lambda r: [(dst, r, smooth(src, r, sy, sz))], min(group, high - low))

    def sweep(src, dst, f, low, high, sy, sz, group=64):
        def body(r):
            p, around = stencil(src, r, sy, sz)
            return [(dst, r, KEEP * p + WEIGHT * (around - f[r]))]

        loop(low, high, body, min(group, high - low))

    def residual(src, f, r, sy, sz):
        p, around = stencil(src, r, sy, sz)
        return f[r] - (around - 12.0 * p)

    own = row_of(side, nz) < own_y

    def source_row(r):
        s1, s2 = S[1, r], S[2, r]
        flat = 0.5 * (S[0, r + 1] - S[0, r - 1] + roll(s1, -1, 0) - roll(s1, 1, 0))
        f = (flat + up0(s2) - down0(s2)) / STEP
        p, around = stencil(PA, r, 1, 1)
        left = jnp.where(own, f - (around - 12.0 * p), 0.0)
        return [(Z, r, left), (R0, (r + RIM - OFF, slice(0, own_y)), left[0:own_y])]

    loop(OFF, OFF + own_x, source_row, G_FINE)
    r_copies = [send(R0, R0, RIM, RIM, 3, dx, dy) for dx, dy in corners]
    r_copies += [send(R0, R0, RIM, RIM, RIM, dx, dy) for dx, dy in faces]

    smooth_all(Z, ZA, 2, rows - 2, 1, 1, G_FINE)
    smooth_all(ZA, ZB, 1, rows - 1, 1, 1, G_FINE)

    def pair(v, stride, axis):
        at = lax.broadcasted_iota(jnp.int32, v.shape, axis)
        even = (at // stride) % 2 == 0
        return v + jnp.where(even, roll(v, -stride, axis), roll(v, stride, axis))

    def spread(v, stride, bit):
        at = (lane_of(v.shape[0], nz) // stride) % 2
        return jnp.where(at == bit, v, roll(v, stride if bit == 0 else -stride, 1))

    sub8 = row_of(y1, nz)

    def fine_residual(i):
        v = pair(ZB[2 * i + 1] + ZB[2 * i + 2], 1, 1)
        rim = 0.5 * v[own_y : own_y + 8]
        rim = jnp.where(sub8 == 0, rim + roll(rim, -1, 0), jnp.where(sub8 == 7, rim + roll(rim, 1, 0), 0.0))
        return [(tmp, i, v[0:own_y]), (H1, (i + 3, slice(y1, 2 * y1)), rim)]

    loop(0, half + 2, fine_residual, half + 2)
    for i in range(half + 2):
        H1[i + 3, 0:y1] = 0.5 * (tmp[i, pl.ds(0, y1, 2), :] + tmp[i, pl.ds(1, y1, 2), :])
    packs = half // 2
    lane1 = lane_of(2 * y1, nz)
    even1 = lane1 % 2 == 0
    for i in range(packs):
        G1[0, 1 + i] = jnp.where(even1, H1[4 + 2 * i], H1[5 + 2 * i])
    rim = jnp.where(even1, H1[half + 4], H1[3])
    G1[0, 0] = rim
    G1[0, packs + 1] = rim
    g_copies = []
    kept = 3
    for dx in (1, -1, 0):
        for dy in range(ny):
            if dx == 0 and dy == 0:
                continue
            k = (ny - dy) % ny
            if dx == 0:
                src, dst = pl.ds(0, packs + 1), pl.ds(0, packs + 1)
            elif dx == 1:
                src, dst = pl.ds(packs + 1 - kept, kept + 1), pl.ds(packs + 2, kept + 1)
            else:
                src, dst = pl.ds(0, kept + 1), pl.ds(packs + 3 + kept, kept + 1)
            g_copies.append(remote(G1.at[0, src], G1.at[k, dst], dx, dy))
    hear(1)
    smooth_all(H1, H1A, 2, half + 6, 1, 2)
    smooth_all(H1A, H1B, 1, half + 7, 1, 2)
    lane8 = lane_of(y1, nz)
    for j in range(quarter + 4):
        tmp1[j] = pair(H1B[2 * j] + H1B[2 * j + 1], 2, 1)
    for which, order in enumerate(((2, 3, 4, 5), (6, 7, 0, 1))):
        gathered = None
        for at, j in enumerate(order):
            v = 0.5 * (tmp1[j, pl.ds(0, y1, 2), :] + tmp1[j, pl.ds(1, y1, 2), :])
            gathered = v if gathered is None else jnp.where(lane8 % 4 == at, v, gathered)
        G2[0, REACH, which] = gathered
    h_copies = [
        remote(G2.at[0, REACH], G2.at[(ny - dy) % ny, REACH - dx], dx, dy) for dx, dy in far
    ]
    finish(r_copies)
    wide = own_x + 2 * RIM
    smooth_all(R0, X1, 1, wide - 1, 1, 1, G_FINE)
    smooth_all(X1, X2, 2, wide - 2, 1, 1, G_FINE)

    def base_row(r):
        total = R0[r] + X1[r] + X2[r] + smooth(X2, r, 1, 1)
        return [(A, r - 3, PA[r - RIM + OFF] - WEIGHT * total)]

    loop(3, wide - 3, base_row, G_FINE)
    finish(g_copies)
    full1 = ny * y1
    count1 = packs + 2 * kept

    def joined(k, q):
        if q < 0:
            v = G1[k, packs + 2 + q + kept]
            return v + jnp.where(even1, 0.0, G1[k, 0]) if q == -1 else v
        if q >= packs:
            v = G1[k, packs + 4 + kept + q - packs]
            return v + jnp.where(even1, G1[k, 0], 0.0) if q == packs else v
        v = G1[k, 1 + q]
        if q == 0:
            v = v + jnp.where(even1, G1[k, packs + 2 + kept], 0.0)
        if q == packs - 1:
            v = v + jnp.where(even1, 0.0, G1[k, packs + 3 + kept])
        return v

    for q in range(-kept, packs + kept):
        frames = [joined(k, q) for k in range(ny)]
        for k in range(ny):
            before, after = frames[(k - 1) % ny][y1:], frames[(k + 1) % ny][y1:]
            edge = before if ny == 2 else jnp.where(sub8 < y1 // 2, before, after)
            v = frames[k][0:y1] + edge
            for bit in (0, 1):
                f = spread(v, 1, bit)
                r = 2 * (q + kept) + bit
                F1[r, k * y1 : (k + 1) * y1, :] = f
                P1A[r, k * y1 : (k + 1) * y1, :] = -WEIGHT * f
    sweep(P1A, P1B, F1, 1, 2 * count1 - 1, 1, 2)
    finish(h_copies)
    full2 = ny * y2
    low2 = lane8 % 4 < 2
    blank8 = jnp.zeros((y1, nz), F32)

    def joined2(k, s):
        before = G2[k, s - 1, 1] if s > 0 else blank8
        after = G2[k, s + 1, 1] if s < 2 * REACH else blank8
        return G2[k, s, 0] + jnp.where(low2, before, after)

    for s in range(2 * REACH + 1):
        frames = [joined2(k, s) for k in range(ny)]
        turned = [roll(v, y2, 0) for v in frames]
        for m in range(ny // 2):
            k = 2 * m
            if ny == 2:
                v = frames[0] + turned[1]
            else:
                lower = frames[k] + jnp.where(sub8 < 2, turned[(k - 1) % ny], turned[(k + 1) % ny])
                upper = turned[k + 1] + jnp.where(sub8 < 6, frames[k], frames[(k + 2) % ny])
                v = jnp.where(sub8 < y2, lower, upper)
            for b0 in (0, 1):
                u = spread(v, 1, b0)
                for b1 in (0, 1):
                    f = spread(u, 2, b1)
                    F2[4 * s + 2 * b1 + b0, 8 * m : 8 * m + 8, :] = f
                    P2A[4 * s + 2 * b1 + b0, 8 * m : 8 * m + 8, :] = -WEIGHT * f
    rows2 = 4 * (2 * REACH + 1)
    sweep(P2A, P2B, F2, 1, rows2 - 1, 1, 4)

    def coarse_source(i):
        v = residual(P2B, F2, 2 * i, 1, 4) + residual(P2B, F2, 2 * i + 1, 1, 4)
        f = 0.5 * pair(pair(v, 4, 1), 1, 0)
        return [(F3, i, f), (P3A, i, -WEIGHT * f)]

    loop(1, rows2 // 2 - 1, coarse_source, rows2 // 2 - 2)
    sweep(P3A, P3B, F3, 2, 16, 2, 8)
    sweep(P3B, P3A, F3, 3, 15, 2, 8)
    sweep(P3A, P3B, F3, 4, 14, 2, 8)

    def line_row(r):
        mean = jnp.mean(residual(P3B, F3, r, 2, 8), axis=0, keepdims=True)
        v = P3B[r] - WEIGHT * mean
        return [(P2B, x, P2B[x] + v) for x in (2 * r, 2 * r + 1)]

    loop(6, 12, line_row, 6)
    sweep(P2B, P2A, F2, 13, 23, 1, 4)

    def second_row(m):
        p, around = stencil(P2A, m, 1, 4)
        v = KEEP * p + WEIGHT * (around - F2[m])
        E1[m - 14, pl.ds(0, full2, 2), :] = v
        E1[m - 14, pl.ds(1, full2, 2), :] = v
        e = E1[m - 14]
        r = 2 * (m - 13)
        P1B[r] = P1B[r] + e
        P1B[r + 1] = P1B[r + 1] + e

    for m in range(14, 22):
        second_row(m)
    sweep(P1B, P1A, F1, 3, 17, 1, 2)
    sweep(P1A, P1B, F1, 4, 16, 1, 2)
    for m in range(4, 16):
        e = m - 4
        for shift in (0, 1):
            E0[e, pl.ds(shift, y1, 2), :] = P1B[m, 0:y1, :]
            E0[e, pl.ds(own_y + shift, 2, 2), :] = P1B[m, y1 : y1 + 2, :]
            E0[e, pl.ds(own_y + 4 + shift, 2, 2), :] = P1B[m, full1 - 2 : full1, :]

    def first_pair(e):
        p = E0[e]
        z = jnp.where(last, p, roll(p, -1, 1)) + jnp.where(first, p, roll(p, 1, 1))
        base = (KEEP + WEIGHT) * p + WEIGHT * (roll(p, -1, 0) + roll(p, 1, 0) + 4.0 * z)
        return [
            (Y1, 2 * e - 2, base + WEIGHT * E0[e - 1]),
            (Y1, 2 * e - 1, base + WEIGHT * E0[e + 1]),
        ]

    loop(1, 11, first_pair, 5)
    loop(1, own_x + 3, lambda r: [(PN, r - 1, A[r - 1] + smooth(Y1, r, 1, 1))], 6)


def closing(S, PN, vel_out, pre_out, vel, pre, sem):
    _, own_x, own_y, nz = vel.shape
    lane = lane_of(PN.shape[1], nz)
    first, last = lane == 0, lane == nz - 1
    copies = []
    part = 4
    for low in range(0, own_x, part):
        for x in range(low, low + part):
            p = PN[x + 1]
            pre[x] = p[0:own_y]
            gx = (0.5 * STEP) * (PN[x + 2] - PN[x])
            gy = (0.5 * STEP) * (roll(p, -1, 0) - roll(p, 1, 0))
            gz = STEP * (jnp.where(last, p, roll(p, -1, 1)) - jnp.where(first, p, roll(p, 1, 1)))
            for a, g in enumerate((gx, gy, gz)):
                vel[a, x] = S[a, OFF + x, 0:own_y] - g[0:own_y]
        span = pl.ds(low, part)
        at = len(copies)
        copies.append(pltpu.make_async_copy(vel.at[:, span], vel_out.at[:, span], sem.at[at]))
        copies.append(pltpu.make_async_copy(pre.at[span], pre_out.at[span], sem.at[at + 1]))
        copies[-2].start()
        copies[-1].start()
    for copy in copies:
        copy.wait()


def per_device(nx, ny, velocity, pressure, land_type, turbine_cells, surface_drag):
    _, own_x, own_y, nz = velocity.shape
    side = (own_y // 8 + 1) * 8
    rows = own_x + 2 * OFF
    wide = own_x + 2 * RIM
    half, quarter = own_x // 2, own_x // 4
    y1 = own_y // 2
    full1, full2 = ny * y1, ny * y1 // 2
    packs = half // 2
    rows2 = quarter * (2 * REACH + 1)

    def window(*shape):
        return pltpu.VMEM((*shape, nz), F32)

    level1 = window(2 * (packs + 6), full1)
    level2 = window(rows2, full2)
    level3 = window(rows2 // 2, full2)
    frame1 = window(half + 8, 2 * y1)
    count = 8 + 4 + 4 + 8 + 3 * ny - 1 + (2 * REACH + 1) * ny - 1
    scratch = [
        window(3, rows, side), window(rows, side), window(rows, side), window(rows, side),
        window(3, rows, side), window(wide, side),
        window(rows, side), window(rows, side), window(rows, side),
        window(wide, side), window(wide, side), window(own_x + 2, side), window(own_x + 4, side),
        window(half + 2, own_y), window(quarter + 4, 2 * y1),
        pltpu.VMEM((own_x, own_y, nz), jnp.int32),
        pltpu.VMEM(land_type.shape, jnp.int32),
        pltpu.SMEM(surface_drag.shape, F32),
        frame1, frame1, frame1, window(ny, packs + 10, 2 * y1),
        level1, level1, level1,
        window(ny, 2 * REACH + 1, 2, y1),
        level2, level2, level2, level3, level3, level3,
        window(8, full1), window(12, side),
        pltpu.SemaphoreType.DMA((5,)),
        pltpu.SemaphoreType.DMA((count,)),
        pltpu.SemaphoreType.DMA((count,)),
        pltpu.SemaphoreType.REGULAR((2, 2)),
    ]
    inside = pl.BlockSpec(memory_space=pltpu.VMEM)
    outside = pl.BlockSpec(memory_space=pltpu.HBM)
    arguments = [
        pltpu.with_memory_space_constraint(a, pltpu.HBM)
        for a in (velocity, pressure, turbine_cells, land_type, surface_drag)
    ]
    star, middle = pl.pallas_call(
        functools.partial(kernel, nx, ny),
        out_shape=(
            jax.ShapeDtypeStruct((3, rows, side, nz), F32),
            jax.ShapeDtypeStruct((own_x + 2, side, nz), F32),
        ),
        in_specs=[outside] * 5,
        out_specs=(inside, inside),
        scratch_shapes=scratch,
        compiler_params=pltpu.CompilerParams(
            collective_id=0, has_side_effects=True, vmem_limit_bytes=VMEM_LIMIT
        ),
    )(*arguments)
    return pl.pallas_call(
        closing,
        out_shape=(
            jax.ShapeDtypeStruct(velocity.shape, F32),
            jax.ShapeDtypeStruct(pressure.shape, F32),
        ),
        in_specs=[inside, inside],
        out_specs=(outside, outside),
        scratch_shapes=[
            pltpu.VMEM(velocity.shape, F32),
            pltpu.VMEM(pressure.shape, F32),
            pltpu.SemaphoreType.DMA((2 * own_x // 4,)),
        ],
        compiler_params=pltpu.CompilerParams(vmem_limit_bytes=VMEM_LIMIT),
    )(star, middle)


def solution(mesh):
    in_specs = (
        P(None, "gx", "gy", None),
        P("gx", "gy", None),
        P("gx", "gy"),
        P("gx", "gy", None),
        P(),
    )
    out_specs = (P(None, "gx", "gy", None), P("gx", "gy", None))
    body = functools.partial(per_device, mesh.shape["gx"], mesh.shape["gy"])
    return jax.shard_map(
        body, mesh=mesh, in_specs=in_specs, out_specs=out_specs, check_vma=False
    )
```

```python
import functools
import math

import jax
import jax.numpy as jnp
from jax import lax
from jax.experimental import pallas as pl
from jax.experimental.pallas import tpu as pltpu
from jax.sharding import PartitionSpec as P

MESH = pl.DeviceIdType.MESH
F32 = jnp.float32
STEP = 0.1
WEIGHT = 0.8 / 12.0
KEEP = 0.2
OFF = 3
RIM = 4
G_STRESS = 4
G_FINE = 8
VMEM_LIMIT = 24000 * 1024
REACH = 4


def loop(low, high, body, group):
    def run(indices):
        found = [store for index in indices for store in body(index)]
        for ref, at, value in found:
            ref[at] = value

    whole = (high - low) // group
    if whole == 1:
        run(range(low, low + group))
    elif whole > 1:

        def step(index, carry):
            run([low + index * group + k for k in range(group)])
            return carry

        lax.fori_loop(0, whole, step, 0)
    if low + whole * group < high:
        run(range(low + whole * group, high))


def lane_of(count, nz):
    return lax.broadcasted_iota(jnp.int32, (count, nz), 1)


def row_of(count, nz):
    return lax.broadcasted_iota(jnp.int32, (count, nz), 0)


def roll(v, shift, axis):
    return pltpu.roll(v, shift % v.shape[axis], axis)


def kernel(
    nx, ny, vel_in, pre_in, turb_in, land_in, coeff_in, S, PN,
    W, D, PA, F, T, R0, Z, ZA, X1, X2, A, Y1, tmp, tmp1, turb, land, coeff,
    H1, H1A, G1, F1, P1A, P1B, G2, F2, P2A, P2B, F3, P3A, P3B, E1, E0,
    spare, load_sem, send_sem, recv_sem, token,
):
    me_x, me_y = lax.axis_index("gx"), lax.axis_index("gy")
    _, own_x, own_y, nz = vel_in.shape
    side = W.shape[2]
    rows = own_x + 2 * OFF
    half, quarter = own_x // 2, own_x // 4
    y1, y2 = own_y // 2, own_y // 4

    loads = [
        pltpu.make_async_copy(turb_in, turb, load_sem.at[0]),
        pltpu.make_async_copy(land_in, land, load_sem.at[1]),
        pltpu.make_async_copy(coeff_in, coeff, load_sem.at[2]),
        pltpu.make_async_copy(vel_in, W.at[:, OFF : OFF + own_x, 0:own_y], load_sem.at[3]),
        pltpu.make_async_copy(pre_in, PA.at[OFF : OFF + own_x, 0:own_y], load_sem.at[4]),
    ]

    def device(dx, dy):
        return (lax.rem(me_x + dx + nx, nx), lax.rem(me_y + dy + ny, ny))

    far = [(dx, dy) for dx in range(-REACH, REACH + 1) for dy in range(ny) if dx or dy]
    close = [(dx, dy) for dx, dy in far if abs(dx) < 2]
    barrier = pltpu.get_barrier_semaphore()
    for dx, dy in close:
        pl.semaphore_signal(barrier, inc=1, device_id=device(dx, dy), device_id_type=MESH)
    for load in loads:
        load.start()

    groups, sent = [], []

    def group():
        groups.append(0)
        return len(groups) - 1

    def lines_of(ref):
        return math.prod(ref.shape) // nz

    def remote(src, dst, dx, dy, at):
        groups[at] += lines_of(dst)
        sent.append(lines_of(src))
        pltpu.make_async_remote_copy(
            src_ref=src, dst_ref=dst, send_sem=send_sem.at[0], recv_sem=recv_sem.at[at],
            device_id=device(dx, dy), device_id_type=MESH,
        ).start()

    def await_lines(sem, count):
        part = spare.at[pl.ds(0, count)]
        pltpu.make_async_copy(part, part, sem).wait()

    def finish(at):
        await_lines(recv_sem.at[at], groups[at])

    def x_spans(dx, width, src_base, dst_base):
        if dx == 0:
            return slice(src_base, src_base + own_x), slice(dst_base, dst_base + own_x)
        if dx == 1:
            high = src_base + own_x
            return slice(high - width, high), slice(dst_base - width, dst_base)
        return slice(src_base, src_base + width), slice(dst_base + own_x, dst_base + own_x + width)

    def y_spans(dy, width):
        if dy == 0:
            return slice(0, own_y), slice(0, own_y)
        if dy == 1:
            return slice(own_y - width, own_y), slice(side - width, side)
        return slice(0, width), slice(own_y, own_y + width)

    def send(at, src, dst, src_base, dst_base, width, dx, dy, lead=False):
        sx, tx = x_spans(dx, width, src_base, dst_base)
        sy, ty = y_spans(dy, width)
        if lead:
            remote(src.at[:, sx, sy], dst.at[:, tx, ty], dx, dy, at)
        else:
            remote(src.at[sx, sy], dst.at[tx, ty], dx, dy, at)

    corners = [(dx, dy) for dx in (1, -1) for dy in (1, -1)]
    faces = [(0, 1), (0, -1), (1, 0), (-1, 0)]

    def tell(turn):
        for dx in (1, -1):
            pl.semaphore_signal(token.at[turn], inc=1, device_id=device(dx, 0), device_id_type=MESH)

    def hear(turn):
        pl.semaphore_wait(token.at[turn], 2)

    pl.semaphore_wait(barrier, len(close))
    tell(0)
    quart = own_x // 4
    inner = (own_x - 2 * quart + 2) // 3
    cuts = [(0, quart), (own_x - quart, own_x)]
    cuts += [(low, min(low + inner, own_x - quart)) for low in range(quart, own_x - quart, inner)]

    def slab(cut):
        low, high = cut
        at = group()
        for dy in (1, -1):
            sy, ty = y_spans(dy, 3)
            remote(vel_in.at[:, low:high, sy], W.at[:, OFF + low : OFF + high, ty], 0, dy, at)
        return at

    w_copies = group()
    for dx, dy in corners:
        send(w_copies, vel_in, W, 0, OFF, 2, dx, dy, True)
    for dx in (1, -1):
        send(w_copies, vel_in, W, 0, OFF, 3, dx, 0, True)
    slabs = [slab(cut) for cut in cuts[:2]]
    shape = (own_y, own_y)
    diagonal = lax.broadcasted_iota(jnp.int32, shape, 0) == lax.broadcasted_iota(jnp.int32, shape, 1)
    lane16 = lane_of(own_y, nz)
    loads[1].wait()
    loads[2].wait()
    kinds = land[...]
    ground = jnp.zeros(kinds.shape, F32)
    for kind in range(coeff.shape[0]):
        ground = jnp.where(kinds == kind, coeff[kind], ground)
    loads[0].wait()
    for x in range(own_x):
        column = jnp.sum(jnp.where(diagonal, ground[x : x + 1, :], 0.0), axis=1, keepdims=True)
        low = jnp.where(lane16 == 0, column, 0.0)
        D[OFF + x, 0:own_y, :] = 2.0 * turb[x].astype(F32) + low
    slabs += [slab(cut) for cut in cuts[2:-1]]
    d_copies = group()
    for dx, dy in faces:
        send(d_copies, D, D, OFF, OFF, 1, dx, dy)
    slabs += [slab(cut) for cut in cuts[-1:]]
    p_copies = group()
    for dx, dy in faces:
        send(p_copies, pre_in, PA, 0, OFF, 1, dx, dy)
    blank = jnp.zeros((side, nz), F32)
    for r in (1, 2, rows - 3, rows - 2):
        Z[r] = blank
    for r in (0, 1, rows - 2, rows - 1):
        ZA[r] = blank
    blank1 = jnp.zeros((2 * y1, nz), F32)
    for r in (1, 2, half + 5, half + 6):
        H1[r] = blank1
    for r in (0, 1, 2, half + 7, half + 8, half + 9):
        H1A[r] = blank1
    loads[3].wait()
    loads[4].wait()
    hear(0)
    tell(1)
    finish(w_copies)
    lane = lane_of(side, nz)
    first, last = lane == 0, lane == nz - 1

    def up0(v):
        return jnp.where(last, 0.0, roll(v, -1, 1))

    def down0(v):
        return jnp.where(first, 0.0, roll(v, 1, 1))

    def stress_row(r):
        v = [W[a, r] for a in range(3)]
        gx = [0.5 * (W[a, r + 1] - W[a, r - 1]) for a in range(3)]
        gy = [0.5 * (roll(v[a], -1, 0) - roll(v[a], 1, 0)) for a in range(3)]
        gz = [up0(v[a]) - down0(v[a]) for a in range(3)]
        e01, e02, e12 = gx[1] + gy[0], gx[2] + gz[0], gy[2] + gz[1]
        q = 2.0 * (gx[0] * gx[0] + gy[1] * gy[1] + gz[2] * gz[2]) + e01 * e01 + e02 * e02 + e12 * e12
        visc = 0.03 * jnp.sqrt(q)
        twice = visc + visc
        t00, t11, t22 = twice * gx[0], twice * gy[1], twice * gz[2]
        t01, t02, t12 = visc * e01, visc * e02, visc * e12
        flat = v[0] * v[0] + v[1] * v[1]
        ghost = 0.03 * jnp.sqrt(2.0 * v[2] * v[2] + flat)
        ghosts = [ghost * v[0], ghost * v[1], (ghost + ghost) * v[2]]
        out = [(T, (0, r), t00), (T, (1, r), t01), (T, (2, r), t02)]
        for a, (ty, tz) in enumerate(((t01, t02), (t11, t12), (t12, t22))):
            change = 0.5 * (roll(ty, -1, 0) - roll(ty, 1, 0))
            change += jnp.where(last, -ghosts[a], roll(tz, -1, 1)) - jnp.where(first, ghosts[a], roll(tz, 1, 1))
            change -= v[0] * gx[a] + v[1] * gy[a] + v[2] * gz[a]
            if a == 0:
                change += 1.0
            out.append((S, (a, r), v[a] + STEP * change))
        return out

    there = set(range(OFF)) | set(range(OFF + own_x, rows))
    waiting = list(range(1, rows - 1))
    for at, (cut, copies) in enumerate(zip(cuts, slabs)):
        finish(copies)
        if at == 1:
            hear(1)
            tell(2)
        there |= set(range(OFF + cut[0], OFF + cut[1]))
        ready = [r for r in waiting if {r - 1, r, r + 1} <= there]
        waiting = [r for r in waiting if r not in ready]
        for low in [r for r in ready if r - 1 not in ready]:
            high = low
            while high in ready:
                high += 1
            loop(low, high, stress_row, G_STRESS)
    finish(d_copies)

    def star_row(r):
        drag = STEP * (D[r] * jnp.sqrt(W[0, r] * W[0, r] + W[1, r] * W[1, r]))
        stores = []
        for a in range(3):
            v = S[a, r] + (0.5 * STEP) * (T[a, r + 1] - T[a, r - 1])
            stores.append((S, (a, r), v - drag * W[a, r] if a < 2 else v))
        return stores

    loop(2, rows - 2, star_row, G_FINE)
    finish(p_copies)

    def stencil(src, r, sy, sz):
        p = src[r]
        lanes = lane_of(p.shape[0], nz)
        z = jnp.where(lanes >= nz - sz, p, roll(p, -sz, 1)) + jnp.where(lanes < sz, p, roll(p, sz, 1))
        s = src[r + 1] + src[r - 1] + roll(p, -sy, 0) + roll(p, sy, 0)
        return p, s + 4.0 * z

    def smooth(src, r, sy, sz):
        p, around = stencil(src, r, sy, sz)
        return KEEP * p + WEIGHT * around

    def smooth_all(src, dst, low, high, sy, sz, group=64):
        loop(low, high, lambda r: [(dst, r, smooth(src, r, sy, sz))], min(group, high - low))

    def sweep(src, dst, f, low, high, sy, sz, group=64):
        def body(r):
            p, around = stencil(src, r, sy, sz)
            return [(dst, r, KEEP * p + WEIGHT * (around - f[r]))]

        loop(low, high, body, min(group, high - low))

    def residual(src, f, r, sy, sz):
        p, around = stencil(src, r, sy, sz)
        return f[r] - (around - 12.0 * p)

    own = row_of(side, nz) < own_y

    def source_row(r):
        s1, s2 = S[1, r], S[2, r]
        flat = 0.5 * (S[0, r + 1] - S[0, r - 1] + roll(s1, -1, 0) - roll(s1, 1, 0))
        f = (flat + up0(s2) - down0(s2)) / STEP
        p, around = stencil(PA, r, 1, 1)
        left = jnp.where(own, f - (around - 12.0 * p), 0.0)
        return [(Z, r, left), (R0, (r + RIM - OFF, slice(0, own_y)), left[0:own_y])]

    loop(OFF, OFF + own_x, source_row, G_FINE)
    r_copies = group()
    for dx, dy in corners:
        send(r_copies, R0, R0, RIM, RIM, 3, dx, dy)
    for dx, dy in faces:
        send(r_copies, R0, R0, RIM, RIM, RIM, dx, dy)

    smooth_all(Z, ZA, 2, rows - 2, 1, 1, G_FINE)

    def pair(v, stride, axis):
        at = lax.broadcasted_iota(jnp.int32, v.shape, axis)
        even = (at // stride) % 2 == 0
        return v + jnp.where(even, roll(v, -stride, axis), roll(v, stride, axis))

    def spread(v, stride, bit):
        at = (lane_of(v.shape[0], nz) // stride) % 2
        return jnp.where(at == bit, v, roll(v, stride if bit == 0 else -stride, 1))

    sub8 = row_of(y1, nz)

    def smooth_pair(src, r, sy, sz):
        a, b = src[r], src[r + 1]
        p = a + b
        lanes = lane_of(p.shape[0], nz)
        z = jnp.where(lanes >= nz - sz, p, roll(p, -sz, 1)) + jnp.where(lanes < sz, p, roll(p, sz, 1))
        around = p + src[r - 1] + src[r + 2] + roll(p, -sy, 0) + roll(p, sy, 0) + 4.0 * z
        return KEEP * p + WEIGHT * around

    def fine_residual(i):
        v = pair(smooth_pair(ZA, 2 * i + 1, 1, 1), 1, 1)
        rim = 0.5 * v[own_y : own_y + 8]
        rim = jnp.where(sub8 == 0, rim + roll(rim, -1, 0), jnp.where(sub8 == 7, rim + roll(rim, 1, 0), 0.0))
        return [(tmp, i, v[0:own_y]), (H1, (i + 3, slice(y1, 2 * y1)), rim)]

    loop(0, half + 2, fine_residual, (half + 2) // 2)
    for i in range(half + 2):
        H1[i + 3, 0:y1] = 0.5 * (tmp[i, pl.ds(0, y1, 2), :] + tmp[i, pl.ds(1, y1, 2), :])
    packs = half // 2
    lane1 = lane_of(2 * y1, nz)
    even1 = lane1 % 2 == 0
    even = lane_of(y1 + 2, nz) % 2 == 0
    def put(slot, v):
        G1[0, slot, 0:y1] = v[0:y1]
        G1[0, slot, y1 : y1 + 1] = v[y1 : y1 + 1]
        G1[0, slot, y1 + 1 : y1 + 2] = v[2 * y1 - 1 : 2 * y1]

    for i in range(packs):
        put(1 + i, jnp.where(even1, H1[4 + 2 * i], H1[5 + 2 * i]))
    rim = jnp.where(even1, H1[half + 4], H1[3])
    put(0, rim)
    put(packs + 1, rim)
    loop(2, half + 6, lambda r: [(H1A, r + 1, smooth(H1, r, 1, 2))], half + 4)
    lane8 = lane_of(y1, nz)
    for j in range(quarter + 4):
        tmp1[j] = pair(smooth_pair(H1A, 2 * j + 1, 1, 2), 2, 1)
    for which, order in enumerate(((2, 3, 4, 5), (6, 7, 0, 1))):
        gathered = None
        for at, j in enumerate(order):
            v = 0.5 * (tmp1[j, pl.ds(0, y1, 2), :] + tmp1[j, pl.ds(1, y1, 2), :])
            gathered = v if gathered is None else jnp.where(lane8 % 4 == at, v, gathered)
        G2[0, REACH, which] = gathered
    hear(2)
    h_copies = group()
    for dx, dy in far:
        remote(G2.at[0, REACH], G2.at[(ny - dy) % ny, REACH - dx], dx, dy, h_copies)
    g_copies = group()
    kept = 3
    for dx in (1, -1, 0):
        for dy in range(ny):
            if dx == 0 and dy == 0:
                continue
            k = (ny - dy) % ny
            if dx == 0:
                src, dst = pl.ds(0, packs + 1), pl.ds(0, packs + 1)
            elif dx == 1:
                src, dst = pl.ds(packs + 1 - kept, kept + 1), pl.ds(packs + 2, kept + 1)
            else:
                src, dst = pl.ds(0, kept + 1), pl.ds(packs + 3 + kept, kept + 1)
            remote(G1.at[0, src], G1.at[k, dst], dx, dy, g_copies)
    finish(r_copies)
    wide = own_x + 2 * RIM
    smooth_all(R0, X1, 1, wide - 1, 1, 1, G_FINE)
    smooth_all(X1, X2, 2, wide - 2, 1, 1, G_FINE)

    def base_row(r):
        total = R0[r] + X1[r] + X2[r] + smooth(X2, r, 1, 1)
        return [(A, r - 3, PA[r - RIM + OFF] - WEIGHT * total)]

    loop(3, wide - 3, base_row, G_FINE)
    finish(h_copies)
    full2 = ny * y2
    low2 = lane8 % 4 < 2
    blank8 = jnp.zeros((y1, nz), F32)

    def joined2(k, s):
        before = G2[k, s - 1, 1] if s > 0 else blank8
        after = G2[k, s + 1, 1] if s < 2 * REACH else blank8
        return G2[k, s, 0] + jnp.where(low2, before, after)

    for s in range(2 * REACH + 1):
        frames = [joined2(k, s) for k in range(ny)]
        turned = [roll(v, y2, 0) for v in frames]
        for m in range(ny // 2):
            k = 2 * m
            if ny == 2:
                v = frames[0] + turned[1]
            else:
                lower = frames[k] + jnp.where(sub8 < 2, turned[(k - 1) % ny], turned[(k + 1) % ny])
                upper = turned[k + 1] + jnp.where(sub8 < 6, frames[k], frames[(k + 2) % ny])
                v = jnp.where(sub8 < y2, lower, upper)
            for b0 in (0, 1):
                u = spread(v, 1, b0)
                for b1 in (0, 1):
                    f = spread(u, 2, b1)
                    F2[4 * s + 2 * b1 + b0, 8 * m : 8 * m + 8, :] = f
                    P2A[4 * s + 2 * b1 + b0, 8 * m : 8 * m + 8, :] = -WEIGHT * f
    rows2 = 4 * (2 * REACH + 1)
    sweep(P2A, P2B, F2, 1, rows2 - 1, 1, 4)

    def coarse_source(i):
        v = residual(P2B, F2, 2 * i, 1, 4) + residual(P2B, F2, 2 * i + 1, 1, 4)
        f = 0.5 * pair(pair(v, 4, 1), 1, 0)
        return [(F3, i, f), (P3A, i, -WEIGHT * f)]

    loop(1, rows2 // 2 - 1, coarse_source, rows2 // 2 - 2)
    sweep(P3A, P3B, F3, 2, 16, 2, 8)
    sweep(P3B, P3A, F3, 3, 15, 2, 8)
    sweep(P3A, P3B, F3, 4, 14, 2, 8)

    def line_row(r):
        mean = jnp.mean(residual(P3B, F3, r, 2, 8), axis=0, keepdims=True)
        v = P3B[r] - WEIGHT * mean
        return [(P2B, x, P2B[x] + v) for x in (2 * r, 2 * r + 1)]

    loop(6, 12, line_row, 6)
    finish(g_copies)
    full1 = ny * y1
    count1 = packs + 2 * kept

    def joined(k, q):
        if q < 0:
            v = G1[k, packs + 2 + q + kept]
            return v + jnp.where(even, 0.0, G1[k, 0]) if q == -1 else v
        if q >= packs:
            v = G1[k, packs + 4 + kept + q - packs]
            return v + jnp.where(even, G1[k, 0], 0.0) if q == packs else v
        v = G1[k, 1 + q]
        if q == 0:
            v = v + jnp.where(even, G1[k, packs + 2 + kept], 0.0)
        if q == packs - 1:
            v = v + jnp.where(even, 0.0, G1[k, packs + 3 + kept])
        return v

    for q in range(-kept, packs + kept):
        frames = [joined(k, q) for k in range(ny)]
        for k in range(ny):
            before, after = frames[(k - 1) % ny], frames[(k + 1) % ny]
            v = frames[k][0:y1] + jnp.where(sub8 == 0, before[y1 : y1 + 1], 0.0)
            v = v + jnp.where(sub8 == y1 - 1, after[y1 + 1 : y1 + 2], 0.0)
            for bit in (0, 1):
                f = spread(v, 1, bit)
                r = 2 * (q + kept) + bit
                F1[r, k * y1 : (k + 1) * y1, :] = f
                P1A[r, k * y1 : (k + 1) * y1, :] = -WEIGHT * f
    sweep(P1A, P1B, F1, 1, 2 * count1 - 1, 1, 2)
    sweep(P2B, P2A, F2, 13, 23, 1, 4)

    def second_row(m):
        p, around = stencil(P2A, m, 1, 4)
        v = KEEP * p + WEIGHT * (around - F2[m])
        E1[m - 14, pl.ds(0, full2, 2), :] = v
        E1[m - 14, pl.ds(1, full2, 2), :] = v
        e = E1[m - 14]
        r = 2 * (m - 13)
        P1B[r] = P1B[r] + e
        P1B[r + 1] = P1B[r + 1] + e

    for m in range(14, 22):
        second_row(m)
    sweep(P1B, P1A, F1, 3, 17, 1, 2)
    sweep(P1A, P1B, F1, 4, 16, 1, 2)
    for m in range(4, 16):
        e = m - 4
        for shift in (0, 1):
            E0[e, pl.ds(shift, y1, 2), :] = P1B[m, 0:y1, :]
            E0[e, pl.ds(own_y + shift, 2, 2), :] = P1B[m, y1 : y1 + 2, :]
            E0[e, pl.ds(own_y + 4 + shift, 2, 2), :] = P1B[m, full1 - 2 : full1, :]

    def first_pair(e):
        p = E0[e]
        z = jnp.where(last, p, roll(p, -1, 1)) + jnp.where(first, p, roll(p, 1, 1))
        base = (KEEP + WEIGHT) * p + WEIGHT * (roll(p, -1, 0) + roll(p, 1, 0) + 4.0 * z)
        return [
            (Y1, 2 * e - 2, base + WEIGHT * E0[e - 1]),
            (Y1, 2 * e - 1, base + WEIGHT * E0[e + 1]),
        ]

    loop(1, 11, first_pair, 5)
    loop(1, own_x + 3, lambda r: [(PN, r - 1, A[r - 1] + smooth(Y1, r, 1, 1))], 6)
    await_lines(send_sem.at[0], sum(sent))


def closing(S, PN, vel_out, pre_out, vel, pre, sem):
    _, own_x, own_y, nz = vel.shape
    lane = lane_of(PN.shape[1], nz)
    first, last = lane == 0, lane == nz - 1
    part = 4
    for low in range(0, own_x, part):
        for x in range(low, low + part):
            p = PN[x + 1]
            pre[x] = p[0:own_y]
            gx = (0.5 * STEP) * (PN[x + 2] - PN[x])
            gy = (0.5 * STEP) * (roll(p, -1, 0) - roll(p, 1, 0))
            gz = STEP * (jnp.where(last, p, roll(p, -1, 1)) - jnp.where(first, p, roll(p, 1, 1)))
            for a, g in enumerate((gx, gy, gz)):
                vel[a, x] = S[a, OFF + x, 0:own_y] - g[0:own_y]
        span = pl.ds(low, part)
        pltpu.make_async_copy(vel.at[:, span], vel_out.at[:, span], sem.at[0]).start()
        pltpu.make_async_copy(pre.at[span], pre_out.at[span], sem.at[1]).start()
    pltpu.make_async_copy(vel, vel_out, sem.at[0]).wait()
    pltpu.make_async_copy(pre, pre_out, sem.at[1]).wait()


def per_device(nx, ny, velocity, pressure, land_type, turbine_cells, surface_drag):
    _, own_x, own_y, nz = velocity.shape
    side = (own_y // 8 + 1) * 8
    rows = own_x + 2 * OFF
    wide = own_x + 2 * RIM
    half, quarter = own_x // 2, own_x // 4
    y1 = own_y // 2
    full1, full2 = ny * y1, ny * y1 // 2
    packs = half // 2
    rows2 = quarter * (2 * REACH + 1)

    def window(*shape):
        return pltpu.VMEM((*shape, nz), F32)

    level1 = window(2 * (packs + 6), full1)
    level2 = window(rows2, full2)
    level3 = window(rows2 // 2, full2)
    frame1 = window(half + 8, 2 * y1)
    corner, face = 4 * (3 * 2 * 2 + 3 * 3), 2 * (own_x + own_y)
    total = corner + face * (3 * 3 + 1 + 1 + RIM)
    total += 5 * (y1 + 2) * 3 * ny + (2 * REACH + 1) * ny * 2 * y1
    scratch = [
        window(3, rows, side), window(rows, side), window(rows, side), window(rows, side),
        window(3, rows, side), window(wide, side),
        window(rows, side), window(rows, side),
        window(wide, side), window(wide, side), window(own_x + 2, side), window(own_x + 4, side),
        window(half + 2, own_y), window(quarter + 4, 2 * y1),
        pltpu.VMEM((own_x, own_y, nz), jnp.int32),
        pltpu.VMEM(land_type.shape, jnp.int32),
        pltpu.SMEM(surface_drag.shape, F32),
        frame1, window(half + 10, 2 * y1), window(ny, packs + 10, y1 + 2),
        level1, level1, level1,
        window(ny, 2 * REACH + 1, 2, y1),
        level2, level2, level2, level3, level3, level3,
        window(8, full1), window(12, side),
        window(total),
        pltpu.SemaphoreType.DMA((5,)),
        pltpu.SemaphoreType.DMA((1,)),
        pltpu.SemaphoreType.DMA((11,)),
        pltpu.SemaphoreType.REGULAR((3,)),
    ]
    inside = pl.BlockSpec(memory_space=pltpu.VMEM)
    outside = pl.BlockSpec(memory_space=pltpu.HBM)
    arguments = [
        pltpu.with_memory_space_constraint(a, pltpu.HBM)
        for a in (velocity, pressure, turbine_cells, land_type, surface_drag)
    ]
    star, middle = pl.pallas_call(
        functools.partial(kernel, nx, ny),
        out_shape=(
            jax.ShapeDtypeStruct((3, rows, side, nz), F32),
            jax.ShapeDtypeStruct((own_x + 2, side, nz), F32),
        ),
        in_specs=[outside] * 5,
        out_specs=(inside, inside),
        scratch_shapes=scratch,
        compiler_params=pltpu.CompilerParams(
            collective_id=0, has_side_effects=True, vmem_limit_bytes=VMEM_LIMIT
        ),
    )(*arguments)
    return pl.pallas_call(
        closing,
        out_shape=(
            jax.ShapeDtypeStruct(velocity.shape, F32),
            jax.ShapeDtypeStruct(pressure.shape, F32),
        ),
        in_specs=[inside, inside],
        out_specs=(outside, outside),
        scratch_shapes=[
            pltpu.VMEM(velocity.shape, F32),
            pltpu.VMEM(pressure.shape, F32),
            pltpu.SemaphoreType.DMA((2,)),
        ],
        compiler_params=pltpu.CompilerParams(vmem_limit_bytes=VMEM_LIMIT),
    )(star, middle)


def solution(mesh):
    in_specs = (
        P(None, "gx", "gy", None),
        P("gx", "gy", None),
        P("gx", "gy"),
        P("gx", "gy", None),
        P(),
    )
    out_specs = (P(None, "gx", "gy", None), P("gx", "gy", None))
    body = functools.partial(per_device, mesh.shape["gx"], mesh.shape["gy"])
    return jax.shard_map(
        body, mesh=mesh, in_specs=in_specs, out_specs=out_specs, check_vma=False
    )
```

```python
import functools
import math

import jax
import jax.numpy as jnp
from jax import lax
from jax.experimental import pallas as pl
from jax.experimental.pallas import tpu as pltpu
from jax.sharding import PartitionSpec as P

MESH = pl.DeviceIdType.MESH
F32 = jnp.float32
STEP = 0.1
WEIGHT = 0.8 / 12.0
KEEP = 0.2
OFF = 3
RIM = 4
G_STRESS = 4
G_FINE = 8
VMEM_LIMIT = 24000 * 1024
REACH = 4


def loop(low, high, body, group):
    def run(indices):
        found = [store for index in indices for store in body(index)]
        for ref, at, value in found:
            ref[at] = value

    whole = (high - low) // group
    if whole == 1:
        run(range(low, low + group))
    elif whole > 1:

        def step(index, carry):
            run([low + index * group + k for k in range(group)])
            return carry

        lax.fori_loop(0, whole, step, 0)
    if low + whole * group < high:
        run(range(low + whole * group, high))


def lane_of(count, nz):
    return lax.broadcasted_iota(jnp.int32, (count, nz), 1)


def row_of(count, nz):
    return lax.broadcasted_iota(jnp.int32, (count, nz), 0)


def roll(v, shift, axis):
    return pltpu.roll(v, shift % v.shape[axis], axis)


def kernel(
    nx, ny, vel_in, pre_in, turb_in, land_in, coeff_in, S, PN,
    W, D, PA, F, T, R0, Z, ZA, X1, X2, A, Y1, tmp, tmp1, turb, land, coeff,
    H1, H1A, G1, F1, P1A, P1B, G2, GX, F2, P2A, P2B, F3, P3A, P3B, E1, E0,
    spare, load_sem, send_sem, recv_sem, token,
):
    me_x, me_y = lax.axis_index("gx"), lax.axis_index("gy")
    _, own_x, own_y, nz = vel_in.shape
    side = W.shape[2]
    rows = own_x + 2 * OFF
    half, quarter = own_x // 2, own_x // 4
    y1, y2 = own_y // 2, own_y // 4

    loads = [
        pltpu.make_async_copy(turb_in, turb, load_sem.at[0]),
        pltpu.make_async_copy(land_in, land, load_sem.at[1]),
        pltpu.make_async_copy(coeff_in, coeff, load_sem.at[2]),
        pltpu.make_async_copy(vel_in, W.at[:, OFF : OFF + own_x, 0:own_y], load_sem.at[3]),
        pltpu.make_async_copy(pre_in, PA.at[OFF : OFF + own_x, 0:own_y], load_sem.at[4]),
    ]

    def device(dx, dy):
        return (lax.rem(me_x + dx + nx, nx), lax.rem(me_y + dy + ny, ny))

    far = [(dx, dy) for dx in range(-REACH, REACH + 1) for dy in range(ny) if dx or dy]
    close = [(dx, dy) for dx, dy in far if abs(dx) < 2]
    barrier = pltpu.get_barrier_semaphore()
    for dx, dy in close:
        pl.semaphore_signal(barrier, inc=1, device_id=device(dx, dy), device_id_type=MESH)
    for load in loads:
        load.start()

    groups, sent = [], []

    def group():
        groups.append(0)
        return len(groups) - 1

    def lines_of(ref):
        return math.prod(ref.shape) // nz

    def remote(src, dst, dx, dy, at):
        groups[at] += lines_of(dst)
        sent.append(lines_of(src))
        pltpu.make_async_remote_copy(
            src_ref=src, dst_ref=dst, send_sem=send_sem.at[0], recv_sem=recv_sem.at[at],
            device_id=device(dx, dy), device_id_type=MESH,
        ).start()

    def await_lines(sem, count):
        part = spare.at[pl.ds(0, count)]
        pltpu.make_async_copy(part, part, sem).wait()

    def finish(at):
        await_lines(recv_sem.at[at], groups[at])

    def x_spans(dx, width, src_base, dst_base):
        if dx == 0:
            return slice(src_base, src_base + own_x), slice(dst_base, dst_base + own_x)
        if dx == 1:
            high = src_base + own_x
            return slice(high - width, high), slice(dst_base - width, dst_base)
        return slice(src_base, src_base + width), slice(dst_base + own_x, dst_base + own_x + width)

    def y_spans(dy, width):
        if dy == 0:
            return slice(0, own_y), slice(0, own_y)
        if dy == 1:
            return slice(own_y - width, own_y), slice(side - width, side)
        return slice(0, width), slice(own_y, own_y + width)

    def send(at, src, dst, src_base, dst_base, width, dx, dy, lead=False):
        sx, tx = x_spans(dx, width, src_base, dst_base)
        sy, ty = y_spans(dy, width)
        if lead:
            remote(src.at[:, sx, sy], dst.at[:, tx, ty], dx, dy, at)
        else:
            remote(src.at[sx, sy], dst.at[tx, ty], dx, dy, at)

    corners = [(dx, dy) for dx in (1, -1) for dy in (1, -1)]
    faces = [(0, 1), (0, -1), (1, 0), (-1, 0)]

    def tell(turn):
        for dx in (1, -1):
            pl.semaphore_signal(token.at[turn], inc=1, device_id=device(dx, 0), device_id_type=MESH)

    def hear(turn):
        pl.semaphore_wait(token.at[turn], 2)

    pl.semaphore_wait(barrier, len(close))
    tell(0)
    piece = own_x // 4
    low_end, high_end = 2 * piece, own_x - own_x // 8
    middle = (low_end + high_end) // 2
    cuts = [(0, piece), (piece, low_end), (low_end, middle), (middle, high_end), (high_end, own_x)]

    def slab(cut):
        low, high = cut
        at = group()
        for dy in (1, -1):
            sy, ty = y_spans(dy, 3)
            remote(vel_in.at[:, low:high, sy], W.at[:, OFF + low : OFF + high, ty], 0, dy, at)
        return at

    w_copies = group()
    for dx, dy in corners:
        send(w_copies, vel_in, W, 0, OFF, 2, dx, dy, True)
    for dx in (1, -1):
        send(w_copies, vel_in, W, 0, OFF, 3, dx, 0, True)
    slabs = [slab(cut) for cut in cuts[:2]]
    shape = (own_y, own_y)
    diagonal = lax.broadcasted_iota(jnp.int32, shape, 0) == lax.broadcasted_iota(jnp.int32, shape, 1)
    lane16 = lane_of(own_y, nz)
    loads[1].wait()
    loads[2].wait()
    kinds = land[...]
    ground = jnp.zeros(kinds.shape, F32)
    for kind in range(coeff.shape[0]):
        ground = jnp.where(kinds == kind, coeff[kind], ground)
    loads[0].wait()
    for x in range(own_x):
        column = jnp.sum(jnp.where(diagonal, ground[x : x + 1, :], 0.0), axis=1, keepdims=True)
        low = jnp.where(lane16 == 0, column, 0.0)
        D[OFF + x, 0:own_y, :] = 2.0 * turb[x].astype(F32) + low
    d_copies = group()
    for dx, dy in faces:
        send(d_copies, D, D, OFF, OFF, 1, dx, dy)
    p_copies = group()
    for dx, dy in faces:
        send(p_copies, pre_in, PA, 0, OFF, 1, dx, dy)
    slabs += [slab(cut) for cut in cuts[2:]]
    blank = jnp.zeros((side, nz), F32)
    for r in (1, 2, rows - 3, rows - 2):
        Z[r] = blank
    for r in (0, 1, rows - 2, rows - 1):
        ZA[r] = blank
    blank1 = jnp.zeros((2 * y1, nz), F32)
    for r in (1, 2, half + 5, half + 6):
        H1[r] = blank1
    for r in (0, 1, 2, half + 7, half + 8, half + 9):
        H1A[r] = blank1
    loads[3].wait()
    loads[4].wait()
    hear(0)
    tell(1)
    lane = lane_of(side, nz)
    first, last = lane == 0, lane == nz - 1

    def up0(v):
        return jnp.where(last, 0.0, roll(v, -1, 1))

    def down0(v):
        return jnp.where(first, 0.0, roll(v, 1, 1))

    def stress_row(r):
        v = [W[a, r] for a in range(3)]
        gx = [0.5 * (W[a, r + 1] - W[a, r - 1]) for a in range(3)]
        gy = [0.5 * (roll(v[a], -1, 0) - roll(v[a], 1, 0)) for a in range(3)]
        gz = [up0(v[a]) - down0(v[a]) for a in range(3)]
        e01, e02, e12 = gx[1] + gy[0], gx[2] + gz[0], gy[2] + gz[1]
        q = 2.0 * (gx[0] * gx[0] + gy[1] * gy[1] + gz[2] * gz[2]) + e01 * e01 + e02 * e02 + e12 * e12
        visc = 0.03 * jnp.sqrt(q)
        twice = visc + visc
        t00, t11, t22 = twice * gx[0], twice * gy[1], twice * gz[2]
        t01, t02, t12 = visc * e01, visc * e02, visc * e12
        flat = v[0] * v[0] + v[1] * v[1]
        ghost = 0.03 * jnp.sqrt(2.0 * v[2] * v[2] + flat)
        ghosts = [ghost * v[0], ghost * v[1], (ghost + ghost) * v[2]]
        out = [(T, (0, r), t00), (T, (1, r), t01), (T, (2, r), t02)]
        for a, (ty, tz) in enumerate(((t01, t02), (t11, t12), (t12, t22))):
            change = 0.5 * (roll(ty, -1, 0) - roll(ty, 1, 0))
            change += jnp.where(last, -ghosts[a], roll(tz, -1, 1)) - jnp.where(first, ghosts[a], roll(tz, 1, 1))
            change -= v[0] * gx[a] + v[1] * gy[a] + v[2] * gz[a]
            if a == 0:
                change += 1.0
            out.append((S, (a, r), v[a] + STEP * change))
        return out

    def star_row(r):
        drag = STEP * (D[r] * jnp.sqrt(W[0, r] * W[0, r] + W[1, r] * W[1, r]))
        stores = []
        for a in range(3):
            v = S[a, r] + (0.5 * STEP) * (T[a, r + 1] - T[a, r - 1])
            stores.append((S, (a, r), v - drag * W[a, r] if a < 2 else v))
        return stores


    def stencil(src, r, sy, sz):
        p = src[r]
        lanes = lane_of(p.shape[0], nz)
        z = jnp.where(lanes >= nz - sz, p, roll(p, -sz, 1)) + jnp.where(lanes < sz, p, roll(p, sz, 1))
        s = src[r + 1] + src[r - 1] + roll(p, -sy, 0) + roll(p, sy, 0)
        return p, s + 4.0 * z

    def smooth(src, r, sy, sz):
        p, around = stencil(src, r, sy, sz)
        return KEEP * p + WEIGHT * around

    def smooth_all(src, dst, low, high, sy, sz, group=64):
        loop(low, high, lambda r: [(dst, r, smooth(src, r, sy, sz))], min(group, high - low))

    def sweep(src, dst, f, low, high, sy, sz, group=64):
        def body(r):
            p, around = stencil(src, r, sy, sz)
            return [(dst, r, KEEP * p + WEIGHT * (around - f[r]))]

        loop(low, high, body, min(group, high - low))

    def residual(src, f, r, sy, sz):
        p, around = stencil(src, r, sy, sz)
        return f[r] - (around - 12.0 * p)

    own = row_of(side, nz) < own_y

    def source_row(r):
        s1, s2 = S[1, r], S[2, r]
        flat = 0.5 * (S[0, r + 1] - S[0, r - 1] + roll(s1, -1, 0) - roll(s1, 1, 0))
        f = (flat + up0(s2) - down0(s2)) / STEP
        p, around = stencil(PA, r, 1, 1)
        left = jnp.where(own, f - (around - 12.0 * p), 0.0)
        return [(Z, r, left), (R0, (r + RIM - OFF, slice(0, own_y)), left[0:own_y])]

    def pair(v, stride, axis):
        at = lax.broadcasted_iota(jnp.int32, v.shape, axis)
        even = (at // stride) % 2 == 0
        return v + jnp.where(even, roll(v, -stride, axis), roll(v, stride, axis))

    def spread(v, stride, bit):
        at = (lane_of(v.shape[0], nz) // stride) % 2
        return jnp.where(at == bit, v, roll(v, stride if bit == 0 else -stride, 1))

    sub8 = row_of(y1, nz)

    def smooth_pair(src, r, sy, sz):
        a, b = src[r], src[r + 1]
        p = a + b
        lanes = lane_of(p.shape[0], nz)
        z = jnp.where(lanes >= nz - sz, p, roll(p, -sz, 1)) + jnp.where(lanes < sz, p, roll(p, sz, 1))
        around = p + src[r - 1] + src[r + 2] + roll(p, -sy, 0) + roll(p, sy, 0) + 4.0 * z
        return KEEP * p + WEIGHT * around

    def fine_residual(i):
        v = pair(smooth_pair(ZA, 2 * i + 1, 1, 1), 1, 1)
        rim = 0.5 * v[own_y : own_y + 8]
        rim = jnp.where(sub8 == 0, rim + roll(rim, -1, 0), jnp.where(sub8 == 7, rim + roll(rim, 1, 0), 0.0))
        return [(tmp, i, v[0:own_y]), (H1, (i + 3, slice(y1, 2 * y1)), rim)]


    def coarsen_row(i):
        return [(H1, (i + 3, slice(0, y1)), 0.5 * (tmp[i, pl.ds(0, y1, 2), :] + tmp[i, pl.ds(1, y1, 2), :]))]

    here = set()
    late = set(range(2, rows - 2))
    zero = {0, 1, 2, rows - 3, rows - 2, rows - 1}
    done = {name: set() for name in ("stress", "star", "source", "smooth", "pair", "coarsen")}

    def around_of(r):
        return {r - 1, r, r + 1}

    def run(name, rows_of, ready, body, size):
        fresh = [r for r in rows_of if r not in done[name] and ready(r)]
        for low in [r for r in fresh if r - 1 not in fresh]:
            high = low
            while high in fresh:
                high += 1
            loop(low, high, body, min(size, high - low))
        done[name] |= set(fresh)

    def advance(sides):
        run("stress", range(1, rows - 1), lambda r: around_of(r) <= here, stress_row, G_STRESS)
        if not sides:
            return
        run("star", range(2, rows - 2), lambda r: around_of(r) <= done["stress"], star_row, G_FINE)
        run("source", range(OFF, OFF + own_x), lambda r: around_of(r) <= done["star"], source_row, G_FINE)
        known = done["source"] | zero
        run("smooth", range(2, rows - 2), lambda r: around_of(r) <= known,
            lambda r: [(ZA, r, smooth(Z, r, 1, 1))], G_FINE)
        known1 = done["smooth"] | {0, 1, rows - 2, rows - 1}
        run("pair", range(half + 2), lambda i: set(range(2 * i, 2 * i + 4)) <= known1, fine_residual, 5)
        run("coarsen", range(half + 2), lambda i: i in done["pair"], coarsen_row, half + 2)

    def r0_faces(low, high):
        for dy in (1, -1):
            sy, ty = y_spans(dy, RIM)
            span = slice(low - OFF + RIM, high - OFF + RIM)
            remote(R0.at[span, sy], R0.at[span, ty], 0, dy, r_copies)

    def r0_side(dx):
        for dy in (1, -1):
            send(r_copies, R0, R0, RIM, RIM, 3, dx, dy)
        send(r_copies, R0, R0, RIM, RIM, RIM, dx, 0)

    r_copies = group()
    for at, (cut, copies) in enumerate(zip(cuts, slabs)):
        with jax.named_scope("SL%d" % at): finish(copies)
        here |= set(range(OFF + cut[0], OFF + cut[1]))
        with jax.named_scope("ST%d" % at): advance(at > 3)
        if at == 1:
            hear(1)
            tell(2)
        if at == 3:
            with jax.named_scope("WX"):
                finish(d_copies)
                finish(p_copies)
                finish(w_copies)
            here |= set(range(OFF)) | set(range(OFF + own_x, rows))
            with jax.named_scope("SX"): advance(True)
            split = OFF
            while split in done["source"]:
                split += 1
            r0_faces(OFF, split)
            r0_side(-1)
    r0_faces(split, OFF + own_x)
    r0_side(1)
    packs = half // 2
    lane1 = lane_of(2 * y1, nz)
    even1 = lane1 % 2 == 0
    even = lane_of(y1 + 2, nz) % 2 == 0
    def put(slot, v):
        G1[0, slot, 0:y1] = v[0:y1]
        G1[0, slot, y1 : y1 + 1] = v[y1 : y1 + 1]
        G1[0, slot, y1 + 1 : y1 + 2] = v[2 * y1 - 1 : 2 * y1]

    for i in range(packs):
        put(1 + i, jnp.where(even1, H1[4 + 2 * i], H1[5 + 2 * i]))
    rim = jnp.where(even1, H1[half + 4], H1[3])
    put(0, rim)
    put(packs + 1, rim)
    loop(2, half + 6, lambda r: [(H1A, r + 1, smooth(H1, r, 1, 2))], half + 4)
    lane8 = lane_of(y1, nz)
    for j in range(quarter + 4):
        tmp1[j] = pair(smooth_pair(H1A, 2 * j + 1, 1, 2), 2, 1)
    for which, order in enumerate(((2, 3, 4, 5), (6, 7, 0, 1))):
        gathered = None
        for at, j in enumerate(order):
            v = 0.5 * (tmp1[j, pl.ds(0, y1, 2), :] + tmp1[j, pl.ds(1, y1, 2), :])
            gathered = v if gathered is None else jnp.where(lane8 % 4 == at, v, gathered)
        G2[0, REACH, which] = gathered
    low2 = lane8 % 4 < 2
    near, beyond = G2[0, REACH, 0], G2[0, REACH, 1]
    GX[0] = jnp.where(low2, beyond, near)
    GX[1] = jnp.where(low2, near, beyond)
    h_copies = group()
    for distance in [3, 2, 4, 1, 0]:
        if distance == REACH:
            hear(2)
        for dx, dy in far:
            if abs(dx) == distance:
                slot = G2.at[(ny - dy) % ny, REACH - dx]
                if distance == REACH:
                    remote(GX.at[0 if dx > 0 else 1], slot.at[0], dx, dy, h_copies)
                else:
                    remote(G2.at[0, REACH], slot, dx, dy, h_copies)
    g_copies = group()
    kept = 3
    for dx in (1, -1, 0):
        for dy in range(ny):
            if dx == 0 and dy == 0:
                continue
            k = (ny - dy) % ny
            if dx == 0:
                src, dst = pl.ds(0, packs + 1), pl.ds(0, packs + 1)
            elif dx == 1:
                src, dst = pl.ds(packs + 1 - kept, kept + 1), pl.ds(packs + 2, kept + 1)
            else:
                src, dst = pl.ds(0, kept + 1), pl.ds(packs + 3 + kept, kept + 1)
            remote(G1.at[0, src], G1.at[k, dst], dx, dy, g_copies)
    finish(r_copies)
    wide = own_x + 2 * RIM
    smooth_all(R0, X1, 1, wide - 1, 1, 1, G_FINE)
    smooth_all(X1, X2, 2, wide - 2, 1, 1, G_FINE)

    def base_row(r):
        total = R0[r] + X1[r] + X2[r] + smooth(X2, r, 1, 1)
        return [(A, r - 3, PA[r - RIM + OFF] - WEIGHT * total)]

    loop(3, wide - 3, base_row, G_FINE)
    finish(h_copies)
    full2 = ny * y2
    blank8 = jnp.zeros((y1, nz), F32)
    ends = (0, 2 * REACH)

    def spill(k, s):
        return G2[k, s, 0 if s in ends else 1]

    def joined2(k, s):
        before = spill(k, s - 1) if s > 0 else blank8
        after = spill(k, s + 1) if s < 2 * REACH else blank8
        return G2[k, s, 0] + jnp.where(low2, before, after)

    for s in range(2 * REACH + 1):
        frames = [joined2(k, s) for k in range(ny)]
        turned = [roll(v, y2, 0) for v in frames]
        for m in range(ny // 2):
            k = 2 * m
            if ny == 2:
                v = frames[0] + turned[1]
            else:
                lower = frames[k] + jnp.where(sub8 < 2, turned[(k - 1) % ny], turned[(k + 1) % ny])
                upper = turned[k + 1] + jnp.where(sub8 < 6, frames[k], frames[(k + 2) % ny])
                v = jnp.where(sub8 < y2, lower, upper)
            for b0 in (0, 1):
                u = spread(v, 1, b0)
                for b1 in (0, 1):
                    f = spread(u, 2, b1)
                    F2[4 * s + 2 * b1 + b0, 8 * m : 8 * m + 8, :] = f
                    P2A[4 * s + 2 * b1 + b0, 8 * m : 8 * m + 8, :] = -WEIGHT * f
    rows2 = 4 * (2 * REACH + 1)
    sweep(P2A, P2B, F2, 1, rows2 - 1, 1, 4)

    def coarse_source(i):
        v = residual(P2B, F2, 2 * i, 1, 4) + residual(P2B, F2, 2 * i + 1, 1, 4)
        f = 0.5 * pair(pair(v, 4, 1), 1, 0)
        return [(F3, i, f), (P3A, i, -WEIGHT * f)]

    loop(1, rows2 // 2 - 1, coarse_source, rows2 // 2 - 2)
    sweep(P3A, P3B, F3, 2, 16, 2, 8)
    sweep(P3B, P3A, F3, 3, 15, 2, 8)
    sweep(P3A, P3B, F3, 4, 14, 2, 8)

    def line_row(r):
        mean = jnp.mean(residual(P3B, F3, r, 2, 8), axis=0, keepdims=True)
        v = P3B[r] - WEIGHT * mean
        return [(P2B, x, P2B[x] + v) for x in (2 * r, 2 * r + 1)]

    loop(6, 12, line_row, 6)
    finish(g_copies)
    full1 = ny * y1
    count1 = packs + 2 * kept

    def joined(k, q):
        if q < 0:
            v = G1[k, packs + 2 + q + kept]
            return v + jnp.where(even, 0.0, G1[k, 0]) if q == -1 else v
        if q >= packs:
            v = G1[k, packs + 4 + kept + q - packs]
            return v + jnp.where(even, G1[k, 0], 0.0) if q == packs else v
        v = G1[k, 1 + q]
        if q == 0:
            v = v + jnp.where(even, G1[k, packs + 2 + kept], 0.0)
        if q == packs - 1:
            v = v + jnp.where(even, 0.0, G1[k, packs + 3 + kept])
        return v

    for q in range(-kept, packs + kept):
        frames = [joined(k, q) for k in range(ny)]
        for k in range(ny):
            before, after = frames[(k - 1) % ny], frames[(k + 1) % ny]
            v = frames[k][0:y1] + jnp.where(sub8 == 0, before[y1 : y1 + 1], 0.0)
            v = v + jnp.where(sub8 == y1 - 1, after[y1 + 1 : y1 + 2], 0.0)
            for bit in (0, 1):
                f = spread(v, 1, bit)
                r = 2 * (q + kept) + bit
                F1[r, k * y1 : (k + 1) * y1, :] = f
                P1A[r, k * y1 : (k + 1) * y1, :] = -WEIGHT * f
    sweep(P1A, P1B, F1, 1, 2 * count1 - 1, 1, 2)
    sweep(P2B, P2A, F2, 13, 23, 1, 4)

    def second_row(m):
        p, around = stencil(P2A, m, 1, 4)
        v = KEEP * p + WEIGHT * (around - F2[m])
        E1[m - 14, pl.ds(0, full2, 2), :] = v
        E1[m - 14, pl.ds(1, full2, 2), :] = v
        e = E1[m - 14]
        r = 2 * (m - 13)
        P1B[r] = P1B[r] + e
        P1B[r + 1] = P1B[r + 1] + e

    for m in range(14, 22):
        second_row(m)
    sweep(P1B, P1A, F1, 3, 17, 1, 2)
    sweep(P1A, P1B, F1, 4, 16, 1, 2)
    for m in range(4, 16):
        e = m - 4
        for shift in (0, 1):
            E0[e, pl.ds(shift, y1, 2), :] = P1B[m, 0:y1, :]
            E0[e, pl.ds(own_y + shift, 2, 2), :] = P1B[m, y1 : y1 + 2, :]
            E0[e, pl.ds(own_y + 4 + shift, 2, 2), :] = P1B[m, full1 - 2 : full1, :]

    def first_pair(e):
        p = E0[e]
        z = jnp.where(last, p, roll(p, -1, 1)) + jnp.where(first, p, roll(p, 1, 1))
        base = (KEEP + WEIGHT) * p + WEIGHT * (roll(p, -1, 0) + roll(p, 1, 0) + 4.0 * z)
        return [
            (Y1, 2 * e - 2, base + WEIGHT * E0[e - 1]),
            (Y1, 2 * e - 1, base + WEIGHT * E0[e + 1]),
        ]

    loop(1, 11, first_pair, 5)
    loop(1, own_x + 3, lambda r: [(PN, r - 1, A[r - 1] + smooth(Y1, r, 1, 1))], 6)
    await_lines(send_sem.at[0], sum(sent))


def closing(S, PN, vel_out, pre_out, vel, pre, sem):
    _, own_x, own_y, nz = vel.shape
    lane = lane_of(PN.shape[1], nz)
    first, last = lane == 0, lane == nz - 1
    part = 4
    for low in range(0, own_x, part):
        for x in range(low, low + part):
            p = PN[x + 1]
            pre[x] = p[0:own_y]
            gx = (0.5 * STEP) * (PN[x + 2] - PN[x])
            gy = (0.5 * STEP) * (roll(p, -1, 0) - roll(p, 1, 0))
            gz = STEP * (jnp.where(last, p, roll(p, -1, 1)) - jnp.where(first, p, roll(p, 1, 1)))
            for a, g in enumerate((gx, gy, gz)):
                vel[a, x] = S[a, OFF + x, 0:own_y] - g[0:own_y]
        span = pl.ds(low, part)
        pltpu.make_async_copy(vel.at[:, span], vel_out.at[:, span], sem.at[0]).start()
        pltpu.make_async_copy(pre.at[span], pre_out.at[span], sem.at[1]).start()
    pltpu.make_async_copy(vel, vel_out, sem.at[0]).wait()
    pltpu.make_async_copy(pre, pre_out, sem.at[1]).wait()


def per_device(nx, ny, velocity, pressure, land_type, turbine_cells, surface_drag):
    _, own_x, own_y, nz = velocity.shape
    side = (own_y // 8 + 1) * 8
    rows = own_x + 2 * OFF
    wide = own_x + 2 * RIM
    half, quarter = own_x // 2, own_x // 4
    y1 = own_y // 2
    full1, full2 = ny * y1, ny * y1 // 2
    packs = half // 2
    rows2 = quarter * (2 * REACH + 1)

    def window(*shape):
        return pltpu.VMEM((*shape, nz), F32)

    level1 = window(2 * (packs + 6), full1)
    level2 = window(rows2, full2)
    level3 = window(rows2 // 2, full2)
    frame1 = window(half + 8, 2 * y1)
    corner, face = 4 * (3 * 2 * 2 + 3 * 3), 2 * (own_x + own_y)
    total = corner + face * (3 * 3 + 1 + 1 + RIM)
    total += 5 * (y1 + 2) * 3 * ny + (2 * REACH + 1) * ny * 2 * y1
    scratch = [
        window(3, rows, side), window(rows, side), window(rows, side), window(rows, side),
        window(3, rows, side), window(wide, side),
        window(rows, side), window(rows, side),
        window(wide, side), window(wide, side), window(own_x + 2, side), window(own_x + 4, side),
        window(half + 2, own_y), window(quarter + 4, 2 * y1),
        pltpu.VMEM((own_x, own_y, nz), jnp.int32),
        pltpu.VMEM(land_type.shape, jnp.int32),
        pltpu.SMEM(surface_drag.shape, F32),
        frame1, window(half + 10, 2 * y1), window(ny, packs + 10, y1 + 2),
        level1, level1, level1,
        window(ny, 2 * REACH + 1, 2, y1), window(2, y1),
        level2, level2, level2, level3, level3, level3,
        window(8, full1), window(12, side),
        window(total),
        pltpu.SemaphoreType.DMA((5,)),
        pltpu.SemaphoreType.DMA((1,)),
        pltpu.SemaphoreType.DMA((11,)),
        pltpu.SemaphoreType.REGULAR((3,)),
    ]
    inside = pl.BlockSpec(memory_space=pltpu.VMEM)
    outside = pl.BlockSpec(memory_space=pltpu.HBM)
    arguments = [
        pltpu.with_memory_space_constraint(a, pltpu.HBM)
        for a in (velocity, pressure, turbine_cells, land_type, surface_drag)
    ]
    star, middle = pl.pallas_call(
        functools.partial(kernel, nx, ny),
        out_shape=(
            jax.ShapeDtypeStruct((3, rows, side, nz), F32),
            jax.ShapeDtypeStruct((own_x + 2, side, nz), F32),
        ),
        in_specs=[outside] * 5,
        out_specs=(inside, inside),
        scratch_shapes=scratch,
        compiler_params=pltpu.CompilerParams(
            collective_id=0, has_side_effects=True, vmem_limit_bytes=VMEM_LIMIT
        ),
    )(*arguments)
    return pl.pallas_call(
        closing,
        out_shape=(
            jax.ShapeDtypeStruct(velocity.shape, F32),
            jax.ShapeDtypeStruct(pressure.shape, F32),
        ),
        in_specs=[inside, inside],
        out_specs=(outside, outside),
        scratch_shapes=[
            pltpu.VMEM(velocity.shape, F32),
            pltpu.VMEM(pressure.shape, F32),
            pltpu.SemaphoreType.DMA((2,)),
        ],
        compiler_params=pltpu.CompilerParams(vmem_limit_bytes=VMEM_LIMIT),
    )(star, middle)


def solution(mesh):
    in_specs = (
        P(None, "gx", "gy", None),
        P("gx", "gy", None),
        P("gx", "gy"),
        P("gx", "gy", None),
        P(),
    )
    out_specs = (P(None, "gx", "gy", None), P("gx", "gy", None))
    body = functools.partial(per_device, mesh.shape["gx"], mesh.shape["gy"])
    return jax.shard_map(
        body, mesh=mesh, in_specs=in_specs, out_specs=out_specs, check_vma=False
    )
```

```python
import functools
import math

import jax
import jax.numpy as jnp
from jax import lax
from jax.experimental import pallas as pl
from jax.experimental.pallas import tpu as pltpu
from jax.sharding import PartitionSpec as P

MESH = pl.DeviceIdType.MESH
F32 = jnp.float32
STEP = 0.1
WEIGHT = 0.8 / 12.0
KEEP = 0.2
OFF = 3
RIM = 4
G_STRESS = 4
G_FINE = 8
VMEM_LIMIT = 24000 * 1024
REACH = 4


def loop(low, high, body, group):
    def run(indices):
        found = [store for index in indices for store in body(index)]
        for ref, at, value in found:
            ref[at] = value

    whole = (high - low) // group
    if whole == 1:
        run(range(low, low + group))
    elif whole > 1:

        def step(index, carry):
            run([low + index * group + k for k in range(group)])
            return carry

        lax.fori_loop(0, whole, step, 0)
    if low + whole * group < high:
        run(range(low + whole * group, high))


def lane_of(count, nz):
    return lax.broadcasted_iota(jnp.int32, (count, nz), 1)


def row_of(count, nz):
    return lax.broadcasted_iota(jnp.int32, (count, nz), 0)


def roll(v, shift, axis):
    return pltpu.roll(v, shift % v.shape[axis], axis)


def kernel(
    nx, ny, vel_in, pre_in, turb_in, land_in, coeff_in, S, PN,
    W, D, PA, F, T, R0, Z, ZA, X1, X2, A, Y1, tmp, tmp1, turb, land, coeff,
    H1, H1A, G1, F1, P1A, P1B, G2, GX, F2, P2A, P2B, F3, P3A, P3B, E1, E0,
    spare, load_sem, send_sem, recv_sem, token,
):
    me_x, me_y = lax.axis_index("gx"), lax.axis_index("gy")
    _, own_x, own_y, nz = vel_in.shape
    side = W.shape[2]
    rows = own_x + 2 * OFF
    half, quarter = own_x // 2, own_x // 4
    y1, y2 = own_y // 2, own_y // 4

    loads = [
        pltpu.make_async_copy(turb_in, turb, load_sem.at[0]),
        pltpu.make_async_copy(land_in, land, load_sem.at[1]),
        pltpu.make_async_copy(coeff_in, coeff, load_sem.at[2]),
        pltpu.make_async_copy(vel_in, W.at[:, OFF : OFF + own_x, 0:own_y], load_sem.at[3]),
        pltpu.make_async_copy(pre_in, PA.at[OFF : OFF + own_x, 0:own_y], load_sem.at[4]),
    ]

    def device(dx, dy):
        return (lax.rem(me_x + dx + nx, nx), lax.rem(me_y + dy + ny, ny))

    far = [(dx, dy) for dx in range(-REACH, REACH + 1) for dy in range(ny) if dx or dy]
    close = [(dx, dy) for dx, dy in far if abs(dx) < 2]
    barrier = pltpu.get_barrier_semaphore()
    for dx, dy in close:
        pl.semaphore_signal(barrier, inc=1, device_id=device(dx, dy), device_id_type=MESH)
    for load in loads:
        load.start()

    groups, sent = [], []

    def group():
        groups.append(0)
        return len(groups) - 1

    def lines_of(ref):
        return math.prod(ref.shape) // nz

    def remote(src, dst, dx, dy, at):
        groups[at] += lines_of(dst)
        sent.append(lines_of(src))
        pltpu.make_async_remote_copy(
            src_ref=src, dst_ref=dst, send_sem=send_sem.at[0], recv_sem=recv_sem.at[at],
            device_id=device(dx, dy), device_id_type=MESH,
        ).start()

    def await_lines(sem, count):
        part = spare.at[pl.ds(0, count)]
        pltpu.make_async_copy(part, part, sem).wait()

    def finish(at):
        await_lines(recv_sem.at[at], groups[at])

    def x_spans(dx, width, src_base, dst_base):
        if dx == 0:
            return slice(src_base, src_base + own_x), slice(dst_base, dst_base + own_x)
        if dx == 1:
            high = src_base + own_x
            return slice(high - width, high), slice(dst_base - width, dst_base)
        return slice(src_base, src_base + width), slice(dst_base + own_x, dst_base + own_x + width)

    def y_spans(dy, width):
        if dy == 0:
            return slice(0, own_y), slice(0, own_y)
        if dy == 1:
            return slice(own_y - width, own_y), slice(side - width, side)
        return slice(0, width), slice(own_y, own_y + width)

    def send(at, src, dst, src_base, dst_base, width, dx, dy, lead=False):
        sx, tx = x_spans(dx, width, src_base, dst_base)
        sy, ty = y_spans(dy, width)
        if lead:
            remote(src.at[:, sx, sy], dst.at[:, tx, ty], dx, dy, at)
        else:
            remote(src.at[sx, sy], dst.at[tx, ty], dx, dy, at)

    corners = [(dx, dy) for dx in (1, -1) for dy in (1, -1)]
    faces = [(0, 1), (0, -1), (1, 0), (-1, 0)]

    def hear(turn, dx):
        at = turn + (0 if dx < 0 else 3)
        pl.semaphore_wait(token.at[at], 1)
        if turn < 2:
            tell(turn + 1, -dx)

    def tell(turn, dx):
        at = turn + (3 if dx < 0 else 0)
        pl.semaphore_signal(token.at[at], inc=1, device_id=device(dx, 0), device_id_type=MESH)

    def hear_right(turn, crosses):
        end = me_x >= nx - 1 - turn

        @pl.when(end if crosses else jnp.logical_not(end))
        def _():
            hear(turn, 1)

    pl.semaphore_wait(barrier, len(close))
    tell(0, 1)
    tell(0, -1)
    piece = own_x // 4
    low_end, high_end = 2 * piece, own_x - own_x // 8
    middle = (low_end + high_end) // 2
    cuts = [(0, piece), (piece, low_end), (low_end, middle), (middle, high_end), (high_end, own_x)]

    def slab(cut):
        low, high = cut
        at = group()
        for dy in (1, -1):
            sy, ty = y_spans(dy, 3)
            remote(vel_in.at[:, low:high, sy], W.at[:, OFF + low : OFF + high, ty], 0, dy, at)
        return at

    low_copies, high_copies = group(), group()
    for dx, at in ((-1, high_copies), (1, low_copies)):
        for dy in (1, -1):
            send(at, vel_in, W, 0, OFF, 2, dx, dy, True)
        send(at, vel_in, W, 0, OFF, 3, dx, 0, True)
    slabs = [slab(cut) for cut in cuts[:2]]
    shape = (own_y, own_y)
    diagonal = lax.broadcasted_iota(jnp.int32, shape, 0) == lax.broadcasted_iota(jnp.int32, shape, 1)
    lane16 = lane_of(own_y, nz)
    loads[1].wait()
    loads[2].wait()
    kinds = land[...]
    ground = jnp.zeros(kinds.shape, F32)
    for kind in range(coeff.shape[0]):
        ground = jnp.where(kinds == kind, coeff[kind], ground)
    loads[0].wait()
    for x in range(own_x):
        column = jnp.sum(jnp.where(diagonal, ground[x : x + 1, :], 0.0), axis=1, keepdims=True)
        low = jnp.where(lane16 == 0, column, 0.0)
        D[OFF + x, 0:own_y, :] = 2.0 * turb[x].astype(F32) + low
    d_copies = group()
    for dx, dy in faces:
        at = high_copies if dx == -1 else d_copies
        send(at, D, D, OFF, OFF, 1, dx, dy)
        send(at, pre_in, PA, 0, OFF, 1, dx, dy)
    slabs += [slab(cut) for cut in cuts[2:]]
    blank = jnp.zeros((side, nz), F32)
    for r in (1, 2, rows - 3, rows - 2):
        Z[r] = blank
    for r in (0, 1, rows - 2, rows - 1):
        ZA[r] = blank
    blank1 = jnp.zeros((2 * y1, nz), F32)
    for r in (1, 2, half + 5, half + 6):
        H1[r] = blank1
    for r in (0, 1, 2, half + 7, half + 8, half + 9):
        H1A[r] = blank1
    loads[3].wait()
    loads[4].wait()
    lane = lane_of(side, nz)
    first, last = lane == 0, lane == nz - 1

    def up0(v):
        return jnp.where(last, 0.0, roll(v, -1, 1))

    def down0(v):
        return jnp.where(first, 0.0, roll(v, 1, 1))

    def stress_row(r):
        v = [W[a, r] for a in range(3)]
        gx = [0.5 * (W[a, r + 1] - W[a, r - 1]) for a in range(3)]
        gy = [0.5 * (roll(v[a], -1, 0) - roll(v[a], 1, 0)) for a in range(3)]
        gz = [up0(v[a]) - down0(v[a]) for a in range(3)]
        e01, e02, e12 = gx[1] + gy[0], gx[2] + gz[0], gy[2] + gz[1]
        q = 2.0 * (gx[0] * gx[0] + gy[1] * gy[1] + gz[2] * gz[2]) + e01 * e01 + e02 * e02 + e12 * e12
        visc = 0.03 * jnp.sqrt(q)
        twice = visc + visc
        t00, t11, t22 = twice * gx[0], twice * gy[1], twice * gz[2]
        t01, t02, t12 = visc * e01, visc * e02, visc * e12
        flat = v[0] * v[0] + v[1] * v[1]
        ghost = 0.03 * jnp.sqrt(2.0 * v[2] * v[2] + flat)
        ghosts = [ghost * v[0], ghost * v[1], (ghost + ghost) * v[2]]
        out = [(T, (0, r), t00), (T, (1, r), t01), (T, (2, r), t02)]
        for a, (ty, tz) in enumerate(((t01, t02), (t11, t12), (t12, t22))):
            change = 0.5 * (roll(ty, -1, 0) - roll(ty, 1, 0))
            change += jnp.where(last, -ghosts[a], roll(tz, -1, 1)) - jnp.where(first, ghosts[a], roll(tz, 1, 1))
            change -= v[0] * gx[a] + v[1] * gy[a] + v[2] * gz[a]
            if a == 0:
                change += 1.0
            out.append((S, (a, r), v[a] + STEP * change))
        return out

    def star_row(r):
        drag = STEP * (D[r] * jnp.sqrt(W[0, r] * W[0, r] + W[1, r] * W[1, r]))
        stores = []
        for a in range(3):
            v = S[a, r] + (0.5 * STEP) * (T[a, r + 1] - T[a, r - 1])
            stores.append((S, (a, r), v - drag * W[a, r] if a < 2 else v))
        return stores


    def stencil(src, r, sy, sz):
        p = src[r]
        lanes = lane_of(p.shape[0], nz)
        z = jnp.where(lanes >= nz - sz, p, roll(p, -sz, 1)) + jnp.where(lanes < sz, p, roll(p, sz, 1))
        s = src[r + 1] + src[r - 1] + roll(p, -sy, 0) + roll(p, sy, 0)
        return p, s + 4.0 * z

    def smooth(src, r, sy, sz):
        p, around = stencil(src, r, sy, sz)
        return KEEP * p + WEIGHT * around

    def smooth_all(src, dst, low, high, sy, sz, group=64):
        loop(low, high, lambda r: [(dst, r, smooth(src, r, sy, sz))], min(group, high - low))

    def sweep(src, dst, f, low, high, sy, sz, group=64):
        def body(r):
            p, around = stencil(src, r, sy, sz)
            return [(dst, r, KEEP * p + WEIGHT * (around - f[r]))]

        loop(low, high, body, min(group, high - low))

    def residual(src, f, r, sy, sz):
        p, around = stencil(src, r, sy, sz)
        return f[r] - (around - 12.0 * p)

    own = row_of(side, nz) < own_y

    def source_row(r):
        s1, s2 = S[1, r], S[2, r]
        flat = 0.5 * (S[0, r + 1] - S[0, r - 1] + roll(s1, -1, 0) - roll(s1, 1, 0))
        f = (flat + up0(s2) - down0(s2)) / STEP
        p, around = stencil(PA, r, 1, 1)
        left = jnp.where(own, f - (around - 12.0 * p), 0.0)
        return [(Z, r, left), (R0, (r + RIM - OFF, slice(0, own_y)), left[0:own_y])]

    def pair(v, stride, axis):
        at = lax.broadcasted_iota(jnp.int32, v.shape, axis)
        even = (at // stride) % 2 == 0
        return v + jnp.where(even, roll(v, -stride, axis), roll(v, stride, axis))

    def spread(v, stride, bit):
        at = (lane_of(v.shape[0], nz) // stride) % 2
        return jnp.where(at == bit, v, roll(v, stride if bit == 0 else -stride, 1))

    sub8 = row_of(y1, nz)

    def smooth_pair(src, r, sy, sz):
        a, b = src[r], src[r + 1]
        p = a + b
        lanes = lane_of(p.shape[0], nz)
        z = jnp.where(lanes >= nz - sz, p, roll(p, -sz, 1)) + jnp.where(lanes < sz, p, roll(p, sz, 1))
        around = p + src[r - 1] + src[r + 2] + roll(p, -sy, 0) + roll(p, sy, 0) + 4.0 * z
        return KEEP * p + WEIGHT * around

    def fine_residual(i):
        v = pair(smooth_pair(ZA, 2 * i + 1, 1, 1), 1, 1)
        rim = 0.5 * v[own_y : own_y + 8]
        rim = jnp.where(sub8 == 0, rim + roll(rim, -1, 0), jnp.where(sub8 == 7, rim + roll(rim, 1, 0), 0.0))
        return [(tmp, i, v[0:own_y]), (H1, (i + 3, slice(y1, 2 * y1)), rim)]


    def coarsen_row(i):
        return [(H1, (i + 3, slice(0, y1)), 0.5 * (tmp[i, pl.ds(0, y1, 2), :] + tmp[i, pl.ds(1, y1, 2), :]))]

    here, behind = set(), set()
    zero = {0, 1, 2, rows - 3, rows - 2, rows - 1}
    done = {name: set() for name in ("stress", "star", "source", "smooth", "pair", "coarsen")}

    def around_of(r):
        return {r - 1, r, r + 1}

    def run(name, rows_of, ready, body, size):
        fresh = [r for r in rows_of if r not in done[name] and ready(r)]
        for low in [r for r in fresh if r - 1 not in fresh]:
            high = low
            while high in fresh:
                high += 1
            loop(low, high, body, min(size, high - low))
        done[name] |= set(fresh)

    def advance(full):
        run("stress", range(1, rows - 1), lambda r: around_of(r) <= here, stress_row, G_STRESS)
        if not full:
            return
        run("star", range(2, rows - 2), lambda r: around_of(r) <= done["stress"] and r in behind, star_row, G_FINE)
        run("source", range(OFF, OFF + own_x), lambda r: around_of(r) <= done["star"] & behind, source_row, G_FINE)
        known = done["source"] | zero
        run("smooth", range(2, rows - 2), lambda r: around_of(r) <= known,
            lambda r: [(ZA, r, smooth(Z, r, 1, 1))], G_FINE)
        known1 = done["smooth"] | {0, 1, rows - 2, rows - 1}
        run("pair", range(half + 2), lambda i: set(range(2 * i, 2 * i + 4)) <= known1, fine_residual, 5)
        run("coarsen", range(half + 2), lambda i: i in done["pair"], coarsen_row, half + 2)

    def r0_faces(low, high):
        for dy in (1, -1):
            sy, ty = y_spans(dy, RIM)
            span = slice(low - OFF + RIM, high - OFF + RIM)
            remote(R0.at[span, sy], R0.at[span, ty], 0, dy, r_copies)

    def r0_side(dx):
        for dy in (1, -1):
            send(r_copies, R0, R0, RIM, RIM, 3, dx, dy)
        send(r_copies, R0, R0, RIM, RIM, RIM, dx, 0)

    r_copies = group()
    split = OFF

    def arrive(copies, low, high, full):
        finish(copies)
        here.update(range(OFF + low, OFF + high))
        advance(full)

    for turn in range(3):
        hear_right(turn, False)
        hear(turn, -1)
    arrive(slabs[0], *cuts[0], False)
    arrive(low_copies, -OFF, 0, False)
    arrive(slabs[1], *cuts[1], False)
    finish(d_copies)
    high_rows = set(range(OFF + own_x, rows))
    behind.update(range(OFF + own_x))
    advance(True)
    arrive(slabs[2], *cuts[2], True)
    arrive(slabs[3], *cuts[3], True)
    while split in done["source"]:
        split += 1
    r0_faces(OFF, split)
    r0_side(-1)
    for turn in range(3):
        hear_right(turn, True)
    finish(high_copies)
    here.update(high_rows)
    behind.update(high_rows)
    arrive(slabs[4], *cuts[4], True)
    r0_faces(split, OFF + own_x)
    r0_side(1)
    packs = half // 2
    lane1 = lane_of(2 * y1, nz)
    even1 = lane1 % 2 == 0
    even = lane_of(y1 + 2, nz) % 2 == 0
    def put(slot, v):
        G1[0, slot, 0:y1] = v[0:y1]
        G1[0, slot, y1 : y1 + 1] = v[y1 : y1 + 1]
        G1[0, slot, y1 + 1 : y1 + 2] = v[2 * y1 - 1 : 2 * y1]

    for i in range(packs):
        put(1 + i, jnp.where(even1, H1[4 + 2 * i], H1[5 + 2 * i]))
    rim = jnp.where(even1, H1[half + 4], H1[3])
    put(0, rim)
    put(packs + 1, rim)
    loop(2, half + 6, lambda r: [(H1A, r + 1, smooth(H1, r, 1, 2))], half + 4)
    lane8 = lane_of(y1, nz)
    for j in range(quarter + 4):
        tmp1[j] = pair(smooth_pair(H1A, 2 * j + 1, 1, 2), 2, 1)
    for which, order in enumerate(((2, 3, 4, 5), (6, 7, 0, 1))):
        gathered = None
        for at, j in enumerate(order):
            v = 0.5 * (tmp1[j, pl.ds(0, y1, 2), :] + tmp1[j, pl.ds(1, y1, 2), :])
            gathered = v if gathered is None else jnp.where(lane8 % 4 == at, v, gathered)
        G2[0, REACH, which] = gathered
    low2 = lane8 % 4 < 2
    near, beyond = G2[0, REACH, 0], G2[0, REACH, 1]
    GX[0] = jnp.where(low2, beyond, near)
    GX[1] = jnp.where(low2, near, beyond)
    h_copies = group()
    order = sorted(far, key=lambda to: (to[0] == 0, abs(to[0]) == 1, -to[0], -to[1]))

    def spread_out(sign):
        for dx, dy in order:
            dx = sign * dx
            slot = G2.at[(ny - dy) % ny, REACH - dx]
            if abs(dx) == REACH:
                remote(GX.at[0 if dx > 0 else 1], slot.at[0], dx, dy, h_copies)
            else:
                remote(G2.at[0, REACH], slot, dx, dy, h_copies)

    second = me_x >= nx // 2
    size = groups[h_copies], len(sent)
    pl.when(second)(lambda: spread_out(1))
    groups[h_copies] = size[0]
    del sent[size[1]:]
    pl.when(jnp.logical_not(second))(lambda: spread_out(-1))
    g_copies = group()
    kept = 3
    for dx in (1, -1, 0):
        for dy in range(ny):
            if dx == 0 and dy == 0:
                continue
            k = (ny - dy) % ny
            if dx == 0:
                src, dst = pl.ds(0, packs + 1), pl.ds(0, packs + 1)
            elif dx == 1:
                src, dst = pl.ds(packs + 1 - kept, kept + 1), pl.ds(packs + 2, kept + 1)
            else:
                src, dst = pl.ds(0, kept + 1), pl.ds(packs + 3 + kept, kept + 1)
            remote(G1.at[0, src], G1.at[k, dst], dx, dy, g_copies)
    finish(r_copies)
    wide = own_x + 2 * RIM
    smooth_all(R0, X1, 1, wide - 1, 1, 1, G_FINE)
    smooth_all(X1, X2, 2, wide - 2, 1, 1, G_FINE)

    def base_row(r):
        total = R0[r] + X1[r] + X2[r] + smooth(X2, r, 1, 1)
        return [(A, r - 3, PA[r - RIM + OFF] - WEIGHT * total)]

    loop(3, wide - 3, base_row, G_FINE)
    finish(h_copies)
    full2 = ny * y2
    blank8 = jnp.zeros((y1, nz), F32)
    ends = (0, 2 * REACH)

    def spill(k, s):
        return G2[k, s, 0 if s in ends else 1]

    def joined2(k, s):
        before = spill(k, s - 1) if s > 0 else blank8
        after = spill(k, s + 1) if s < 2 * REACH else blank8
        return G2[k, s, 0] + jnp.where(low2, before, after)

    for s in range(2 * REACH + 1):
        frames = [joined2(k, s) for k in range(ny)]
        turned = [roll(v, y2, 0) for v in frames]
        for m in range(ny // 2):
            k = 2 * m
            if ny == 2:
                v = frames[0] + turned[1]
            else:
                lower = frames[k] + jnp.where(sub8 < 2, turned[(k - 1) % ny], turned[(k + 1) % ny])
                upper = turned[k + 1] + jnp.where(sub8 < 6, frames[k], frames[(k + 2) % ny])
                v = jnp.where(sub8 < y2, lower, upper)
            for b0 in (0, 1):
                u = spread(v, 1, b0)
                for b1 in (0, 1):
                    f = spread(u, 2, b1)
                    F2[4 * s + 2 * b1 + b0, 8 * m : 8 * m + 8, :] = f
                    P2A[4 * s + 2 * b1 + b0, 8 * m : 8 * m + 8, :] = -WEIGHT * f
    rows2 = 4 * (2 * REACH + 1)
    sweep(P2A, P2B, F2, 1, rows2 - 1, 1, 4)

    def coarse_source(i):
        v = residual(P2B, F2, 2 * i, 1, 4) + residual(P2B, F2, 2 * i + 1, 1, 4)
        f = 0.5 * pair(pair(v, 4, 1), 1, 0)
        return [(F3, i, f), (P3A, i, -WEIGHT * f)]

    loop(1, rows2 // 2 - 1, coarse_source, rows2 // 2 - 2)
    sweep(P3A, P3B, F3, 2, 16, 2, 8)
    sweep(P3B, P3A, F3, 3, 15, 2, 8)
    sweep(P3A, P3B, F3, 4, 14, 2, 8)

    def line_row(r):
        mean = jnp.mean(residual(P3B, F3, r, 2, 8), axis=0, keepdims=True)
        v = P3B[r] - WEIGHT * mean
        return [(P2B, x, P2B[x] + v) for x in (2 * r, 2 * r + 1)]

    loop(6, 12, line_row, 6)
    finish(g_copies)
    full1 = ny * y1
    count1 = packs + 2 * kept

    def joined(k, q):
        if q < 0:
            v = G1[k, packs + 2 + q + kept]
            return v + jnp.where(even, 0.0, G1[k, 0]) if q == -1 else v
        if q >= packs:
            v = G1[k, packs + 4 + kept + q - packs]
            return v + jnp.where(even, G1[k, 0], 0.0) if q == packs else v
        v = G1[k, 1 + q]
        if q == 0:
            v = v + jnp.where(even, G1[k, packs + 2 + kept], 0.0)
        if q == packs - 1:
            v = v + jnp.where(even, 0.0, G1[k, packs + 3 + kept])
        return v

    for q in range(-kept, packs + kept):
        frames = [joined(k, q) for k in range(ny)]
        for k in range(ny):
            before, after = frames[(k - 1) % ny], frames[(k + 1) % ny]
            v = frames[k][0:y1] + jnp.where(sub8 == 0, before[y1 : y1 + 1], 0.0)
            v = v + jnp.where(sub8 == y1 - 1, after[y1 + 1 : y1 + 2], 0.0)
            for bit in (0, 1):
                f = spread(v, 1, bit)
                r = 2 * (q + kept) + bit
                F1[r, k * y1 : (k + 1) * y1, :] = f
                P1A[r, k * y1 : (k + 1) * y1, :] = -WEIGHT * f
    sweep(P1A, P1B, F1, 1, 2 * count1 - 1, 1, 2)
    sweep(P2B, P2A, F2, 13, 23, 1, 4)

    def second_row(m):
        p, around = stencil(P2A, m, 1, 4)
        v = KEEP * p + WEIGHT * (around - F2[m])
        E1[m - 14, pl.ds(0, full2, 2), :] = v
        E1[m - 14, pl.ds(1, full2, 2), :] = v
        e = E1[m - 14]
        r = 2 * (m - 13)
        P1B[r] = P1B[r] + e
        P1B[r + 1] = P1B[r + 1] + e

    for m in range(14, 22):
        second_row(m)
    sweep(P1B, P1A, F1, 3, 17, 1, 2)
    sweep(P1A, P1B, F1, 4, 16, 1, 2)
    for m in range(4, 16):
        e = m - 4
        for shift in (0, 1):
            E0[e, pl.ds(shift, y1, 2), :] = P1B[m, 0:y1, :]
            E0[e, pl.ds(own_y + shift, 2, 2), :] = P1B[m, y1 : y1 + 2, :]
            E0[e, pl.ds(own_y + 4 + shift, 2, 2), :] = P1B[m, full1 - 2 : full1, :]

    def first_pair(e):
        p = E0[e]
        z = jnp.where(last, p, roll(p, -1, 1)) + jnp.where(first, p, roll(p, 1, 1))
        base = (KEEP + WEIGHT) * p + WEIGHT * (roll(p, -1, 0) + roll(p, 1, 0) + 4.0 * z)
        return [
            (Y1, 2 * e - 2, base + WEIGHT * E0[e - 1]),
            (Y1, 2 * e - 1, base + WEIGHT * E0[e + 1]),
        ]

    loop(1, 11, first_pair, 5)
    loop(1, own_x + 3, lambda r: [(PN, r - 1, A[r - 1] + smooth(Y1, r, 1, 1))], 6)
    await_lines(send_sem.at[0], sum(sent))


def closing(S, PN, vel_out, pre_out, vel, pre, sem):
    _, own_x, own_y, nz = vel.shape
    lane = lane_of(PN.shape[1], nz)
    first, last = lane == 0, lane == nz - 1
    part = 4
    for low in range(0, own_x, part):
        for x in range(low, low + part):
            p = PN[x + 1]
            pre[x] = p[0:own_y]
            gx = (0.5 * STEP) * (PN[x + 2] - PN[x])
            gy = (0.5 * STEP) * (roll(p, -1, 0) - roll(p, 1, 0))
            gz = STEP * (jnp.where(last, p, roll(p, -1, 1)) - jnp.where(first, p, roll(p, 1, 1)))
            for a, g in enumerate((gx, gy, gz)):
                vel[a, x] = S[a, OFF + x, 0:own_y] - g[0:own_y]
        span = pl.ds(low, part)
        pltpu.make_async_copy(vel.at[:, span], vel_out.at[:, span], sem.at[0]).start()
        pltpu.make_async_copy(pre.at[span], pre_out.at[span], sem.at[1]).start()
    pltpu.make_async_copy(vel, vel_out, sem.at[0]).wait()
    pltpu.make_async_copy(pre, pre_out, sem.at[1]).wait()


def per_device(nx, ny, velocity, pressure, land_type, turbine_cells, surface_drag):
    _, own_x, own_y, nz = velocity.shape
    side = (own_y // 8 + 1) * 8
    rows = own_x + 2 * OFF
    wide = own_x + 2 * RIM
    half, quarter = own_x // 2, own_x // 4
    y1 = own_y // 2
    full1, full2 = ny * y1, ny * y1 // 2
    packs = half // 2
    rows2 = quarter * (2 * REACH + 1)

    def window(*shape):
        return pltpu.VMEM((*shape, nz), F32)

    level1 = window(2 * (packs + 6), full1)
    level2 = window(rows2, full2)
    level3 = window(rows2 // 2, full2)
    frame1 = window(half + 8, 2 * y1)
    corner, face = 4 * (3 * 2 * 2 + 3 * 3), 2 * (own_x + own_y)
    total = corner + face * (3 * 3 + 1 + 1 + RIM)
    total += 5 * (y1 + 2) * 3 * ny + (2 * REACH + 1) * ny * 2 * y1
    scratch = [
        window(3, rows, side), window(rows, side), window(rows, side), window(rows, side),
        window(3, rows, side), window(wide, side),
        window(rows, side), window(rows, side),
        window(wide, side), window(wide, side), window(own_x + 2, side), window(own_x + 4, side),
        window(half + 2, own_y), window(quarter + 4, 2 * y1),
        pltpu.VMEM((own_x, own_y, nz), jnp.int32),
        pltpu.VMEM(land_type.shape, jnp.int32),
        pltpu.SMEM(surface_drag.shape, F32),
        frame1, window(half + 10, 2 * y1), window(ny, packs + 10, y1 + 2),
        level1, level1, level1,
        window(ny, 2 * REACH + 1, 2, y1), window(2, y1),
        level2, level2, level2, level3, level3, level3,
        window(8, full1), window(12, side),
        window(total),
        pltpu.SemaphoreType.DMA((5,)),
        pltpu.SemaphoreType.DMA((1,)),
        pltpu.SemaphoreType.DMA((11,)),
        pltpu.SemaphoreType.REGULAR((6,)),
    ]
    inside = pl.BlockSpec(memory_space=pltpu.VMEM)
    outside = pl.BlockSpec(memory_space=pltpu.HBM)
    arguments = [
        pltpu.with_memory_space_constraint(a, pltpu.HBM)
        for a in (velocity, pressure, turbine_cells, land_type, surface_drag)
    ]
    star, middle = pl.pallas_call(
        functools.partial(kernel, nx, ny),
        out_shape=(
            jax.ShapeDtypeStruct((3, rows, side, nz), F32),
            jax.ShapeDtypeStruct((own_x + 2, side, nz), F32),
        ),
        in_specs=[outside] * 5,
        out_specs=(inside, inside),
        scratch_shapes=scratch,
        compiler_params=pltpu.CompilerParams(
            collective_id=0, has_side_effects=True, vmem_limit_bytes=VMEM_LIMIT
        ),
    )(*arguments)
    return pl.pallas_call(
        closing,
        out_shape=(
            jax.ShapeDtypeStruct(velocity.shape, F32),
            jax.ShapeDtypeStruct(pressure.shape, F32),
        ),
        in_specs=[inside, inside],
        out_specs=(outside, outside),
        scratch_shapes=[
            pltpu.VMEM(velocity.shape, F32),
            pltpu.VMEM(pressure.shape, F32),
            pltpu.SemaphoreType.DMA((2,)),
        ],
        compiler_params=pltpu.CompilerParams(vmem_limit_bytes=VMEM_LIMIT),
    )(star, middle)


def solution(mesh):
    in_specs = (
        P(None, "gx", "gy", None),
        P("gx", "gy", None),
        P("gx", "gy"),
        P("gx", "gy", None),
        P(),
    )
    out_specs = (P(None, "gx", "gy", None), P("gx", "gy", None))
    body = functools.partial(per_device, mesh.shape["gx"], mesh.shape["gy"])
    return jax.shard_map(
        body, mesh=mesh, in_specs=in_specs, out_specs=out_specs, check_vma=False
    )
```

```python
import functools
import math

import jax
import jax.numpy as jnp
from jax import lax
from jax.experimental import pallas as pl
from jax.experimental.pallas import tpu as pltpu
from jax.sharding import PartitionSpec as P

MESH = pl.DeviceIdType.MESH
F32 = jnp.float32
STEP = 0.1
WEIGHT = 0.8 / 12.0
KEEP = 0.2
OFF = 3
RIM = 4
G_STRESS = 4
G_FINE = 8
VMEM_LIMIT = 24000 * 1024
REACH = 4


def loop(low, high, body, group):
    def run(indices):
        found = [store for index in indices for store in body(index)]
        for ref, at, value in found:
            ref[at] = value

    whole = (high - low) // group
    if whole == 1:
        run(range(low, low + group))
    elif whole > 1:

        def step(index, carry):
            run([low + index * group + k for k in range(group)])
            return carry

        lax.fori_loop(0, whole, step, 0)
    if low + whole * group < high:
        run(range(low + whole * group, high))


def lane_of(count, nz):
    return lax.broadcasted_iota(jnp.int32, (count, nz), 1)


def row_of(count, nz):
    return lax.broadcasted_iota(jnp.int32, (count, nz), 0)


def roll(v, shift, axis):
    return pltpu.roll(v, shift % v.shape[axis], axis)


def kernel(
    nx, ny, vel_in, pre_in, turb_in, land_in, coeff_in, S, PN,
    W, D, PA, F, T, R0, Z, ZA, X1, X2, A, Y1, tmp, tmp1, turb, land, coeff,
    H1, H1A, G1, F1, P1A, P1B, G2, GX, F2, P2A, P2B, F3, P3A, P3B, P3C, E1, E0,
    spare, load_sem, send_sem, recv_sem, token,
):
    me_x, me_y = lax.axis_index("gx"), lax.axis_index("gy")
    _, own_x, own_y, nz = vel_in.shape
    side = W.shape[2]
    rows = own_x + 2 * OFF
    half, quarter = own_x // 2, own_x // 4
    y1, y2 = own_y // 2, own_y // 4

    loads = [
        pltpu.make_async_copy(turb_in, turb, load_sem.at[0]),
        pltpu.make_async_copy(land_in, land, load_sem.at[1]),
        pltpu.make_async_copy(coeff_in, coeff, load_sem.at[2]),
        pltpu.make_async_copy(vel_in, W.at[:, OFF : OFF + own_x, 0:own_y], load_sem.at[3]),
        pltpu.make_async_copy(pre_in, PA.at[OFF : OFF + own_x, 0:own_y], load_sem.at[4]),
    ]

    def device(dx, dy):
        return (lax.rem(me_x + dx + nx, nx), lax.rem(me_y + dy + ny, ny))

    far = [(dx, dy) for dx in range(-REACH, REACH + 1) for dy in range(ny) if dx or dy]
    close = [(dx, dy) for dx, dy in far if abs(dx) < 2]
    barrier = pltpu.get_barrier_semaphore()
    for dx, dy in close:
        pl.semaphore_signal(barrier, inc=1, device_id=device(dx, dy), device_id_type=MESH)
    for load in loads:
        load.start()

    groups, sent = [], []

    def group():
        groups.append(0)
        return len(groups) - 1

    def lines_of(ref):
        return math.prod(ref.shape) // nz

    def remote(src, dst, dx, dy, at):
        groups[at] += lines_of(dst)
        sent.append(lines_of(src))
        pltpu.make_async_remote_copy(
            src_ref=src, dst_ref=dst, send_sem=send_sem.at[0], recv_sem=recv_sem.at[at],
            device_id=device(dx, dy), device_id_type=MESH,
        ).start()

    def await_lines(sem, count):
        part = spare.at[pl.ds(0, count)]
        pltpu.make_async_copy(part, part, sem).wait()

    def finish(at):
        await_lines(recv_sem.at[at], groups[at])

    def x_spans(dx, width, src_base, dst_base):
        if dx == 0:
            return slice(src_base, src_base + own_x), slice(dst_base, dst_base + own_x)
        if dx == 1:
            high = src_base + own_x
            return slice(high - width, high), slice(dst_base - width, dst_base)
        return slice(src_base, src_base + width), slice(dst_base + own_x, dst_base + own_x + width)

    def y_spans(dy, width):
        if dy == 0:
            return slice(0, own_y), slice(0, own_y)
        if dy == 1:
            return slice(own_y - width, own_y), slice(side - width, side)
        return slice(0, width), slice(own_y, own_y + width)

    def send(at, src, dst, src_base, dst_base, width, dx, dy, lead=False):
        sx, tx = x_spans(dx, width, src_base, dst_base)
        sy, ty = y_spans(dy, width)
        if lead:
            remote(src.at[:, sx, sy], dst.at[:, tx, ty], dx, dy, at)
        else:
            remote(src.at[sx, sy], dst.at[tx, ty], dx, dy, at)

    corners = [(dx, dy) for dx in (1, -1) for dy in (1, -1)]
    faces = [(0, 1), (0, -1), (1, 0), (-1, 0)]

    def hear(turn, dx):
        at = turn + (0 if dx < 0 else 3)
        pl.semaphore_wait(token.at[at], 1)
        if turn < 2:
            tell(turn + 1, -dx)

    def tell(turn, dx):
        at = turn + (3 if dx < 0 else 0)
        pl.semaphore_signal(token.at[at], inc=1, device_id=device(dx, 0), device_id_type=MESH)

    def hear_right(turn, crosses):
        end = me_x >= nx - 1 - turn

        @pl.when(end if crosses else jnp.logical_not(end))
        def _():
            hear(turn, 1)

    pl.semaphore_wait(barrier, len(close))
    tell(0, 1)
    tell(0, -1)
    piece = own_x // 4
    low_end, high_end = 2 * piece, own_x - own_x // 8
    middle = (low_end + high_end) // 2
    cuts = [(0, piece), (piece, low_end), (low_end, middle), (middle, high_end), (high_end, own_x)]

    def slab(cut):
        low, high = cut
        at = group()
        for dy in (1, -1):
            sy, ty = y_spans(dy, 3)
            remote(vel_in.at[:, low:high, sy], W.at[:, OFF + low : OFF + high, ty], 0, dy, at)
        return at

    low_copies, high_copies = group(), group()
    for dx, at in ((-1, high_copies), (1, low_copies)):
        for dy in (1, -1):
            send(at, vel_in, W, 0, OFF, 2, dx, dy, True)
        send(at, vel_in, W, 0, OFF, 3, dx, 0, True)
    slabs = [slab(cut) for cut in cuts[:2]]
    shape = (own_y, own_y)
    diagonal = lax.broadcasted_iota(jnp.int32, shape, 0) == lax.broadcasted_iota(jnp.int32, shape, 1)
    lane16 = lane_of(own_y, nz)
    loads[1].wait()
    loads[2].wait()
    kinds = land[...]
    ground = jnp.zeros(kinds.shape, F32)
    for kind in range(coeff.shape[0]):
        ground = jnp.where(kinds == kind, coeff[kind], ground)
    loads[0].wait()
    for x in range(own_x):
        column = jnp.sum(jnp.where(diagonal, ground[x : x + 1, :], 0.0), axis=1, keepdims=True)
        low = jnp.where(lane16 == 0, column, 0.0)
        D[OFF + x, 0:own_y, :] = 2.0 * turb[x].astype(F32) + low
    d_copies = group()
    for dx, dy in faces:
        at = high_copies if dx == -1 else d_copies
        send(at, D, D, OFF, OFF, 1, dx, dy)
        send(at, pre_in, PA, 0, OFF, 1, dx, dy)
    slabs += [slab(cut) for cut in cuts[2:]]
    blank = jnp.zeros((side, nz), F32)
    for r in (1, 2, rows - 3, rows - 2):
        Z[r] = blank
    for r in (0, 1, rows - 2, rows - 1):
        ZA[r] = blank
    blank1 = jnp.zeros((2 * y1, nz), F32)
    for r in (1, 2, half + 5, half + 6):
        H1[r] = blank1
    for r in (0, 1, 2, half + 7, half + 8, half + 9):
        H1A[r] = blank1
    loads[3].wait()
    loads[4].wait()
    lane = lane_of(side, nz)
    first, last = lane == 0, lane == nz - 1

    def up0(v):
        return jnp.where(last, 0.0, roll(v, -1, 1))

    def down0(v):
        return jnp.where(first, 0.0, roll(v, 1, 1))

    def stress_row(r):
        v = [W[a, r] for a in range(3)]
        gx = [0.5 * (W[a, r + 1] - W[a, r - 1]) for a in range(3)]
        gy = [0.5 * (roll(v[a], -1, 0) - roll(v[a], 1, 0)) for a in range(3)]
        gz = [up0(v[a]) - down0(v[a]) for a in range(3)]
        e01, e02, e12 = gx[1] + gy[0], gx[2] + gz[0], gy[2] + gz[1]
        q = 2.0 * (gx[0] * gx[0] + gy[1] * gy[1] + gz[2] * gz[2]) + e01 * e01 + e02 * e02 + e12 * e12
        visc = 0.03 * jnp.sqrt(q)
        twice = visc + visc
        t00, t11, t22 = twice * gx[0], twice * gy[1], twice * gz[2]
        t01, t02, t12 = visc * e01, visc * e02, visc * e12
        flat = v[0] * v[0] + v[1] * v[1]
        ghost = 0.03 * jnp.sqrt(2.0 * v[2] * v[2] + flat)
        ghosts = [ghost * v[0], ghost * v[1], (ghost + ghost) * v[2]]
        out = [(T, (0, r), t00), (T, (1, r), t01), (T, (2, r), t02)]
        for a, (ty, tz) in enumerate(((t01, t02), (t11, t12), (t12, t22))):
            change = 0.5 * (roll(ty, -1, 0) - roll(ty, 1, 0))
            change += jnp.where(last, -ghosts[a], roll(tz, -1, 1)) - jnp.where(first, ghosts[a], roll(tz, 1, 1))
            change -= v[0] * gx[a] + v[1] * gy[a] + v[2] * gz[a]
            if a == 0:
                change += 1.0
            out.append((S, (a, r), v[a] + STEP * change))
        return out

    def star_row(r):
        drag = STEP * (D[r] * jnp.sqrt(W[0, r] * W[0, r] + W[1, r] * W[1, r]))
        stores = []
        for a in range(3):
            v = S[a, r] + (0.5 * STEP) * (T[a, r + 1] - T[a, r - 1])
            stores.append((S, (a, r), v - drag * W[a, r] if a < 2 else v))
        return stores


    def stencil(src, r, sy, sz):
        p = src[r]
        lanes = lane_of(p.shape[0], nz)
        z = jnp.where(lanes >= nz - sz, p, roll(p, -sz, 1)) + jnp.where(lanes < sz, p, roll(p, sz, 1))
        s = src[r + 1] + src[r - 1] + roll(p, -sy, 0) + roll(p, sy, 0)
        return p, s + 4.0 * z

    def smooth(src, r, sy, sz):
        p, around = stencil(src, r, sy, sz)
        return KEEP * p + WEIGHT * around

    def smooth_all(src, dst, low, high, sy, sz, group=64):
        loop(low, high, lambda r: [(dst, r, smooth(src, r, sy, sz))], min(group, high - low))

    def sweep(src, dst, f, low, high, sy, sz, group=64):
        def body(r):
            p, around = stencil(src, r, sy, sz)
            return [(dst, r, KEEP * p + WEIGHT * (around - f[r]))]

        loop(low, high, body, min(group, high - low))

    def residual(src, f, r, sy, sz):
        p, around = stencil(src, r, sy, sz)
        return f[r] - (around - 12.0 * p)

    own = row_of(side, nz) < own_y

    def source_row(r):
        s1, s2 = S[1, r], S[2, r]
        flat = 0.5 * (S[0, r + 1] - S[0, r - 1] + roll(s1, -1, 0) - roll(s1, 1, 0))
        f = (flat + up0(s2) - down0(s2)) / STEP
        p, around = stencil(PA, r, 1, 1)
        left = jnp.where(own, f - (around - 12.0 * p), 0.0)
        return [(Z, r, left), (R0, (r + RIM - OFF, slice(0, own_y)), left[0:own_y])]

    def pair(v, stride, axis):
        at = lax.broadcasted_iota(jnp.int32, v.shape, axis)
        even = (at // stride) % 2 == 0
        return v + jnp.where(even, roll(v, -stride, axis), roll(v, stride, axis))

    def spread(v, stride, bit):
        at = (lane_of(v.shape[0], nz) // stride) % 2
        return jnp.where(at == bit, v, roll(v, stride if bit == 0 else -stride, 1))

    sub8 = row_of(y1, nz)

    def smooth_pair(src, r, sy, sz):
        a, b = src[r], src[r + 1]
        p = a + b
        lanes = lane_of(p.shape[0], nz)
        z = jnp.where(lanes >= nz - sz, p, roll(p, -sz, 1)) + jnp.where(lanes < sz, p, roll(p, sz, 1))
        around = p + src[r - 1] + src[r + 2] + roll(p, -sy, 0) + roll(p, sy, 0) + 4.0 * z
        return KEEP * p + WEIGHT * around

    def fine_residual(i):
        v = pair(smooth_pair(ZA, 2 * i + 1, 1, 1), 1, 1)
        rim = 0.5 * v[own_y : own_y + 8]
        rim = jnp.where(sub8 == 0, rim + roll(rim, -1, 0), jnp.where(sub8 == 7, rim + roll(rim, 1, 0), 0.0))
        return [(tmp, i, v[0:own_y]), (H1, (i + 3, slice(y1, 2 * y1)), rim)]


    def coarsen_row(i):
        return [(H1, (i + 3, slice(0, y1)), 0.5 * (tmp[i, pl.ds(0, y1, 2), :] + tmp[i, pl.ds(1, y1, 2), :]))]

    here, behind = set(), set()
    zero = {0, 1, 2, rows - 3, rows - 2, rows - 1}
    done = {name: set() for name in ("stress", "star", "source", "smooth", "pair", "coarsen")}

    def around_of(r):
        return {r - 1, r, r + 1}

    def run(name, rows_of, ready, body, size):
        fresh = [r for r in rows_of if r not in done[name] and ready(r)]
        for low in [r for r in fresh if r - 1 not in fresh]:
            high = low
            while high in fresh:
                high += 1
            loop(low, high, body, min(size, high - low))
        done[name] |= set(fresh)

    def advance(full):
        run("stress", range(1, rows - 1), lambda r: around_of(r) <= here, stress_row, G_STRESS)
        if not full:
            return
        run("star", range(2, rows - 2), lambda r: around_of(r) <= done["stress"] and r in behind, star_row, G_FINE)
        run("source", range(OFF, OFF + own_x), lambda r: around_of(r) <= done["star"] & behind, source_row, G_FINE)
        known = done["source"] | zero
        run("smooth", range(2, rows - 2), lambda r: around_of(r) <= known,
            lambda r: [(ZA, r, smooth(Z, r, 1, 1))], G_FINE)
        known1 = done["smooth"] | {0, 1, rows - 2, rows - 1}
        run("pair", range(half + 2), lambda i: set(range(2 * i, 2 * i + 4)) <= known1, fine_residual, 5)
        run("coarsen", range(half + 2), lambda i: i in done["pair"], coarsen_row, half + 2)

    def r0_faces(low, high):
        for dy in (1, -1):
            sy, ty = y_spans(dy, RIM)
            span = slice(low - OFF + RIM, high - OFF + RIM)
            remote(R0.at[span, sy], R0.at[span, ty], 0, dy, face_copies)

    def r0_side(dx):
        at = left_copies if dx == 1 else right_copies
        for dy in (1, -1):
            send(at, R0, R0, RIM, RIM, 3, dx, dy)
        send(at, R0, R0, RIM, RIM, RIM, dx, 0)

    face_copies, left_copies, right_copies = group(), group(), group()
    split = OFF

    def arrive(copies, low, high, full):
        finish(copies)
        here.update(range(OFF + low, OFF + high))
        advance(full)

    for turn in range(3):
        hear_right(turn, False)
        hear(turn, -1)
    arrive(slabs[0], *cuts[0], False)
    arrive(low_copies, -OFF, 0, False)
    arrive(slabs[1], *cuts[1], False)
    finish(d_copies)
    high_rows = set(range(OFF + own_x, rows))
    behind.update(range(OFF + own_x))
    advance(True)
    hear_right(0, True)
    arrive(slabs[2], *cuts[2], True)
    hear_right(1, True)
    arrive(slabs[3], *cuts[3], True)
    while split in done["source"]:
        split += 1
    r0_faces(OFF, split)
    r0_side(-1)
    hear_right(2, True)
    finish(high_copies)
    here.update(high_rows)
    behind.update(high_rows)
    arrive(slabs[4], *cuts[4], True)
    r0_faces(split, OFF + own_x)
    r0_side(1)
    packs = half // 2
    lane1 = lane_of(2 * y1, nz)
    even1 = lane1 % 2 == 0
    even = lane_of(y1 + 2, nz) % 2 == 0
    def put(slot, v):
        G1[0, slot, 0:y1] = v[0:y1]
        G1[0, slot, y1 : y1 + 1] = v[y1 : y1 + 1]
        G1[0, slot, y1 + 1 : y1 + 2] = v[2 * y1 - 1 : 2 * y1]

    for i in range(packs):
        put(1 + i, jnp.where(even1, H1[4 + 2 * i], H1[5 + 2 * i]))
    rim = jnp.where(even1, H1[half + 4], H1[3])
    put(0, rim)
    put(packs + 1, rim)
    g_copies = group()
    kept = 3
    for dx in (1, -1, 0):
        for dy in range(ny):
            if dx == 0 and dy == 0:
                continue
            k = (ny - dy) % ny
            if dx == 0:
                src, dst = pl.ds(0, packs + 1), pl.ds(0, packs + 1)
            elif dx == 1:
                src, dst = pl.ds(packs + 1 - kept, kept + 1), pl.ds(packs + 2, kept + 1)
            else:
                src, dst = pl.ds(0, kept + 1), pl.ds(packs + 3 + kept, kept + 1)
            remote(G1.at[0, src], G1.at[k, dst], dx, dy, g_copies)
    loop(2, half + 6, lambda r: [(H1A, r + 1, smooth(H1, r, 1, 2))], half + 4)
    lane8 = lane_of(y1, nz)
    for j in range(quarter + 4):
        tmp1[j] = pair(smooth_pair(H1A, 2 * j + 1, 1, 2), 2, 1)
    for which, order in enumerate(((2, 3, 4, 5), (6, 7, 0, 1))):
        gathered = None
        for at, j in enumerate(order):
            v = 0.5 * (tmp1[j, pl.ds(0, y1, 2), :] + tmp1[j, pl.ds(1, y1, 2), :])
            gathered = v if gathered is None else jnp.where(lane8 % 4 == at, v, gathered)
        G2[0, REACH, which] = gathered
    low2 = lane8 % 4 < 2
    near, beyond = G2[0, REACH, 0], G2[0, REACH, 1]
    GX[0] = jnp.where(low2, beyond, near)
    GX[1] = jnp.where(low2, near, beyond)
    h_copies = group()
    order = sorted(far, key=lambda to: (to[0] == 0, abs(to[0]) == 1, -to[0], -to[1]))

    def spread_out(sign):
        for dx, dy in order:
            dx = sign * dx
            slot = G2.at[(ny - dy) % ny, REACH - dx]
            if abs(dx) == REACH:
                remote(GX.at[0 if dx > 0 else 1], slot.at[0], dx, dy, h_copies)
            else:
                remote(G2.at[0, REACH], slot, dx, dy, h_copies)

    second = me_x >= nx // 2
    size = groups[h_copies], len(sent)
    pl.when(second)(lambda: spread_out(1))
    groups[h_copies] = size[0]
    del sent[size[1]:]
    pl.when(jnp.logical_not(second))(lambda: spread_out(-1))
    wide = own_x + 2 * RIM

    def base_row(r):
        total = R0[r] + X1[r] + X2[r] + smooth(X2, r, 1, 1)
        return [(A, r - 3, PA[r - RIM + OFF] - WEIGHT * total)]

    known = set()
    done.update({"first": set(), "second": set(), "base": set()})

    def refine(copies, low, high):
        finish(copies)
        known.update(range(low, high))
        run("first", range(1, wide - 1), lambda r: around_of(r) <= known,
            lambda r: [(X1, r, smooth(R0, r, 1, 1))], G_FINE)
        run("second", range(2, wide - 2), lambda r: around_of(r) <= done["first"],
            lambda r: [(X2, r, smooth(X1, r, 1, 1))], G_FINE)
        run("base", range(3, wide - 3), lambda r: around_of(r) <= done["second"], base_row, G_FINE)

    refine(face_copies, RIM, RIM + own_x)
    refine(left_copies, 0, RIM)
    refine(right_copies, RIM + own_x, wide)
    finish(g_copies)
    full1 = ny * y1
    count1 = packs + 2 * kept

    def joined(k, q):
        if q < 0:
            v = G1[k, packs + 2 + q + kept]
            return v + jnp.where(even, 0.0, G1[k, 0]) if q == -1 else v
        if q >= packs:
            v = G1[k, packs + 4 + kept + q - packs]
            return v + jnp.where(even, G1[k, 0], 0.0) if q == packs else v
        v = G1[k, 1 + q]
        if q == 0:
            v = v + jnp.where(even, G1[k, packs + 2 + kept], 0.0)
        if q == packs - 1:
            v = v + jnp.where(even, 0.0, G1[k, packs + 3 + kept])
        return v

    for q in range(-kept, packs + kept):
        frames = [joined(k, q) for k in range(ny)]
        for k in range(ny):
            before, after = frames[(k - 1) % ny], frames[(k + 1) % ny]
            v = frames[k][0:y1] + jnp.where(sub8 == 0, before[y1 : y1 + 1], 0.0)
            v = v + jnp.where(sub8 == y1 - 1, after[y1 + 1 : y1 + 2], 0.0)
            for bit in (0, 1):
                f = spread(v, 1, bit)
                r = 2 * (q + kept) + bit
                F1[r, k * y1 : (k + 1) * y1, :] = f
                P1A[r, k * y1 : (k + 1) * y1, :] = -WEIGHT * f
    sweep(P1A, P1B, F1, 1, 2 * count1 - 1, 1, 2)
    finish(h_copies)
    full2 = ny * y2
    blank8 = jnp.zeros((y1, nz), F32)
    ends = (0, 2 * REACH)

    def spill(k, s):
        return G2[k, s, 0 if s in ends else 1]

    def joined2(k, s):
        before = spill(k, s - 1) if s > 0 else blank8
        after = spill(k, s + 1) if s < 2 * REACH else blank8
        return G2[k, s, 0] + jnp.where(low2, before, after)

    for s in range(2 * REACH + 1):
        frames = [joined2(k, s) for k in range(ny)]
        turned = [roll(v, y2, 0) for v in frames]
        for m in range(ny // 2):
            k = 2 * m
            if ny == 2:
                v = frames[0] + turned[1]
            else:
                lower = frames[k] + jnp.where(sub8 < 2, turned[(k - 1) % ny], turned[(k + 1) % ny])
                upper = turned[k + 1] + jnp.where(sub8 < 6, frames[k], frames[(k + 2) % ny])
                v = jnp.where(sub8 < y2, lower, upper)
            moved = {by: roll(v, by, 1) if by else v for by in range(-3, 4)}
            for row in range(4):
                f = moved[-row]
                for at in range(1, 4):
                    f = jnp.where(lane8 % 4 == at, moved[at - row], f)
                F2[4 * s + row, 8 * m : 8 * m + 8, :] = f
    rows2 = 4 * (2 * REACH + 1)
    middle2 = range(12, rows2 - 12)

    def level2_row(r):
        v = smooth(F2, r, 1, 4)
        stores = [(P2A, r, v)]
        if r in middle2:
            stores.append((P2B, r, -WEIGHT * (F2[r] + v)))
        return stores

    loop(3, rows2 - 3, level2_row, rows2 - 6)
    rows3 = rows2 // 2

    def coarse_source(i):
        p = P2A[2 * i] + P2A[2 * i + 1]
        line = row_of(p.shape[0], nz) % 2 == 0
        up, down = roll(p, -1, 0), roll(p, 1, 0)
        pairs = p + jnp.where(line, up, down)
        beside = P2A[2 * i - 1] + P2A[2 * i + 2]
        sides = pairs + jnp.where(line, down + roll(p, -2, 0), up + roll(p, 2, 0))
        beside = beside + jnp.where(line, roll(beside, -1, 0), roll(beside, 1, 0))
        lanes = lane_of(p.shape[0], nz)
        inner = KEEP * pairs + WEIGHT * (pairs + beside + sides)
        low = (lanes // 4) % 2 == 0
        inner = inner + jnp.where(low, roll(inner, -4, 1), roll(inner, 4, 1))
        above = jnp.where(lanes >= nz - 4, pairs, roll(pairs, -4, 1))
        below = jnp.where(lanes < 4, pairs, roll(pairs, 4, 1))
        above2 = jnp.where(lanes >= nz - 8, above, roll(pairs, -8, 1))
        below2 = jnp.where(lanes < 8, below, roll(pairs, 8, 1))
        outer = pairs + above + below + jnp.where(low, above2, below2)
        return [(F3, i, 0.5 * (inner + 4.0 * WEIGHT * outer))]

    loop(2, rows3 - 2, coarse_source, rows3 - 4)
    smooth_all(F3, P3A, 3, rows3 - 3, 2, 8)
    smooth_all(P3A, P3B, 4, rows3 - 4, 2, 8)
    smooth_all(P3B, P3C, 5, rows3 - 5, 2, 8)

    def line_row(r):
        left = smooth(P3C, r, 2, 8)
        eight = sum(left[8 * m : 8 * m + 8] for m in range(full2 // 8))
        four = eight + roll(eight, 2, 0) + roll(eight, 4, 0) + roll(eight, 6, 0)
        mean = jnp.concatenate([(2.0 / full2) * four] * (full2 // 8), axis=0)
        v = -WEIGHT * (F3[r] + P3A[r] + P3B[r] + P3C[r] + mean)
        return [(P2B, x, P2B[x] + v) for x in (2 * r, 2 * r + 1)]

    loop(6, rows3 - 6, line_row, rows3 - 12)
    sweep(P2B, P2A, F2, 13, 23, 1, 4)

    def second_row(m):
        p, around = stencil(P2A, m, 1, 4)
        v = KEEP * p + WEIGHT * (around - F2[m])
        E1[m - 14, pl.ds(0, full2, 2), :] = v
        E1[m - 14, pl.ds(1, full2, 2), :] = v
        e = E1[m - 14]
        r = 2 * (m - 13)
        P1B[r] = P1B[r] + e
        P1B[r + 1] = P1B[r + 1] + e

    for m in range(14, 22):
        second_row(m)
    sweep(P1B, P1A, F1, 3, 17, 1, 2)
    sweep(P1A, P1B, F1, 4, 16, 1, 2)
    for m in range(4, 16):
        e = m - 4
        for shift in (0, 1):
            E0[e, pl.ds(shift, y1, 2), :] = P1B[m, 0:y1, :]
            E0[e, pl.ds(own_y + shift, 2, 2), :] = P1B[m, y1 : y1 + 2, :]
            E0[e, pl.ds(own_y + 4 + shift, 2, 2), :] = P1B[m, full1 - 2 : full1, :]

    def first_pair(e):
        p = E0[e]
        z = jnp.where(last, p, roll(p, -1, 1)) + jnp.where(first, p, roll(p, 1, 1))
        base = (KEEP + WEIGHT) * p + WEIGHT * (roll(p, -1, 0) + roll(p, 1, 0) + 4.0 * z)
        return [
            (Y1, 2 * e - 2, base + WEIGHT * E0[e - 1]),
            (Y1, 2 * e - 1, base + WEIGHT * E0[e + 1]),
        ]

    loop(1, 11, first_pair, 10)
    loop(1, own_x + 3, lambda r: [(PN, r - 1, A[r - 1] + smooth(Y1, r, 1, 1))], own_x + 2)
    await_lines(send_sem.at[0], sum(sent))


def closing(S, PN, vel_out, pre_out, vel, pre, sem):
    _, own_x, own_y, nz = vel.shape
    lane = lane_of(PN.shape[1], nz)
    first, last = lane == 0, lane == nz - 1
    part = 4
    for low in range(0, own_x, part):
        for x in range(low, low + part):
            p = PN[x + 1]
            pre[x] = p[0:own_y]
            gx = (0.5 * STEP) * (PN[x + 2] - PN[x])
            gy = (0.5 * STEP) * (roll(p, -1, 0) - roll(p, 1, 0))
            gz = STEP * (jnp.where(last, p, roll(p, -1, 1)) - jnp.where(first, p, roll(p, 1, 1)))
            for a, g in enumerate((gx, gy, gz)):
                vel[a, x] = S[a, OFF + x, 0:own_y] - g[0:own_y]
        span = pl.ds(low, part)
        pltpu.make_async_copy(vel.at[:, span], vel_out.at[:, span], sem.at[0]).start()
        pltpu.make_async_copy(pre.at[span], pre_out.at[span], sem.at[1]).start()
    pltpu.make_async_copy(vel, vel_out, sem.at[0]).wait()
    pltpu.make_async_copy(pre, pre_out, sem.at[1]).wait()


def per_device(nx, ny, velocity, pressure, land_type, turbine_cells, surface_drag):
    _, own_x, own_y, nz = velocity.shape
    side = (own_y // 8 + 1) * 8
    rows = own_x + 2 * OFF
    wide = own_x + 2 * RIM
    half, quarter = own_x // 2, own_x // 4
    y1 = own_y // 2
    full1, full2 = ny * y1, ny * y1 // 2
    packs = half // 2
    rows2 = quarter * (2 * REACH + 1)

    def window(*shape):
        return pltpu.VMEM((*shape, nz), F32)

    level1 = window(2 * (packs + 6), full1)
    level2 = window(rows2, full2)
    level3 = window(rows2 // 2, full2)
    frame1 = window(half + 8, 2 * y1)
    corner, face = 4 * (3 * 2 * 2 + 3 * 3), 2 * (own_x + own_y)
    total = corner + face * (3 * 3 + 1 + 1 + RIM)
    total += 5 * (y1 + 2) * 3 * ny + (2 * REACH + 1) * ny * 2 * y1
    scratch = [
        window(3, rows, side), window(rows, side), window(rows, side), window(rows, side),
        window(3, rows, side), window(wide, side),
        window(rows, side), window(rows, side),
        window(wide, side), window(wide, side), window(own_x + 2, side), window(own_x + 4, side),
        window(half + 2, own_y), window(quarter + 4, 2 * y1),
        pltpu.VMEM((own_x, own_y, nz), jnp.int32),
        pltpu.VMEM(land_type.shape, jnp.int32),
        pltpu.SMEM(surface_drag.shape, F32),
        frame1, window(half + 10, 2 * y1), window(ny, packs + 10, y1 + 2),
        level1, level1, level1,
        window(ny, 2 * REACH + 1, 2, y1), window(2, y1),
        level2, level2, level2, level3, level3, level3, level3,
        window(8, full1), window(12, side),
        window(total),
        pltpu.SemaphoreType.DMA((5,)),
        pltpu.SemaphoreType.DMA((1,)),
        pltpu.SemaphoreType.DMA((13,)),
        pltpu.SemaphoreType.REGULAR((6,)),
    ]
    inside = pl.BlockSpec(memory_space=pltpu.VMEM)
    outside = pl.BlockSpec(memory_space=pltpu.HBM)
    arguments = [
        pltpu.with_memory_space_constraint(a, pltpu.HBM)
        for a in (velocity, pressure, turbine_cells, land_type, surface_drag)
    ]
    star, middle = pl.pallas_call(
        functools.partial(kernel, nx, ny),
        out_shape=(
            jax.ShapeDtypeStruct((3, rows, side, nz), F32),
            jax.ShapeDtypeStruct((own_x + 2, side, nz), F32),
        ),
        in_specs=[outside] * 5,
        out_specs=(inside, inside),
        scratch_shapes=scratch,
        compiler_params=pltpu.CompilerParams(
            collective_id=0, has_side_effects=True, vmem_limit_bytes=VMEM_LIMIT
        ),
    )(*arguments)
    return pl.pallas_call(
        closing,
        out_shape=(
            jax.ShapeDtypeStruct(velocity.shape, F32),
            jax.ShapeDtypeStruct(pressure.shape, F32),
        ),
        in_specs=[inside, inside],
        out_specs=(outside, outside),
        scratch_shapes=[
            pltpu.VMEM(velocity.shape, F32),
            pltpu.VMEM(pressure.shape, F32),
            pltpu.SemaphoreType.DMA((2,)),
        ],
        compiler_params=pltpu.CompilerParams(vmem_limit_bytes=VMEM_LIMIT),
    )(star, middle)


def solution(mesh):
    in_specs = (
        P(None, "gx", "gy", None),
        P("gx", "gy", None),
        P("gx", "gy"),
        P("gx", "gy", None),
        P(),
    )
    out_specs = (P(None, "gx", "gy", None), P("gx", "gy", None))
    body = functools.partial(per_device, mesh.shape["gx"], mesh.shape["gy"])
    return jax.shard_map(
        body, mesh=mesh, in_specs=in_specs, out_specs=out_specs, check_vma=False
    )
```

```python
import functools
import math

import jax
import jax.numpy as jnp
from jax import lax
from jax.experimental import pallas as pl
from jax.experimental.pallas import tpu as pltpu
from jax.sharding import PartitionSpec as P

MESH = pl.DeviceIdType.MESH
F32 = jnp.float32
STEP = 0.1
WEIGHT = 0.8 / 12.0
KEEP = 0.2
OFF = 3
RIM = 4
G_STRESS = 4
G_FINE = 8
VMEM_LIMIT = 24000 * 1024
REACH = 4


def loop(low, high, body, group):
    def run(indices):
        found = [store for index in indices for store in body(index)]
        for ref, at, value in found:
            ref[at] = value

    whole = (high - low) // group
    if whole == 1:
        run(range(low, low + group))
    elif whole > 1:

        def step(index, carry):
            run([low + index * group + k for k in range(group)])
            return carry

        lax.fori_loop(0, whole, step, 0)
    if low + whole * group < high:
        run(range(low + whole * group, high))


def lane_of(count, nz):
    return lax.broadcasted_iota(jnp.int32, (count, nz), 1)


def row_of(count, nz):
    return lax.broadcasted_iota(jnp.int32, (count, nz), 0)


def roll(v, shift, axis):
    return pltpu.roll(v, shift % v.shape[axis], axis)


def kernel(
    nx, ny, vel_in, pre_in, turb_in, land_in, coeff_in, S, PN,
    W, D, PA, F, T, R0, Z, ZA, X1, X2, A, Y1, tmp, tmp1, turb, land, coeff,
    H1, H1A, G1, F1, P1A, P1B, G2, GX, F2, P2A, P2B, F3, P3A, P3B, P3C, E1, E0,
    spare, load_sem, send_sem, recv_sem, token,
):
    me_x, me_y = lax.axis_index("gx"), lax.axis_index("gy")
    _, own_x, own_y, nz = vel_in.shape
    side = W.shape[2]
    rows = own_x + 2 * OFF
    half, quarter = own_x // 2, own_x // 4
    y1, y2 = own_y // 2, own_y // 4

    loads = [
        pltpu.make_async_copy(turb_in, turb, load_sem.at[0]),
        pltpu.make_async_copy(land_in, land, load_sem.at[1]),
        pltpu.make_async_copy(coeff_in, coeff, load_sem.at[2]),
        pltpu.make_async_copy(vel_in, W.at[:, OFF : OFF + own_x, 0:own_y], load_sem.at[3]),
        pltpu.make_async_copy(pre_in, PA.at[OFF : OFF + own_x, 0:own_y], load_sem.at[4]),
    ]

    def device(dx, dy):
        return (lax.rem(me_x + dx + nx, nx), lax.rem(me_y + dy + ny, ny))

    far = [(dx, dy) for dx in range(-REACH, REACH + 1) for dy in range(ny) if dx or dy]
    close = [(dx, dy) for dx, dy in far if dx == 0 or (dy == 0 and abs(dx) < 2)]
    barrier = pltpu.get_barrier_semaphore()
    for dx, dy in close:
        pl.semaphore_signal(barrier, inc=1, device_id=device(dx, dy), device_id_type=MESH)
    for load in loads:
        load.start()

    groups, sent = [], []

    def group():
        groups.append(0)
        return len(groups) - 1

    def lines_of(ref):
        return math.prod(ref.shape) // nz

    def remote(src, dst, dx, dy, at):
        groups[at] += lines_of(dst)
        sent.append(lines_of(src))
        pltpu.make_async_remote_copy(
            src_ref=src, dst_ref=dst, send_sem=send_sem.at[0], recv_sem=recv_sem.at[at],
            device_id=device(dx, dy), device_id_type=MESH,
        ).start()

    def await_lines(sem, count):
        part = spare.at[pl.ds(0, count)]
        pltpu.make_async_copy(part, part, sem).wait()

    def finish(at):
        await_lines(recv_sem.at[at], groups[at])

    def x_spans(dx, width, src_base, dst_base):
        if dx == 0:
            return slice(src_base, src_base + own_x), slice(dst_base, dst_base + own_x)
        if dx == 1:
            high = src_base + own_x
            return slice(high - width, high), slice(dst_base - width, dst_base)
        return slice(src_base, src_base + width), slice(dst_base + own_x, dst_base + own_x + width)

    def y_spans(dy, width):
        if dy == 0:
            return slice(0, own_y), slice(0, own_y)
        if dy == 1:
            return slice(own_y - width, own_y), slice(side - width, side)
        return slice(0, width), slice(own_y, own_y + width)

    def send(at, src, dst, src_base, dst_base, width, dx, dy, lead=False):
        sx, tx = x_spans(dx, width, src_base, dst_base)
        sy, ty = y_spans(dy, width)
        if lead:
            remote(src.at[:, sx, sy], dst.at[:, tx, ty], dx, dy, at)
        else:
            remote(src.at[sx, sy], dst.at[tx, ty], dx, dy, at)

    corners = [(dx, dy) for dx in (1, -1) for dy in (1, -1)]
    faces = [(0, 1), (0, -1), (1, 0), (-1, 0)]

    def hear(turn, dx):
        at = turn + (0 if dx < 0 else 3)
        pl.semaphore_wait(token.at[at], 1)
        if turn < 2:
            tell(turn + 1, -dx)

    def tell(turn, dx):
        at = turn + (3 if dx < 0 else 0)
        pl.semaphore_signal(token.at[at], inc=1, device_id=device(dx, 0), device_id_type=MESH)

    def listen(turn, crosses):
        for dx, end in ((1, me_x >= nx - 1 - turn), (-1, me_x <= turn + 1)):
            pl.when(end if crosses else jnp.logical_not(end))(functools.partial(hear, turn, dx))

    pl.semaphore_wait(barrier, len(close))
    for dy in range(1, ny):
        pl.semaphore_signal(token.at[6], inc=1, device_id=device(0, dy), device_id_type=MESH)
    piece = own_x // 4
    low_end, high_end = 2 * piece, own_x - own_x // 8
    middle = (low_end + high_end) // 2
    cuts = [(0, piece), (piece, low_end), (low_end, middle), (middle, high_end), (high_end, own_x)]

    def slab(cut):
        low, high = cut
        at = group()
        for dy in (1, -1):
            sy, ty = y_spans(dy, 3)
            remote(vel_in.at[:, low:high, sy], W.at[:, OFF + low : OFF + high, ty], 0, dy, at)
        return at

    low_copies, high_copies = group(), group()
    for dx, at in ((-1, high_copies), (1, low_copies)):
        send(at, vel_in, W, 0, OFF, 3, dx, 0, True)
    slabs = [slab(cut) for cut in cuts[:2]]
    shape = (own_y, own_y)
    diagonal = lax.broadcasted_iota(jnp.int32, shape, 0) == lax.broadcasted_iota(jnp.int32, shape, 1)
    lane16 = lane_of(own_y, nz)
    loads[1].wait()
    loads[2].wait()
    kinds = land[...]
    ground = jnp.zeros(kinds.shape, F32)
    for kind in range(coeff.shape[0]):
        ground = jnp.where(kinds == kind, coeff[kind], ground)
    loads[0].wait()
    for x in range(own_x):
        column = jnp.sum(jnp.where(diagonal, ground[x : x + 1, :], 0.0), axis=1, keepdims=True)
        low = jnp.where(lane16 == 0, column, 0.0)
        D[OFF + x, 0:own_y, :] = 2.0 * turb[x].astype(F32) + low
    d_copies = group()
    for dx, dy in faces:
        at = high_copies if dx == -1 else d_copies
        send(at, D, D, OFF, OFF, 1, dx, dy)
        send(at, pre_in, PA, 0, OFF, 1, dx, dy)
    slabs += [slab(cut) for cut in cuts[2:3]]
    pl.semaphore_wait(token.at[6], ny - 1)
    tell(0, 1)
    tell(0, -1)
    for dx, at in ((-1, high_copies), (1, low_copies)):
        for dy in (1, -1):
            send(at, vel_in, W, 0, OFF, 2, dx, dy, True)
    slabs += [slab(cut) for cut in cuts[3:]]
    blank = jnp.zeros((side, nz), F32)
    for r in (1, 2, rows - 3, rows - 2):
        Z[r] = blank
    for r in (0, 1, rows - 2, rows - 1):
        ZA[r] = blank
    blank1 = jnp.zeros((2 * y1, nz), F32)
    for r in (1, 2, half + 5, half + 6):
        H1[r] = blank1
    for r in (0, 1, 2, half + 7, half + 8, half + 9):
        H1A[r] = blank1
    loads[3].wait()
    loads[4].wait()
    lane = lane_of(side, nz)
    first, last = lane == 0, lane == nz - 1

    def up0(v):
        return jnp.where(last, 0.0, roll(v, -1, 1))

    def down0(v):
        return jnp.where(first, 0.0, roll(v, 1, 1))

    def stress_row(r):
        v = [W[a, r] for a in range(3)]
        gx = [0.5 * (W[a, r + 1] - W[a, r - 1]) for a in range(3)]
        gy = [0.5 * (roll(v[a], -1, 0) - roll(v[a], 1, 0)) for a in range(3)]
        gz = [up0(v[a]) - down0(v[a]) for a in range(3)]
        e01, e02, e12 = gx[1] + gy[0], gx[2] + gz[0], gy[2] + gz[1]
        q = 2.0 * (gx[0] * gx[0] + gy[1] * gy[1] + gz[2] * gz[2]) + e01 * e01 + e02 * e02 + e12 * e12
        visc = 0.03 * jnp.sqrt(q)
        twice = visc + visc
        t00, t11, t22 = twice * gx[0], twice * gy[1], twice * gz[2]
        t01, t02, t12 = visc * e01, visc * e02, visc * e12
        flat = v[0] * v[0] + v[1] * v[1]
        ghost = 0.03 * jnp.sqrt(2.0 * v[2] * v[2] + flat)
        ghosts = [ghost * v[0], ghost * v[1], (ghost + ghost) * v[2]]
        out = [(T, (0, r), t00), (T, (1, r), t01), (T, (2, r), t02)]
        for a, (ty, tz) in enumerate(((t01, t02), (t11, t12), (t12, t22))):
            change = 0.5 * (roll(ty, -1, 0) - roll(ty, 1, 0))
            change += jnp.where(last, -ghosts[a], roll(tz, -1, 1)) - jnp.where(first, ghosts[a], roll(tz, 1, 1))
            change -= v[0] * gx[a] + v[1] * gy[a] + v[2] * gz[a]
            if a == 0:
                change += 1.0
            out.append((S, (a, r), v[a] + STEP * change))
        return out

    def star_row(r):
        drag = STEP * (D[r] * jnp.sqrt(W[0, r] * W[0, r] + W[1, r] * W[1, r]))
        stores = []
        for a in range(3):
            v = S[a, r] + (0.5 * STEP) * (T[a, r + 1] - T[a, r - 1])
            stores.append((S, (a, r), v - drag * W[a, r] if a < 2 else v))
        return stores


    def stencil(src, r, sy, sz):
        p = src[r]
        lanes = lane_of(p.shape[0], nz)
        z = jnp.where(lanes >= nz - sz, p, roll(p, -sz, 1)) + jnp.where(lanes < sz, p, roll(p, sz, 1))
        s = src[r + 1] + src[r - 1] + roll(p, -sy, 0) + roll(p, sy, 0)
        return p, s + 4.0 * z

    def smooth(src, r, sy, sz):
        p, around = stencil(src, r, sy, sz)
        return KEEP * p + WEIGHT * around

    def smooth_all(src, dst, low, high, sy, sz, group=64):
        loop(low, high, lambda r: [(dst, r, smooth(src, r, sy, sz))], min(group, high - low))

    def sweep(src, dst, f, low, high, sy, sz, group=64):
        def body(r):
            p, around = stencil(src, r, sy, sz)
            return [(dst, r, KEEP * p + WEIGHT * (around - f[r]))]

        loop(low, high, body, min(group, high - low))

    def residual(src, f, r, sy, sz):
        p, around = stencil(src, r, sy, sz)
        return f[r] - (around - 12.0 * p)

    own = row_of(side, nz) < own_y

    def source_row(r):
        s1, s2 = S[1, r], S[2, r]
        flat = 0.5 * (S[0, r + 1] - S[0, r - 1] + roll(s1, -1, 0) - roll(s1, 1, 0))
        f = (flat + up0(s2) - down0(s2)) / STEP
        p, around = stencil(PA, r, 1, 1)
        left = jnp.where(own, f - (around - 12.0 * p), 0.0)
        return [(Z, r, left), (R0, (r + RIM - OFF, slice(0, own_y)), left[0:own_y])]

    def pair(v, stride, axis):
        at = lax.broadcasted_iota(jnp.int32, v.shape, axis)
        even = (at // stride) % 2 == 0
        return v + jnp.where(even, roll(v, -stride, axis), roll(v, stride, axis))

    def spread(v, stride, bit):
        at = (lane_of(v.shape[0], nz) // stride) % 2
        return jnp.where(at == bit, v, roll(v, stride if bit == 0 else -stride, 1))

    sub8 = row_of(y1, nz)

    def smooth_pair(src, r, sy, sz):
        a, b = src[r], src[r + 1]
        p = a + b
        lanes = lane_of(p.shape[0], nz)
        z = jnp.where(lanes >= nz - sz, p, roll(p, -sz, 1)) + jnp.where(lanes < sz, p, roll(p, sz, 1))
        around = p + src[r - 1] + src[r + 2] + roll(p, -sy, 0) + roll(p, sy, 0) + 4.0 * z
        return KEEP * p + WEIGHT * around

    def fine_residual(i):
        v = pair(smooth_pair(ZA, 2 * i + 1, 1, 1), 1, 1)
        rim = 0.5 * v[own_y : own_y + 8]
        rim = jnp.where(sub8 == 0, rim + roll(rim, -1, 0), jnp.where(sub8 == 7, rim + roll(rim, 1, 0), 0.0))
        return [(tmp, i, v[0:own_y]), (H1, (i + 3, slice(y1, 2 * y1)), rim)]


    def coarsen_row(i):
        return [(H1, (i + 3, slice(0, y1)), 0.5 * (tmp[i, pl.ds(0, y1, 2), :] + tmp[i, pl.ds(1, y1, 2), :]))]

    here, behind = set(), set()
    zero = {0, 1, 2, rows - 3, rows - 2, rows - 1}
    done = {name: set() for name in ("stress", "star", "source", "smooth", "pair", "coarsen")}

    def around_of(r):
        return {r - 1, r, r + 1}

    def run(name, rows_of, ready, body, size):
        fresh = [r for r in rows_of if r not in done[name] and ready(r)]
        for low in [r for r in fresh if r - 1 not in fresh]:
            high = low
            while high in fresh:
                high += 1
            loop(low, high, body, min(size, high - low))
        done[name] |= set(fresh)

    def advance(full):
        run("stress", range(1, rows - 1), lambda r: around_of(r) <= here, stress_row, G_STRESS)
        if not full:
            return
        run("star", range(2, rows - 2), lambda r: around_of(r) <= done["stress"] and r in behind, star_row, G_FINE)
        run("source", range(OFF, OFF + own_x), lambda r: around_of(r) <= done["star"] & behind, source_row, G_FINE)
        known = done["source"] | zero
        run("smooth", range(2, rows - 2), lambda r: around_of(r) <= known,
            lambda r: [(ZA, r, smooth(Z, r, 1, 1))], G_FINE)
        known1 = done["smooth"] | {0, 1, rows - 2, rows - 1}
        run("pair", range(half + 2), lambda i: set(range(2 * i, 2 * i + 4)) <= known1, fine_residual, 5)
        run("coarsen", range(half + 2), lambda i: i in done["pair"], coarsen_row, half + 2)

    def r0_faces(low, high):
        for dy in (1, -1):
            sy, ty = y_spans(dy, RIM)
            span = slice(low - OFF + RIM, high - OFF + RIM)
            remote(R0.at[span, sy], R0.at[span, ty], 0, dy, face_copies)

    def r0_side(dx):
        at = left_copies if dx == 1 else right_copies
        for dy in (1, -1):
            send(at, R0, R0, RIM, RIM, 3, dx, dy)
        send(at, R0, R0, RIM, RIM, RIM, dx, 0)

    face_copies, left_copies, right_copies = group(), group(), group()
    split = OFF

    def arrive(copies, low, high, full):
        finish(copies)
        here.update(range(OFF + low, OFF + high))
        advance(full)

    for turn in range(3):
        listen(turn, False)
    arrive(slabs[0], *cuts[0], False)
    arrive(slabs[1], *cuts[1], False)
    finish(d_copies)
    high_rows = set(range(OFF + own_x, rows))
    behind.update(range(OFF + own_x))
    advance(True)
    listen(0, True)
    arrive(slabs[2], *cuts[2], True)
    arrive(low_copies, -OFF, 0, False)
    listen(1, True)
    arrive(slabs[3], *cuts[3], True)
    while split in done["source"]:
        split += 1
    r0_faces(OFF, split)
    r0_side(-1)
    listen(2, True)
    finish(high_copies)
    here.update(high_rows)
    behind.update(high_rows)
    arrive(slabs[4], *cuts[4], True)
    r0_faces(split, OFF + own_x)
    r0_side(1)
    packs = half // 2
    lane1 = lane_of(2 * y1, nz)
    even1 = lane1 % 2 == 0
    even = lane_of(y1 + 2, nz) % 2 == 0
    def put(slot, v):
        G1[0, slot, 0:y1] = v[0:y1]
        G1[0, slot, y1 : y1 + 1] = v[y1 : y1 + 1]
        G1[0, slot, y1 + 1 : y1 + 2] = v[2 * y1 - 1 : 2 * y1]

    for i in range(packs):
        put(1 + i, jnp.where(even1, H1[4 + 2 * i], H1[5 + 2 * i]))
    rim = jnp.where(even1, H1[half + 4], H1[3])
    put(0, rim)
    put(packs + 1, rim)
    g_copies = group()
    kept = 3
    for dx in (1, -1, 0):
        for dy in range(ny):
            if dx == 0 and dy == 0:
                continue
            k = (ny - dy) % ny
            if dx == 0:
                src, dst = pl.ds(0, packs + 1), pl.ds(0, packs + 1)
            elif dx == 1:
                src, dst = pl.ds(packs + 1 - kept, kept + 1), pl.ds(packs + 2, kept + 1)
            else:
                src, dst = pl.ds(0, kept + 1), pl.ds(packs + 3 + kept, kept + 1)
            remote(G1.at[0, src], G1.at[k, dst], dx, dy, g_copies)
    loop(2, half + 6, lambda r: [(H1A, r + 1, smooth(H1, r, 1, 2))], half + 4)
    lane8 = lane_of(y1, nz)
    for j in range(quarter + 4):
        tmp1[j] = pair(smooth_pair(H1A, 2 * j + 1, 1, 2), 2, 1)
    for which, order in enumerate(((2, 3, 4, 5), (6, 7, 0, 1))):
        gathered = None
        for at, j in enumerate(order):
            v = 0.5 * (tmp1[j, pl.ds(0, y1, 2), :] + tmp1[j, pl.ds(1, y1, 2), :])
            gathered = v if gathered is None else jnp.where(lane8 % 4 == at, v, gathered)
        G2[0, REACH, which] = gathered
    low2 = lane8 % 4 < 2
    near, beyond = G2[0, REACH, 0], G2[0, REACH, 1]
    GX[0] = jnp.where(low2, beyond, near)
    GX[1] = jnp.where(low2, near, beyond)
    h_copies = group()
    order = sorted(far, key=lambda to: (to[0] <= 0, to[0] if to[0]>0 else -to[0], -to[1]))

    def spread_out(sign):
        for dx, dy in order:
            dx = sign * dx
            slot = G2.at[(ny - dy) % ny, REACH - dx]
            if abs(dx) == REACH:
                remote(GX.at[0 if dx > 0 else 1], slot.at[0], dx, dy, h_copies)
            else:
                remote(G2.at[0, REACH], slot, dx, dy, h_copies)

    second = me_x >= nx // 2
    size = groups[h_copies], len(sent)
    pl.when(second)(lambda: spread_out(1))
    groups[h_copies] = size[0]
    del sent[size[1]:]
    pl.when(jnp.logical_not(second))(lambda: spread_out(-1))
    wide = own_x + 2 * RIM

    def base_row(r):
        total = R0[r] + X1[r] + X2[r] + smooth(X2, r, 1, 1)
        return [(A, r - 3, PA[r - RIM + OFF] - WEIGHT * total)]

    known = set()
    done.update({"first": set(), "second": set(), "base": set()})

    def refine(copies, low, high):
        finish(copies)
        known.update(range(low, high))
        run("first", range(1, wide - 1), lambda r: around_of(r) <= known,
            lambda r: [(X1, r, smooth(R0, r, 1, 1))], G_FINE)
        run("second", range(2, wide - 2), lambda r: around_of(r) <= done["first"],
            lambda r: [(X2, r, smooth(X1, r, 1, 1))], G_FINE)
        run("base", range(3, wide - 3), lambda r: around_of(r) <= done["second"], base_row, G_FINE)

    refine(face_copies, RIM, RIM + own_x)
    refine(left_copies, 0, RIM)
    refine(right_copies, RIM + own_x, wide)
    finish(g_copies)
    full1 = ny * y1
    count1 = packs + 2 * kept

    def joined(k, q):
        if q < 0:
            v = G1[k, packs + 2 + q + kept]
            return v + jnp.where(even, 0.0, G1[k, 0]) if q == -1 else v
        if q >= packs:
            v = G1[k, packs + 4 + kept + q - packs]
            return v + jnp.where(even, G1[k, 0], 0.0) if q == packs else v
        v = G1[k, 1 + q]
        if q == 0:
            v = v + jnp.where(even, G1[k, packs + 2 + kept], 0.0)
        if q == packs - 1:
            v = v + jnp.where(even, 0.0, G1[k, packs + 3 + kept])
        return v

    for q in range(-kept, packs + kept):
        frames = [joined(k, q) for k in range(ny)]
        for k in range(ny):
            before, after = frames[(k - 1) % ny], frames[(k + 1) % ny]
            v = frames[k][0:y1] + jnp.where(sub8 == 0, before[y1 : y1 + 1], 0.0)
            v = v + jnp.where(sub8 == y1 - 1, after[y1 + 1 : y1 + 2], 0.0)
            for bit in (0, 1):
                f = spread(v, 1, bit)
                r = 2 * (q + kept) + bit
                F1[r, k * y1 : (k + 1) * y1, :] = f
                P1A[r, k * y1 : (k + 1) * y1, :] = -WEIGHT * f
    sweep(P1A, P1B, F1, 1, 2 * count1 - 1, 1, 2)
    finish(h_copies)
    full2 = ny * y2
    blank8 = jnp.zeros((y1, nz), F32)
    ends = (0, 2 * REACH)

    def spill(k, s):
        return G2[k, s, 0 if s in ends else 1]

    def joined2(k, s):
        before = spill(k, s - 1) if s > 0 else blank8
        after = spill(k, s + 1) if s < 2 * REACH else blank8
        return G2[k, s, 0] + jnp.where(low2, before, after)

    for s in range(2 * REACH + 1):
        frames = [joined2(k, s) for k in range(ny)]
        turned = [roll(v, y2, 0) for v in frames]
        for m in range(ny // 2):
            k = 2 * m
            if ny == 2:
                v = frames[0] + turned[1]
            else:
                lower = frames[k] + jnp.where(sub8 < 2, turned[(k - 1) % ny], turned[(k + 1) % ny])
                upper = turned[k + 1] + jnp.where(sub8 < 6, frames[k], frames[(k + 2) % ny])
                v = jnp.where(sub8 < y2, lower, upper)
            moved = {by: roll(v, by, 1) if by else v for by in range(-3, 4)}
            for row in range(4):
                f = moved[-row]
                for at in range(1, 4):
                    f = jnp.where(lane8 % 4 == at, moved[at - row], f)
                F2[4 * s + row, 8 * m : 8 * m + 8, :] = f
    rows2 = 4 * (2 * REACH + 1)
    middle2 = range(12, rows2 - 12)

    def level2_row(r):
        v = smooth(F2, r, 1, 4)
        stores = [(P2A, r, v)]
        if r in middle2:
            stores.append((P2B, r, -WEIGHT * (F2[r] + v)))
        return stores

    loop(3, rows2 - 3, level2_row, rows2 - 6)
    rows3 = rows2 // 2

    def coarse_source(i):
        p = P2A[2 * i] + P2A[2 * i + 1]
        line = row_of(p.shape[0], nz) % 2 == 0
        up, down = roll(p, -1, 0), roll(p, 1, 0)
        pairs = p + jnp.where(line, up, down)
        beside = P2A[2 * i - 1] + P2A[2 * i + 2]
        sides = pairs + jnp.where(line, down + roll(p, -2, 0), up + roll(p, 2, 0))
        beside = beside + jnp.where(line, roll(beside, -1, 0), roll(beside, 1, 0))
        lanes = lane_of(p.shape[0], nz)
        inner = KEEP * pairs + WEIGHT * (pairs + beside + sides)
        low = (lanes // 4) % 2 == 0
        inner = inner + jnp.where(low, roll(inner, -4, 1), roll(inner, 4, 1))
        above = jnp.where(lanes >= nz - 4, pairs, roll(pairs, -4, 1))
        below = jnp.where(lanes < 4, pairs, roll(pairs, 4, 1))
        above2 = jnp.where(lanes >= nz - 8, above, roll(pairs, -8, 1))
        below2 = jnp.where(lanes < 8, below, roll(pairs, 8, 1))
        outer = pairs + above + below + jnp.where(low, above2, below2)
        return [(F3, i, 0.5 * (inner + 4.0 * WEIGHT * outer))]

    loop(2, rows3 - 2, coarse_source, rows3 - 4)
    smooth_all(F3, P3A, 3, rows3 - 3, 2, 8)
    smooth_all(P3A, P3B, 4, rows3 - 4, 2, 8)
    smooth_all(P3B, P3C, 5, rows3 - 5, 2, 8)

    def line_row(r):
        left = smooth(P3C, r, 2, 8)
        eight = sum(left[8 * m : 8 * m + 8] for m in range(full2 // 8))
        four = eight + roll(eight, 2, 0) + roll(eight, 4, 0) + roll(eight, 6, 0)
        mean = jnp.concatenate([(2.0 / full2) * four] * (full2 // 8), axis=0)
        v = -WEIGHT * (F3[r] + P3A[r] + P3B[r] + P3C[r] + mean)
        return [(P2B, x, P2B[x] + v) for x in (2 * r, 2 * r + 1)]

    loop(6, rows3 - 6, line_row, rows3 - 12)
    sweep(P2B, P2A, F2, 13, 23, 1, 4)

    def second_row(m):
        p, around = stencil(P2A, m, 1, 4)
        v = KEEP * p + WEIGHT * (around - F2[m])
        E1[m - 14, pl.ds(0, full2, 2), :] = v
        E1[m - 14, pl.ds(1, full2, 2), :] = v
        e = E1[m - 14]
        r = 2 * (m - 13)
        P1B[r] = P1B[r] + e
        P1B[r + 1] = P1B[r + 1] + e

    for m in range(14, 22):
        second_row(m)
    sweep(P1B, P1A, F1, 3, 17, 1, 2)
    sweep(P1A, P1B, F1, 4, 16, 1, 2)
    for m in range(4, 16):
        e = m - 4
        for shift in (0, 1):
            E0[e, pl.ds(shift, y1, 2), :] = P1B[m, 0:y1, :]
            E0[e, pl.ds(own_y + shift, 2, 2), :] = P1B[m, y1 : y1 + 2, :]
            E0[e, pl.ds(own_y + 4 + shift, 2, 2), :] = P1B[m, full1 - 2 : full1, :]

    def first_pair(e):
        p = E0[e]
        z = jnp.where(last, p, roll(p, -1, 1)) + jnp.where(first, p, roll(p, 1, 1))
        base = (KEEP + WEIGHT) * p + WEIGHT * (roll(p, -1, 0) + roll(p, 1, 0) + 4.0 * z)
        return [
            (Y1, 2 * e - 2, base + WEIGHT * E0[e - 1]),
            (Y1, 2 * e - 1, base + WEIGHT * E0[e + 1]),
        ]

    loop(1, 11, first_pair, 10)
    loop(1, own_x + 3, lambda r: [(PN, r - 1, A[r - 1] + smooth(Y1, r, 1, 1))], own_x + 2)
    await_lines(send_sem.at[0], sum(sent))


def closing(S, PN, vel_out, pre_out, vel, pre, sem):
    _, own_x, own_y, nz = vel.shape
    lane = lane_of(PN.shape[1], nz)
    first, last = lane == 0, lane == nz - 1
    part = 4
    for low in range(0, own_x, part):
        for x in range(low, low + part):
            p = PN[x + 1]
            pre[x] = p[0:own_y]
            gx = (0.5 * STEP) * (PN[x + 2] - PN[x])
            gy = (0.5 * STEP) * (roll(p, -1, 0) - roll(p, 1, 0))
            gz = STEP * (jnp.where(last, p, roll(p, -1, 1)) - jnp.where(first, p, roll(p, 1, 1)))
            for a, g in enumerate((gx, gy, gz)):
                vel[a, x] = S[a, OFF + x, 0:own_y] - g[0:own_y]
        span = pl.ds(low, part)
        pltpu.make_async_copy(vel.at[:, span], vel_out.at[:, span], sem.at[0]).start()
        pltpu.make_async_copy(pre.at[span], pre_out.at[span], sem.at[1]).start()
    pltpu.make_async_copy(vel, vel_out, sem.at[0]).wait()
    pltpu.make_async_copy(pre, pre_out, sem.at[1]).wait()


def per_device(nx, ny, velocity, pressure, land_type, turbine_cells, surface_drag):
    _, own_x, own_y, nz = velocity.shape
    side = (own_y // 8 + 1) * 8
    rows = own_x + 2 * OFF
    wide = own_x + 2 * RIM
    half, quarter = own_x // 2, own_x // 4
    y1 = own_y // 2
    full1, full2 = ny * y1, ny * y1 // 2
    packs = half // 2
    rows2 = quarter * (2 * REACH + 1)

    def window(*shape):
        return pltpu.VMEM((*shape, nz), F32)

    level1 = window(2 * (packs + 6), full1)
    level2 = window(rows2, full2)
    level3 = window(rows2 // 2, full2)
    frame1 = window(half + 8, 2 * y1)
    corner, face = 4 * (3 * 2 * 2 + 3 * 3), 2 * (own_x + own_y)
    total = corner + face * (3 * 3 + 1 + 1 + RIM)
    total += 5 * (y1 + 2) * 3 * ny + (2 * REACH + 1) * ny * 2 * y1
    scratch = [
        window(3, rows, side), window(rows, side), window(rows, side), window(rows, side),
        window(3, rows, side), window(wide, side),
        window(rows, side), window(rows, side),
        window(wide, side), window(wide, side), window(own_x + 2, side), window(own_x + 4, side),
        window(half + 2, own_y), window(quarter + 4, 2 * y1),
        pltpu.VMEM((own_x, own_y, nz), jnp.int32),
        pltpu.VMEM(land_type.shape, jnp.int32),
        pltpu.SMEM(surface_drag.shape, F32),
        frame1, window(half + 10, 2 * y1), window(ny, packs + 10, y1 + 2),
        level1, level1, level1,
        window(ny, 2 * REACH + 1, 2, y1), window(2, y1),
        level2, level2, level2, level3, level3, level3, level3,
        window(8, full1), window(12, side),
        window(total),
        pltpu.SemaphoreType.DMA((5,)),
        pltpu.SemaphoreType.DMA((1,)),
        pltpu.SemaphoreType.DMA((13,)),
        pltpu.SemaphoreType.REGULAR((7,)),
    ]
    inside = pl.BlockSpec(memory_space=pltpu.VMEM)
    outside = pl.BlockSpec(memory_space=pltpu.HBM)
    arguments = [
        pltpu.with_memory_space_constraint(a, pltpu.HBM)
        for a in (velocity, pressure, turbine_cells, land_type, surface_drag)
    ]
    star, middle = pl.pallas_call(
        functools.partial(kernel, nx, ny),
        out_shape=(
            jax.ShapeDtypeStruct((3, rows, side, nz), F32),
            jax.ShapeDtypeStruct((own_x + 2, side, nz), F32),
        ),
        in_specs=[outside] * 5,
        out_specs=(inside, inside),
        scratch_shapes=scratch,
        compiler_params=pltpu.CompilerParams(
            collective_id=0, has_side_effects=True, vmem_limit_bytes=VMEM_LIMIT
        ),
    )(*arguments)
    return pl.pallas_call(
        closing,
        out_shape=(
            jax.ShapeDtypeStruct(velocity.shape, F32),
            jax.ShapeDtypeStruct(pressure.shape, F32),
        ),
        in_specs=[inside, inside],
        out_specs=(outside, outside),
        scratch_shapes=[
            pltpu.VMEM(velocity.shape, F32),
            pltpu.VMEM(pressure.shape, F32),
            pltpu.SemaphoreType.DMA((2,)),
        ],
        compiler_params=pltpu.CompilerParams(vmem_limit_bytes=VMEM_LIMIT),
    )(star, middle)


def solution(mesh):
    in_specs = (
        P(None, "gx", "gy", None),
        P("gx", "gy", None),
        P("gx", "gy"),
        P("gx", "gy", None),
        P(),
    )
    out_specs = (P(None, "gx", "gy", None), P("gx", "gy", None))
    body = functools.partial(per_device, mesh.shape["gx"], mesh.shape["gy"])
    return jax.shard_map(
        body, mesh=mesh, in_specs=in_specs, out_specs=out_specs, check_vma=False
    )
```

```python
import functools
import math

import jax
import jax.numpy as jnp
from jax import lax
from jax.experimental import pallas as pl
from jax.experimental.pallas import tpu as pltpu
from jax.sharding import PartitionSpec as P

MESH = pl.DeviceIdType.MESH
F32 = jnp.float32
STEP = 0.1
WEIGHT = 0.8 / 12.0
KEEP = 0.2
OFF = 3
RIM = 4
G_STRESS = 4
G_FINE = 8
VMEM_LIMIT = 24000 * 1024
REACH = 4


def loop(low, high, body, group):
    def run(indices):
        found = [store for index in indices for store in body(index)]
        for ref, at, value in found:
            ref[at] = value

    whole = (high - low) // group
    if whole == 1:
        run(range(low, low + group))
    elif whole > 1:

        def step(index, carry):
            run([low + index * group + k for k in range(group)])
            return carry

        lax.fori_loop(0, whole, step, 0)
    if low + whole * group < high:
        run(range(low + whole * group, high))


def lane_of(count, nz):
    return lax.broadcasted_iota(jnp.int32, (count, nz), 1)


def row_of(count, nz):
    return lax.broadcasted_iota(jnp.int32, (count, nz), 0)


def roll(v, shift, axis):
    return pltpu.roll(v, shift % v.shape[axis], axis)


def kernel(
    nx, ny, vel_in, pre_in, turb_in, land_in, coeff_in, S, PN,
    W, D, PA, F, T, R0, Z, ZA, X1, X2, A, Y1, tmp, tmp1, turb, land, coeff,
    H1, H1A, G1, F1, P1A, P1B, G2, GX, F2, P2A, P2B, F3, P3A, P3B, P3C, E1, E0,
    spare, load_sem, send_sem, recv_sem, token,
):
    me_x, me_y = lax.axis_index("gx"), lax.axis_index("gy")
    _, own_x, own_y, nz = vel_in.shape
    side = W.shape[2]
    rows = own_x + 2 * OFF
    half, quarter = own_x // 2, own_x // 4
    y1, y2 = own_y // 2, own_y // 4

    loads = [
        pltpu.make_async_copy(turb_in, turb, load_sem.at[0]),
        pltpu.make_async_copy(land_in, land, load_sem.at[1]),
        pltpu.make_async_copy(coeff_in, coeff, load_sem.at[2]),
        pltpu.make_async_copy(vel_in, W.at[:, OFF : OFF + own_x, 0:own_y], load_sem.at[3]),
        pltpu.make_async_copy(pre_in, PA.at[OFF : OFF + own_x, 0:own_y], load_sem.at[3]),
    ]

    def device(dx, dy):
        return (lax.rem(me_x + dx + nx, nx), lax.rem(me_y + dy + ny, ny))

    far = [(dx, dy) for dx in range(-REACH, REACH + 1) for dy in range(ny) if dx or dy]
    close = [(dx, dy) for dx, dy in far if dx == 0 or (dy == 0 and abs(dx) < 2)]
    barrier = pltpu.get_barrier_semaphore()
    for dx, dy in close:
        pl.semaphore_signal(barrier, inc=1, device_id=device(dx, dy), device_id_type=MESH)
    for load in loads:
        load.start()

    groups, sent = [], []

    def group():
        groups.append(0)
        return len(groups) - 1

    def lines_of(ref):
        return math.prod(ref.shape) // nz

    def remote(src, dst, dx, dy, at):
        groups[at] += lines_of(dst)
        sent.append(lines_of(src))
        pltpu.make_async_remote_copy(
            src_ref=src, dst_ref=dst, send_sem=send_sem.at[0], recv_sem=recv_sem.at[at],
            device_id=device(dx, dy), device_id_type=MESH,
        ).start()

    def await_lines(sem, count):
        part = spare.at[pl.ds(0, count)]
        pltpu.make_async_copy(part, part, sem).wait()

    def finish(at):
        await_lines(recv_sem.at[at], groups[at])

    def x_spans(dx, width, src_base, dst_base):
        if dx == 0:
            return slice(src_base, src_base + own_x), slice(dst_base, dst_base + own_x)
        if dx == 1:
            high = src_base + own_x
            return slice(high - width, high), slice(dst_base - width, dst_base)
        return slice(src_base, src_base + width), slice(dst_base + own_x, dst_base + own_x + width)

    def y_spans(dy, width):
        if dy == 0:
            return slice(0, own_y), slice(0, own_y)
        if dy == 1:
            return slice(own_y - width, own_y), slice(side - width, side)
        return slice(0, width), slice(own_y, own_y + width)

    def send(at, src, dst, src_base, dst_base, width, dx, dy, lead=False):
        sx, tx = x_spans(dx, width, src_base, dst_base)
        sy, ty = y_spans(dy, width)
        if lead:
            remote(src.at[:, sx, sy], dst.at[:, tx, ty], dx, dy, at)
        else:
            remote(src.at[sx, sy], dst.at[tx, ty], dx, dy, at)

    corners = [(dx, dy) for dx in (1, -1) for dy in (1, -1)]
    faces = [(0, 1), (0, -1), (1, 0), (-1, 0)]

    def hear(turn, dx):
        at = turn + (0 if dx < 0 else 3)
        pl.semaphore_wait(token.at[at], 1)
        if turn < 2:
            tell(turn + 1, -dx)

    def tell(turn, dx):
        at = turn + (3 if dx < 0 else 0)
        pl.semaphore_signal(token.at[at], inc=1, device_id=device(dx, 0), device_id_type=MESH)

    def listen(turn, crosses):
        for dx, end in ((1, me_x >= nx - 1 - turn), (-1, me_x <= turn + 1)):
            pl.when(end if crosses else jnp.logical_not(end))(functools.partial(hear, turn, dx))

    pl.semaphore_wait(barrier, len(close))
    for dy in range(1, ny):
        pl.semaphore_signal(token.at[6], inc=1, device_id=device(0, dy), device_id_type=MESH)
    piece = own_x // 4
    low_end, high_end = 2 * piece, own_x - own_x // 8
    middle = (low_end + high_end) // 2
    middle -= 1
    cuts = [(0, piece), (piece, low_end), (low_end, middle), (middle, high_end), (high_end, own_x)]

    def slab(cut):
        low, high = cut
        at = group()
        for dy in (1, -1):
            sy, ty = y_spans(dy, 3)
            remote(vel_in.at[:, low:high, sy], W.at[:, OFF + low : OFF + high, ty], 0, dy, at)
        return at

    low_copies, high_copies = group(), group()
    for dx, at in ((-1, high_copies), (1, low_copies)):
        send(at, vel_in, W, 0, OFF, 3, dx, 0, True)
    slabs = [slab(cut) for cut in cuts[:2]]
    shape = (own_y, own_y)
    diagonal = lax.broadcasted_iota(jnp.int32, shape, 0) == lax.broadcasted_iota(jnp.int32, shape, 1)
    lane16 = lane_of(own_y, nz)
    loads[1].wait()
    loads[2].wait()
    kinds = land[...]
    ground = jnp.zeros(kinds.shape, F32)
    for kind in range(coeff.shape[0]):
        ground = jnp.where(kinds == kind, coeff[kind], ground)
    loads[0].wait()
    for x in range(own_x):
        column = jnp.sum(jnp.where(diagonal, ground[x : x + 1, :], 0.0), axis=1, keepdims=True)
        low = jnp.where(lane16 == 0, column, 0.0)
        D[OFF + x, 0:own_y, :] = 2.0 * turb[x].astype(F32) + low
    d_copies = group()
    for dx, dy in faces:
        at = high_copies if dx == -1 else d_copies
        send(at, D, D, OFF, OFF, 1, dx, dy)
        send(at, pre_in, PA, 0, OFF, 1, dx, dy)
    slabs += [slab(cut) for cut in cuts[2:3]]
    pl.semaphore_wait(token.at[6], ny - 1)
    tell(0, 1)
    tell(0, -1)
    for dx, at in ((-1, high_copies), (1, low_copies)):
        for dy in (1, -1):
            send(at, vel_in, W, 0, OFF, 2, dx, dy, True)
    slabs += [slab(cut) for cut in cuts[3:]]
    blank = jnp.zeros((side, nz), F32)
    for r in (1, 2, rows - 3, rows - 2):
        Z[r] = blank
    for r in (0, 1, rows - 2, rows - 1):
        ZA[r] = blank
    blank1 = jnp.zeros((2 * y1, nz), F32)
    for r in (1, 2, half + 5, half + 6):
        H1[r] = blank1
    for r in (0, 1, 2, half + 7, half + 8, half + 9):
        H1A[r] = blank1
    await_lines(load_sem.at[3], lines_of(vel_in) + lines_of(pre_in))
    lane = lane_of(side, nz)
    first, last = lane == 0, lane == nz - 1

    def up0(v):
        return jnp.where(last, 0.0, roll(v, -1, 1))

    def down0(v):
        return jnp.where(first, 0.0, roll(v, 1, 1))

    def stress_row(r):
        v = [W[a, r] for a in range(3)]
        gx = [0.5 * (W[a, r + 1] - W[a, r - 1]) for a in range(3)]
        gy = [0.5 * (roll(v[a], -1, 0) - roll(v[a], 1, 0)) for a in range(3)]
        gz = [up0(v[a]) - down0(v[a]) for a in range(3)]
        e01, e02, e12 = gx[1] + gy[0], gx[2] + gz[0], gy[2] + gz[1]
        q = 2.0 * (gx[0] * gx[0] + gy[1] * gy[1] + gz[2] * gz[2]) + e01 * e01 + e02 * e02 + e12 * e12
        visc = 0.03 * jnp.sqrt(q)
        twice = visc + visc
        t00, t11, t22 = twice * gx[0], twice * gy[1], twice * gz[2]
        t01, t02, t12 = visc * e01, visc * e02, visc * e12
        flat = v[0] * v[0] + v[1] * v[1]
        ghost = 0.03 * jnp.sqrt(2.0 * v[2] * v[2] + flat)
        ghosts = [ghost * v[0], ghost * v[1], (ghost + ghost) * v[2]]
        out = [(T, (0, r), t00), (T, (1, r), t01), (T, (2, r), t02)]
        for a, (ty, tz) in enumerate(((t01, t02), (t11, t12), (t12, t22))):
            change = 0.5 * (roll(ty, -1, 0) - roll(ty, 1, 0))
            change += jnp.where(last, -ghosts[a], roll(tz, -1, 1)) - jnp.where(first, ghosts[a], roll(tz, 1, 1))
            change -= v[0] * gx[a] + v[1] * gy[a] + v[2] * gz[a]
            if a == 0:
                change += 1.0
            out.append((S, (a, r), v[a] + STEP * change))
        return out

    def star_row(r):
        drag = STEP * (D[r] * jnp.sqrt(W[0, r] * W[0, r] + W[1, r] * W[1, r]))
        stores = []
        for a in range(3):
            v = S[a, r] + (0.5 * STEP) * (T[a, r + 1] - T[a, r - 1])
            stores.append((S, (a, r), v - drag * W[a, r] if a < 2 else v))
        return stores


    def stencil(src, r, sy, sz):
        p = src[r]
        lanes = lane_of(p.shape[0], nz)
        z = jnp.where(lanes >= nz - sz, p, roll(p, -sz, 1)) + jnp.where(lanes < sz, p, roll(p, sz, 1))
        s = src[r + 1] + src[r - 1] + roll(p, -sy, 0) + roll(p, sy, 0)
        return p, s + 4.0 * z

    def smooth(src, r, sy, sz):
        p, around = stencil(src, r, sy, sz)
        return KEEP * p + WEIGHT * around

    def smooth_all(src, dst, low, high, sy, sz, group=64):
        loop(low, high, lambda r: [(dst, r, smooth(src, r, sy, sz))], min(group, high - low))

    def sweep(src, dst, f, low, high, sy, sz, group=64):
        def body(r):
            p, around = stencil(src, r, sy, sz)
            return [(dst, r, KEEP * p + WEIGHT * (around - f[r]))]

        loop(low, high, body, min(group, high - low))

    def residual(src, f, r, sy, sz):
        p, around = stencil(src, r, sy, sz)
        return f[r] - (around - 12.0 * p)

    own = row_of(side, nz) < own_y

    def source_row(r):
        s1, s2 = S[1, r], S[2, r]
        flat = 0.5 * (S[0, r + 1] - S[0, r - 1] + roll(s1, -1, 0) - roll(s1, 1, 0))
        f = (flat + up0(s2) - down0(s2)) / STEP
        p, around = stencil(PA, r, 1, 1)
        left = jnp.where(own, f - (around - 12.0 * p), 0.0)
        return [(Z, r, left), (R0, (r + RIM - OFF, slice(0, own_y)), left[0:own_y])]

    def pair(v, stride, axis):
        at = lax.broadcasted_iota(jnp.int32, v.shape, axis)
        even = (at // stride) % 2 == 0
        return v + jnp.where(even, roll(v, -stride, axis), roll(v, stride, axis))

    def spread(v, stride, bit):
        at = (lane_of(v.shape[0], nz) // stride) % 2
        return jnp.where(at == bit, v, roll(v, stride if bit == 0 else -stride, 1))

    sub8 = row_of(y1, nz)

    def smooth_pair(src, r, sy, sz):
        a, b = src[r], src[r + 1]
        p = a + b
        lanes = lane_of(p.shape[0], nz)
        z = jnp.where(lanes >= nz - sz, p, roll(p, -sz, 1)) + jnp.where(lanes < sz, p, roll(p, sz, 1))
        around = p + src[r - 1] + src[r + 2] + roll(p, -sy, 0) + roll(p, sy, 0) + 4.0 * z
        return KEEP * p + WEIGHT * around

    def fine_residual(i):
        v = pair(smooth_pair(ZA, 2 * i + 1, 1, 1), 1, 1)
        rim = 0.5 * v[own_y : own_y + 8]
        rim = jnp.where(sub8 == 0, rim + roll(rim, -1, 0), jnp.where(sub8 == 7, rim + roll(rim, 1, 0), 0.0))
        return [(tmp, i, v[0:own_y]), (H1, (i + 3, slice(y1, 2 * y1)), rim)]


    def coarsen_row(i):
        return [(H1, (i + 3, slice(0, y1)), 0.5 * (tmp[i, pl.ds(0, y1, 2), :] + tmp[i, pl.ds(1, y1, 2), :]))]

    here, behind = set(), set()
    zero = {0, 1, 2, rows - 3, rows - 2, rows - 1}
    done = {name: set() for name in ("stress", "star", "source", "smooth", "pair", "coarsen")}

    def around_of(r):
        return {r - 1, r, r + 1}

    def run(name, rows_of, ready, body, size):
        fresh = [r for r in rows_of if r not in done[name] and ready(r)]
        for low in [r for r in fresh if r - 1 not in fresh]:
            high = low
            while high in fresh:
                high += 1
            loop(low, high, body, min(size, high - low))
        done[name] |= set(fresh)

    def advance(full):
        run("stress", range(1, rows - 1), lambda r: around_of(r) <= here, stress_row, G_STRESS)
        if not full:
            return
        run("star", range(2, rows - 2), lambda r: around_of(r) <= done["stress"] and r in behind, star_row, G_FINE)
        run("source", range(OFF, OFF + own_x), lambda r: around_of(r) <= done["star"] & behind, source_row, G_FINE)
        known = done["source"] | zero
        run("smooth", range(2, rows - 2), lambda r: around_of(r) <= known,
            lambda r: [(ZA, r, smooth(Z, r, 1, 1))], G_FINE)
        known1 = done["smooth"] | {0, 1, rows - 2, rows - 1}
        run("pair", range(half + 2), lambda i: set(range(2 * i, 2 * i + 4)) <= known1, fine_residual, 5)
        run("coarsen", range(half + 2), lambda i: i in done["pair"], coarsen_row, half + 2)

    def r0_faces(low, high):
        for dy in (1, -1):
            sy, ty = y_spans(dy, RIM)
            span = slice(low - OFF + RIM, high - OFF + RIM)
            remote(R0.at[span, sy], R0.at[span, ty], 0, dy, face_copies)

    def r0_side(dx):
        at = left_copies if dx == 1 else right_copies
        for dy in (1, -1):
            send(at, R0, R0, RIM, RIM, 3, dx, dy)
        send(at, R0, R0, RIM, RIM, RIM, dx, 0)

    face_copies, left_copies, right_copies = group(), group(), group()
    split = OFF

    def arrive(copies, low, high, full):
        finish(copies)
        here.update(range(OFF + low, OFF + high))
        advance(full)

    for turn in range(3):
        listen(turn, False)
    arrive(slabs[0], *cuts[0], False)
    arrive(slabs[1], *cuts[1], False)
    finish(d_copies)
    high_rows = set(range(OFF + own_x, rows))
    behind.update(range(OFF + own_x))
    advance(True)
    listen(0, True)
    arrive(slabs[2], *cuts[2], True)
    arrive(low_copies, -OFF, 0, False)
    listen(1, True)
    arrive(slabs[3], *cuts[3], True)
    while split in done["source"]:
        split += 1
    r0_faces(OFF, split)
    r0_side(-1)
    listen(2, True)
    finish(high_copies)
    here.update(high_rows)
    behind.update(high_rows)
    arrive(slabs[4], *cuts[4], True)
    r0_faces(split, OFF + own_x)
    r0_side(1)
    packs = half // 2
    lane1 = lane_of(2 * y1, nz)
    even1 = lane1 % 2 == 0
    even = lane_of(y1 + 2, nz) % 2 == 0
    def put(slot, v):
        G1[0, slot, 0:y1] = v[0:y1]
        G1[0, slot, y1 : y1 + 1] = v[y1 : y1 + 1]
        G1[0, slot, y1 + 1 : y1 + 2] = v[2 * y1 - 1 : 2 * y1]

    for i in range(packs):
        put(1 + i, jnp.where(even1, H1[4 + 2 * i], H1[5 + 2 * i]))
    rim = jnp.where(even1, H1[half + 4], H1[3])
    put(0, rim)
    put(packs + 1, rim)
    g_copies = group()
    kept = 3
    for dx in (1, -1, 0):
        for dy in range(ny):
            if dx == 0 and dy == 0:
                continue
            k = (ny - dy) % ny
            if dx == 0:
                src, dst = pl.ds(0, packs + 1), pl.ds(0, packs + 1)
            elif dx == 1:
                src, dst = pl.ds(packs + 1 - kept, kept + 1), pl.ds(packs + 2, kept + 1)
            else:
                src, dst = pl.ds(0, kept + 1), pl.ds(packs + 3 + kept, kept + 1)
            remote(G1.at[0, src], G1.at[k, dst], dx, dy, g_copies)
    loop(2, half + 6, lambda r: [(H1A, r + 1, smooth(H1, r, 1, 2))], half + 4)
    lane8 = lane_of(y1, nz)
    for j in range(quarter + 4):
        tmp1[j] = pair(smooth_pair(H1A, 2 * j + 1, 1, 2), 2, 1)
    for which, order in enumerate(((2, 3, 4, 5), (6, 7, 0, 1))):
        gathered = None
        for at, j in enumerate(order):
            v = 0.5 * (tmp1[j, pl.ds(0, y1, 2), :] + tmp1[j, pl.ds(1, y1, 2), :])
            gathered = v if gathered is None else jnp.where(lane8 % 4 == at, v, gathered)
        G2[0, REACH, which] = gathered
    low2 = lane8 % 4 < 2
    near, beyond = G2[0, REACH, 0], G2[0, REACH, 1]
    GX[0] = jnp.where(low2, beyond, near)
    GX[1] = jnp.where(low2, near, beyond)
    h_copies = group()
    order = sorted(far, key=lambda to: (to[0] <= 0, to[0] if to[0]>0 else -to[0], -to[1]))

    def spread_out(sign):
        for dx, dy in order:
            dx = sign * dx
            slot = G2.at[(ny - dy) % ny, REACH - dx]
            if abs(dx) == REACH:
                remote(GX.at[0 if dx > 0 else 1], slot.at[0], dx, dy, h_copies)
            else:
                remote(G2.at[0, REACH], slot, dx, dy, h_copies)

    second = me_x >= nx // 2
    size = groups[h_copies], len(sent)
    pl.when(second)(lambda: spread_out(1))
    groups[h_copies] = size[0]
    del sent[size[1]:]
    pl.when(jnp.logical_not(second))(lambda: spread_out(-1))
    wide = own_x + 2 * RIM

    def base_row(r):
        total = R0[r] + X1[r] + X2[r] + smooth(X2, r, 1, 1)
        return [(A, r - 3, PA[r - RIM + OFF] - WEIGHT * total)]

    known = set()
    done.update({"first": set(), "second": set(), "base": set()})

    def refine(copies, low, high):
        finish(copies)
        known.update(range(low, high))
        run("first", range(1, wide - 1), lambda r: around_of(r) <= known,
            lambda r: [(X1, r, smooth(R0, r, 1, 1))], G_FINE)
        run("second", range(2, wide - 2), lambda r: around_of(r) <= done["first"],
            lambda r: [(X2, r, smooth(X1, r, 1, 1))], G_FINE)
        run("base", range(3, wide - 3), lambda r: around_of(r) <= done["second"], base_row, G_FINE)

    refine(face_copies, RIM, RIM + own_x)
    refine(right_copies, RIM + own_x, wide)
    refine(left_copies, 0, RIM)
    finish(g_copies)
    full1 = ny * y1
    count1 = packs + 2 * kept

    def joined(k, q):
        if q < 0:
            v = G1[k, packs + 2 + q + kept]
            return v + jnp.where(even, 0.0, G1[k, 0]) if q == -1 else v
        if q >= packs:
            v = G1[k, packs + 4 + kept + q - packs]
            return v + jnp.where(even, G1[k, 0], 0.0) if q == packs else v
        v = G1[k, 1 + q]
        if q == 0:
            v = v + jnp.where(even, G1[k, packs + 2 + kept], 0.0)
        if q == packs - 1:
            v = v + jnp.where(even, 0.0, G1[k, packs + 3 + kept])
        return v

    for q in range(-kept, packs + kept):
        frames = [joined(k, q) for k in range(ny)]
        for k in range(ny):
            before, after = frames[(k - 1) % ny], frames[(k + 1) % ny]
            v = frames[k][0:y1] + jnp.where(sub8 == 0, before[y1 : y1 + 1], 0.0)
            v = v + jnp.where(sub8 == y1 - 1, after[y1 + 1 : y1 + 2], 0.0)
            for bit in (0, 1):
                f = spread(v, 1, bit)
                r = 2 * (q + kept) + bit
                F1[r, k * y1 : (k + 1) * y1, :] = f
                P1A[r, k * y1 : (k + 1) * y1, :] = -WEIGHT * f
    sweep(P1A, P1B, F1, 1, 2 * count1 - 1, 1, 2)
    finish(h_copies)
    full2 = ny * y2
    blank8 = jnp.zeros((y1, nz), F32)
    ends = (0, 2 * REACH)

    def spill(k, s):
        return G2[k, s, 0 if s in ends else 1]

    def joined2(k, s):
        before = spill(k, s - 1) if s > 0 else blank8
        after = spill(k, s + 1) if s < 2 * REACH else blank8
        return G2[k, s, 0] + jnp.where(low2, before, after)

    for s in range(2 * REACH + 1):
        frames = [joined2(k, s) for k in range(ny)]
        turned = [roll(v, y2, 0) for v in frames]
        for m in range(ny // 2):
            k = 2 * m
            if ny == 2:
                v = frames[0] + turned[1]
            else:
                lower = frames[k] + jnp.where(sub8 < 2, turned[(k - 1) % ny], turned[(k + 1) % ny])
                upper = turned[k + 1] + jnp.where(sub8 < 6, frames[k], frames[(k + 2) % ny])
                v = jnp.where(sub8 < y2, lower, upper)
            moved = {by: roll(v, by, 1) if by else v for by in range(-3, 4)}
            for row in range(4):
                f = moved[-row]
                for at in range(1, 4):
                    f = jnp.where(lane8 % 4 == at, moved[at - row], f)
                F2[4 * s + row, 8 * m : 8 * m + 8, :] = f
    rows2 = 4 * (2 * REACH + 1)
    middle2 = range(12, rows2 - 12)

    def level2_row(r):
        v = smooth(F2, r, 1, 4)
        stores = [(P2A, r, v)]
        if r in middle2:
            stores.append((P2B, r, -WEIGHT * (F2[r] + v)))
        return stores

    loop(3, rows2 - 3, level2_row, rows2 - 6)
    rows3 = rows2 // 2

    def coarse_source(i):
        p = P2A[2 * i] + P2A[2 * i + 1]
        line = row_of(p.shape[0], nz) % 2 == 0
        up, down = roll(p, -1, 0), roll(p, 1, 0)
        pairs = p + jnp.where(line, up, down)
        beside = P2A[2 * i - 1] + P2A[2 * i + 2]
        sides = pairs + jnp.where(line, down + roll(p, -2, 0), up + roll(p, 2, 0))
        beside = beside + jnp.where(line, roll(beside, -1, 0), roll(beside, 1, 0))
        lanes = lane_of(p.shape[0], nz)
        inner = KEEP * pairs + WEIGHT * (pairs + beside + sides)
        low = (lanes // 4) % 2 == 0
        inner = inner + jnp.where(low, roll(inner, -4, 1), roll(inner, 4, 1))
        above = jnp.where(lanes >= nz - 4, pairs, roll(pairs, -4, 1))
        below = jnp.where(lanes < 4, pairs, roll(pairs, 4, 1))
        above2 = jnp.where(lanes >= nz - 8, above, roll(pairs, -8, 1))
        below2 = jnp.where(lanes < 8, below, roll(pairs, 8, 1))
        outer = pairs + above + below + jnp.where(low, above2, below2)
        return [(F3, i, 0.5 * (inner + 4.0 * WEIGHT * outer))]

    loop(2, rows3 - 2, coarse_source, rows3 - 4)
    smooth_all(F3, P3A, 3, rows3 - 3, 2, 8)
    smooth_all(P3A, P3B, 4, rows3 - 4, 2, 8)
    smooth_all(P3B, P3C, 5, rows3 - 5, 2, 8)

    def line_row(r):
        left = smooth(P3C, r, 2, 8)
        eight = sum(left[8 * m : 8 * m + 8] for m in range(full2 // 8))
        four = eight + roll(eight, 2, 0) + roll(eight, 4, 0) + roll(eight, 6, 0)
        mean = jnp.concatenate([(2.0 / full2) * four] * (full2 // 8), axis=0)
        v = -WEIGHT * (F3[r] + P3A[r] + P3B[r] + P3C[r] + mean)
        return [(P2B, x, P2B[x] + v) for x in (2 * r, 2 * r + 1)]

    loop(6, rows3 - 6, line_row, rows3 - 12)
    sweep(P2B, P2A, F2, 13, 23, 1, 4)

    def second_row(m):
        p, around = stencil(P2A, m, 1, 4)
        v = KEEP * p + WEIGHT * (around - F2[m])
        E1[m - 14, pl.ds(0, full2, 2), :] = v
        E1[m - 14, pl.ds(1, full2, 2), :] = v
        e = E1[m - 14]
        r = 2 * (m - 13)
        P1B[r] = P1B[r] + e
        P1B[r + 1] = P1B[r + 1] + e

    for m in range(14, 22):
        second_row(m)
    sweep(P1B, P1A, F1, 3, 17, 1, 2)
    sweep(P1A, P1B, F1, 4, 16, 1, 2)
    for m in range(4, 16):
        e = m - 4
        for shift in (0, 1):
            E0[e, pl.ds(shift, y1, 2), :] = P1B[m, 0:y1, :]
            E0[e, pl.ds(own_y + shift, 2, 2), :] = P1B[m, y1 : y1 + 2, :]
            E0[e, pl.ds(own_y + 4 + shift, 2, 2), :] = P1B[m, full1 - 2 : full1, :]

    def first_pair(e):
        p = E0[e]
        z = jnp.where(last, p, roll(p, -1, 1)) + jnp.where(first, p, roll(p, 1, 1))
        base = (KEEP + WEIGHT) * p + WEIGHT * (roll(p, -1, 0) + roll(p, 1, 0) + 4.0 * z)
        return [
            (Y1, 2 * e - 2, base + WEIGHT * E0[e - 1]),
            (Y1, 2 * e - 1, base + WEIGHT * E0[e + 1]),
        ]

    loop(1, 11, first_pair, 10)
    loop(1, own_x + 3, lambda r: [(PN, r - 1, A[r - 1] + smooth(Y1, r, 1, 1))], own_x + 2)
    await_lines(send_sem.at[0], sum(sent))


def closing(S, PN, vel_out, pre_out, vel, pre, sem):
    _, own_x, own_y, nz = vel.shape
    lane = lane_of(PN.shape[1], nz)
    first, last = lane == 0, lane == nz - 1
    part = 4
    for low in range(0, own_x, part):
        for x in range(low, low + part):
            p = PN[x + 1]
            pre[x] = p[0:own_y]
            gx = (0.5 * STEP) * (PN[x + 2] - PN[x])
            gy = (0.5 * STEP) * (roll(p, -1, 0) - roll(p, 1, 0))
            gz = STEP * (jnp.where(last, p, roll(p, -1, 1)) - jnp.where(first, p, roll(p, 1, 1)))
            for a, g in enumerate((gx, gy, gz)):
                vel[a, x] = S[a, OFF + x, 0:own_y] - g[0:own_y]
        span = pl.ds(low, part)
        pltpu.make_async_copy(vel.at[:, span], vel_out.at[:, span], sem.at[0]).start()
        pltpu.make_async_copy(pre.at[span], pre_out.at[span], sem.at[1]).start()
    pltpu.make_async_copy(vel, vel_out, sem.at[0]).wait()
    pltpu.make_async_copy(pre, pre_out, sem.at[1]).wait()


def per_device(nx, ny, velocity, pressure, land_type, turbine_cells, surface_drag):
    _, own_x, own_y, nz = velocity.shape
    side = (own_y // 8 + 1) * 8
    rows = own_x + 2 * OFF
    wide = own_x + 2 * RIM
    half, quarter = own_x // 2, own_x // 4
    y1 = own_y // 2
    full1, full2 = ny * y1, ny * y1 // 2
    packs = half // 2
    rows2 = quarter * (2 * REACH + 1)

    def window(*shape):
        return pltpu.VMEM((*shape, nz), F32)

    level1 = window(2 * (packs + 6), full1)
    level2 = window(rows2, full2)
    level3 = window(rows2 // 2, full2)
    frame1 = window(half + 8, 2 * y1)
    corner, face = 4 * (3 * 2 * 2 + 3 * 3), 2 * (own_x + own_y)
    total = corner + face * (3 * 3 + 1 + 1 + RIM)
    total += 5 * (y1 + 2) * 3 * ny + (2 * REACH + 1) * ny * 2 * y1
    scratch = [
        window(3, rows, side), window(rows, side), window(rows, side), window(rows, side),
        window(3, rows, side), window(wide, side),
        window(rows, side), window(rows, side),
        window(wide, side), window(wide, side), window(own_x + 2, side), window(own_x + 4, side),
        window(half + 2, own_y), window(quarter + 4, 2 * y1),
        pltpu.VMEM((own_x, own_y, nz), jnp.int32),
        pltpu.VMEM(land_type.shape, jnp.int32),
        pltpu.SMEM(surface_drag.shape, F32),
        frame1, window(half + 10, 2 * y1), window(ny, packs + 10, y1 + 2),
        level1, level1, level1,
        window(ny, 2 * REACH + 1, 2, y1), window(2, y1),
        level2, level2, level2, level3, level3, level3, level3,
        window(8, full1), window(12, side),
        window(total),
        pltpu.SemaphoreType.DMA((4,)),
        pltpu.SemaphoreType.DMA((1,)),
        pltpu.SemaphoreType.DMA((13,)),
        pltpu.SemaphoreType.REGULAR((7,)),
    ]
    inside = pl.BlockSpec(memory_space=pltpu.VMEM)
    outside = pl.BlockSpec(memory_space=pltpu.HBM)
    arguments = [
        pltpu.with_memory_space_constraint(a, pltpu.HBM)
        for a in (velocity, pressure, turbine_cells, land_type, surface_drag)
    ]
    star, middle = pl.pallas_call(
        functools.partial(kernel, nx, ny),
        out_shape=(
            jax.ShapeDtypeStruct((3, rows, side, nz), F32),
            jax.ShapeDtypeStruct((own_x + 2, side, nz), F32),
        ),
        in_specs=[outside] * 5,
        out_specs=(inside, inside),
        scratch_shapes=scratch,
        compiler_params=pltpu.CompilerParams(
            collective_id=0, has_side_effects=True, vmem_limit_bytes=VMEM_LIMIT
        ),
    )(*arguments)
    return pl.pallas_call(
        closing,
        out_shape=(
            jax.ShapeDtypeStruct(velocity.shape, F32),
            jax.ShapeDtypeStruct(pressure.shape, F32),
        ),
        in_specs=[inside, inside],
        out_specs=(outside, outside),
        scratch_shapes=[
            pltpu.VMEM(velocity.shape, F32),
            pltpu.VMEM(pressure.shape, F32),
            pltpu.SemaphoreType.DMA((2,)),
        ],
        compiler_params=pltpu.CompilerParams(vmem_limit_bytes=VMEM_LIMIT),
    )(star, middle)


def solution(mesh):
    in_specs = (
        P(None, "gx", "gy", None),
        P("gx", "gy", None),
        P("gx", "gy"),
        P("gx", "gy", None),
        P(),
    )
    out_specs = (P(None, "gx", "gy", None), P("gx", "gy", None))
    body = functools.partial(per_device, mesh.shape["gx"], mesh.shape["gy"])
    return jax.shard_map(
        body, mesh=mesh, in_specs=in_specs, out_specs=out_specs, check_vma=False
    )
```
